32 devices in a mesh: seq: 8 (over z, y), head: 4 (over x, core).
Axes of the slice: x: 2, y: 2, z: 4, core: 2. Of those that a mesh axis runs over, the one named last changes fastest.
Arguments:
- x_in: bfloat16 [1024, 8192], P('seq', 'head'), may hold values from -6 to 6
- bc_in: bfloat16 [1024, 2, 128], P('seq'), may hold values from -0.59765625 to 0.59765625
- conv_x: bfloat16 [4, 8192], P(None, 'head'), may hold values from -3 to 3
- conv_bc: bfloat16 [4, 2, 128], replicated, may hold values from -3 to 3
- log_decay: float32 [1024, 64], P('seq', 'head'), may hold values from -2 to 0, as said below
- skip: float32 [64], P('head'), may hold values from 0.5 to 1.5
- queries: bfloat16 [1024, 8192], P('seq', 'head'), may hold values from -12 to 12
- keys: bfloat16 [1024, 1024], P('seq', 'head'), may hold values from -5 to 5
- values: bfloat16 [1024, 1024], P('seq', 'head'), may hold values from -6 to 6
- d_mixed: bfloat16 [1024, 8192], P('seq', 'head'), may hold values from -6 to 6
Outputs:
- mixed: bfloat16 [1024, 8192], P('seq', 'head')
- d_queries: float32 [1024, 8192], P('seq', 'head')
- d_keys: float32 [1024, 1024], P('seq', 'head')
- d_values: float32 [1024, 1024], P('seq', 'head')
- d_x_in: float32 [1024, 8192], P('seq', 'head')
- d_bc_in: float32 [1024, 2, 128], P('seq')
- d_log_decay: float32 [1024, 64], P('seq', 'head')
The draws below stay inside these ranges and needn't reach their ends.
Inputs may be any that keep to these rules, and one draw needn't show every extreme that they name: `log_decay`: every entry is negative.
All inputs are finite; a program needn't handle non-finite values.
Results may differ from the reference program's by a relative error of at most 0.012.
The reference program's roundings to bfloat16 on the way count: a program that leaves them out, or rounds other values in their place, can miss the bound.
Values may be sent and summed in bfloat16 or wider, within the bound.
A program may use at most 128 MiB of HBM per device.

```python
import math
from functools import partial
import jax
import jax.numpy as jnp
from jax import lax

TOK_DEV = 128
SEQ = 1024
SSM_HEADS = 64
SSM_DIM = 128
STATE = 128
CONV = 4
Q_HEADS = 64
KV_HEADS = 8
HEAD_DIM = 128


def draw_log_decay(key, part):
    subkeys = jax.random.split(key, 7)
    share = 5
    fast = jax.random.randint(subkeys[0], (SSM_HEADS,), 0, 10) < share
    fast_rate = jax.random.uniform(subkeys[1], (SSM_HEADS,), jnp.float32, 0.02, 0.04)
    slow_rate = jax.random.uniform(subkeys[2], (SSM_HEADS,), jnp.float32, 0.1, 0.3) / SEQ
    descent_stepsize = jnp.where(fast, fast_rate, slow_rate)
    multiplier_coefficient = jnp.exp(jax.random.uniform(subkeys[3], (SEQ // TOK_DEV, 1, SSM_HEADS), jnp.float32, -0.7, 0.7))
    multiplier_coefficient = jnp.broadcast_to(multiplier_coefficient, (SEQ // TOK_DEV, TOK_DEV, SSM_HEADS)).reshape(SEQ, SSM_HEADS)
    approximate_guess = jnp.exp(jax.random.uniform(subkeys[4], (SEQ, SSM_HEADS), jnp.float32, -0.7, 0.7))
    sequence_slots = jax.random.randint(subkeys[5], (2, SSM_HEADS), 0, SEQ)
    number_of_branches = jax.random.uniform(subkeys[6], (2, SSM_HEADS), jnp.float32, 0.22, 0.7)
    element_indices = jnp.arange(SEQ, dtype=jnp.int32)[:, None, None]
    span_count = jnp.sum(jnp.where(element_indices == sequence_slots[None], number_of_branches[None], 0.0), axis=1)
    return -(descent_stepsize[None, :] * multiplier_coefficient * approximate_guess) - span_count


def draw_keys(key, part):
    base_key = jax.random.fold_in(key, 202)
    shape = (SEQ, KV_HEADS, HEAD_DIM)
    result = jnp.clip(jax.random.normal(base_key, shape, jnp.float32), -5.0, 5.0)
    return result.reshape(SEQ, KV_HEADS * HEAD_DIM).astype(jnp.bfloat16)


def draw_queries(key, part):
    base_key = jax.random.fold_in(key, 303)
    ratio = Q_HEADS // KV_HEADS
    shape = (SEQ, KV_HEADS, ratio, HEAD_DIM)
    result = jnp.clip(2.5 * jax.random.normal(base_key, shape, jnp.float32), -12.0, 12.0)
    return result.reshape(SEQ, Q_HEADS * HEAD_DIM).astype(jnp.bfloat16)


def block_levels(own_key, extent, pieces, least, largest):
    gain, own = 1.0, jax.random.fold_in(own_key, 6)
    for position, shards_of in pieces:
        draws = jnp.exp(jax.random.uniform(jax.random.fold_in(own, position), (shards_of,), jnp.float32, least / len(pieces), largest / len(pieces)))
        gain = gain * jnp.repeat(draws, extent[position] // shards_of).reshape([-1 if axis == position else 1 for axis in range(len(extent))])
    return gain


def gaussian(rng, shape, scale, most, shards=(), kind=jnp.bfloat16):
    loudness = block_levels(rng, shape, shards, -0.22, 0.18) if shards else 1.0
    entries = jax.random.normal(rng, shape, jnp.float32) * scale * loudness
    return jnp.minimum(jnp.maximum(entries, -most), most).astype(kind)


def setup_inputs(seed: int = 0) -> dict:
    key_of = jax.random.split(jax.random.key(seed), 11)
    x_in = gaussian(key_of[0], (SEQ, SSM_HEADS * SSM_DIM), 1.0, 6.0, ((0, 8), (1, 4)))
    bc_in = gaussian(key_of[1], (SEQ, 2, STATE), 0.1, 0.59765625, ((0, 8),))
    conv_x = gaussian(key_of[2], (CONV, SSM_HEADS * SSM_DIM), CONV ** -0.5, 3.0, ((1, 4),))
    conv_bc = gaussian(key_of[3], (CONV, 2, STATE), CONV ** -0.5, 3.0)
    log_decay = draw_log_decay(jax.random.fold_in(key_of[10], 71), 0)
    skip = jnp.clip(0.5 + 1.0 * jax.random.uniform(key_of[5], (SSM_HEADS,), jnp.float32) ** block_levels(key_of[5], (SSM_HEADS,), ((0, 4),), -0.2, 0.2), 0.5, 1.5)
    queries = draw_queries(jax.random.fold_in(key_of[10], 71), 0)
    keys = draw_keys(jax.random.fold_in(key_of[10], 71), 0)
    values = gaussian(key_of[8], (SEQ, KV_HEADS * HEAD_DIM), 1.0, 6.0, ((0, 8), (1, 4)))
    d_mixed = gaussian(key_of[9], (SEQ, SSM_HEADS * SSM_DIM), 1.0, 6.0, ((0, 8), (1, 4)))
    return {"x_in": x_in, "bc_in": bc_in, "conv_x": conv_x, "conv_bc": conv_bc, "log_decay": log_decay, "skip": skip, "queries": queries, "keys": keys, "values": values, "d_mixed": d_mixed}


masked_value = -1e+30
highest_precision = lax.Precision.HIGHEST

def silu_slope(pre):
    sigmoid = jax.nn.sigmoid(pre)
    return sigmoid * (1.0 + pre * (1.0 - sigmoid))

def conv_forward(inputs, before, weight):
    padded = jnp.concatenate([before, inputs], axis=0)
    length = inputs.shape[0]
    total = jnp.zeros(inputs.shape, jnp.float32)
    for tap in range(weight.shape[0]):
        total = total + weight[tap].astype(jnp.float32) * padded[tap:tap + length].astype(jnp.float32)
    return total

def conv_backward(grads, after, weight):
    width = weight.shape[0]
    padded = jnp.concatenate([grads, after], axis=0)
    length = grads.shape[0]
    total = jnp.zeros(grads.shape, jnp.float32)
    for tap in range(width):
        offset = width - 1 - tap
        total = total + weight[tap].astype(jnp.float32) * padded[offset:offset + length]
    return total

def span_step(state, x_blk, b_blk, c_blk, a_blk, skip):
    size = x_blk.shape[0]
    running = jnp.cumsum(a_blk, axis=0)
    gaps = running[:, None, :] - running[None, :, :]
    order = jnp.arange(size, dtype=jnp.int32)
    allowed = (order[:, None] >= order[None, :])[:, :, None]
    fading = jnp.exp(jnp.where(allowed, gaps, masked_value))
    inner = jnp.dot(c_blk, b_blk.T, precision=highest_precision)
    outputs = jnp.einsum('tsh,shp->thp', inner[:, :, None] * fading, x_blk, precision=highest_precision)
    carried = jnp.einsum('tn,hpn->thp', c_blk, state, precision=highest_precision)
    outputs = outputs + jnp.exp(running)[:, :, None] * carried + skip[None, :, None] * x_blk
    final = running[-1]
    tail_fade = jnp.exp(final[None, :] - running)
    state = jnp.exp(final)[:, None, None] * state + jnp.einsum('sh,shp,sn->hpn', tail_fade, x_blk, b_blk, precision=highest_precision)
    return (outputs, state)

def ssd_run(x_rows, b_rows, c_rows, decay, skip):
    size = math.gcd(128, TOK_DEV)
    blocks = SEQ // size
    x_blocks = x_rows.reshape(blocks, size, SSM_HEADS, SSM_DIM)
    b_blocks = b_rows.reshape(blocks, size, STATE)
    c_blocks = c_rows.reshape(blocks, size, STATE)
    a_blocks = decay.reshape(blocks, size, SSM_HEADS)

    def advance(state, item):
        x_blk, b_blk, c_blk, a_blk = item
        outputs, state = span_step(state, x_blk, b_blk, c_blk, a_blk, skip)
        return (state, outputs)
    initial = jnp.zeros((SSM_HEADS, SSM_DIM, STATE), x_rows.dtype)
    _, outputs = lax.scan(advance, initial, (x_blocks, b_blocks, c_blocks, a_blocks))
    return outputs.reshape(SEQ, SSM_HEADS, SSM_DIM)

def reference(x_in, bc_in, conv_x, conv_bc, log_decay, skip, queries, keys, values, d_mixed):
    edge = CONV - 1
    pre_x = conv_forward(x_in, jnp.zeros((edge, x_in.shape[1]), x_in.dtype), conv_x)
    pre_bc = conv_forward(bc_in, jnp.zeros((edge,) + bc_in.shape[1:], bc_in.dtype), conv_bc)
    x_conv = jax.nn.silu(pre_x).astype(jnp.bfloat16)
    bc_conv = jax.nn.silu(pre_bc).astype(jnp.bfloat16)
    x_rows = x_conv.astype(jnp.float32).reshape(SEQ, SSM_HEADS, SSM_DIM)
    b_rows = bc_conv[:, 0].astype(jnp.float32)
    c_rows = bc_conv[:, 1].astype(jnp.float32)
    ssm_out, ssd_back = jax.vjp(partial(ssd_run, skip=skip), x_rows, b_rows, c_rows, log_decay)
    ratio = Q_HEADS // KV_HEADS
    softmax_scale = HEAD_DIM ** (-0.5)
    query_heads = queries.reshape(SEQ, Q_HEADS, HEAD_DIM).transpose(1, 0, 2)
    grad_heads = d_mixed.reshape(SEQ, Q_HEADS, HEAD_DIM).transpose(1, 0, 2)
    key_heads = keys.reshape(SEQ, KV_HEADS, HEAD_DIM).transpose(1, 0, 2)
    value_heads = values.reshape(SEQ, KV_HEADS, HEAD_DIM).transpose(1, 0, 2)
    order = jnp.arange(SEQ, dtype=jnp.int32)
    allowed = order[None, :] <= order[:, None]

    def one_head(head):
        group = head // ratio
        query = query_heads[head]
        grad = grad_heads[head]
        key_rows = key_heads[group]
        value_rows = value_heads[group]
        attention_scores = jnp.where(allowed, jnp.dot(query, key_rows.T, preferred_element_type=jnp.float32) * softmax_scale, masked_value)
        top = lax.optimization_barrier(jnp.max(attention_scores, axis=-1))
        lse = top + jnp.log(lax.optimization_barrier(jnp.sum(jnp.exp(attention_scores - top[:, None]), axis=-1)))
        probs = jnp.exp(attention_scores - lse[:, None])
        attention_weights = probs.astype(jnp.bfloat16)
        attended_output = jnp.dot(attention_weights, value_rows, preferred_element_type=jnp.float32)
        delta_terms = lax.optimization_barrier(jnp.sum(grad.astype(jnp.float32) * attended_output, axis=-1))
        weight_gradient = jnp.dot(grad, value_rows.T, preferred_element_type=jnp.float32)
        score_gradient = (probs * (weight_gradient - delta_terms[:, None])).astype(jnp.bfloat16)
        dquery = jnp.dot(score_gradient, key_rows, preferred_element_type=jnp.float32) * softmax_scale
        dkey = jnp.dot(score_gradient.T, query, preferred_element_type=jnp.float32) * softmax_scale
        value_gradient = jnp.dot(attention_weights.T, grad, preferred_element_type=jnp.float32)
        return (attended_output, dquery, dkey, value_gradient)
    attended_output, dquery, dkey, value_gradient = lax.map(one_head, jnp.arange(Q_HEADS, dtype=jnp.int32))
    attended_flat = attended_output.transpose(1, 0, 2).reshape(SEQ, Q_HEADS * HEAD_DIM)
    mixed = (ssm_out.reshape(SEQ, SSM_HEADS * SSM_DIM) + attended_flat).astype(jnp.bfloat16)
    d_queries = dquery.transpose(1, 0, 2).reshape(SEQ, Q_HEADS * HEAD_DIM)
    d_keys = dkey.reshape(KV_HEADS, ratio, SEQ, HEAD_DIM).sum(axis=1).transpose(1, 0, 2).reshape(SEQ, KV_HEADS * HEAD_DIM)
    d_values = value_gradient.reshape(KV_HEADS, ratio, SEQ, HEAD_DIM).sum(axis=1).transpose(1, 0, 2).reshape(SEQ, KV_HEADS * HEAD_DIM)
    grad_y = d_mixed.astype(jnp.float32).reshape(SEQ, SSM_HEADS, SSM_DIM)
    grad_x, grad_b, grad_c, d_log_decay = ssd_back(grad_y)
    grad_pre_x = grad_x.reshape(SEQ, SSM_HEADS * SSM_DIM) * silu_slope(pre_x)
    grad_pre_bc = jnp.stack([grad_b, grad_c], axis=1) * silu_slope(pre_bc)
    d_x_in = conv_backward(grad_pre_x, jnp.zeros((edge, grad_pre_x.shape[1]), jnp.float32), conv_x)
    d_bc_in = conv_backward(grad_pre_bc, jnp.zeros((edge,) + grad_pre_bc.shape[1:], jnp.float32), conv_bc)
    return (mixed, d_queries, d_keys, d_values, d_x_in, d_bc_in, d_log_decay)
```

```python
import functools
import math

import jax
import jax.numpy as jnp
from jax import lax
from jax.experimental import pallas as pl
from jax.experimental.pallas import tpu as pltpu
from jax.sharding import PartitionSpec as P

D = 128
W = 2 * D
EDGE = 16
F32 = jnp.float32
BF16 = jnp.bfloat16
MESH = pl.DeviceIdType.MESH
VMEM = pl.BlockSpec(memory_space=pltpu.VMEM)
HBM = pl.BlockSpec(memory_space=pltpu.HBM)
SMEM = pl.BlockSpec(memory_space=pltpu.SMEM)
SCALE = D ** (-0.5)
LOG2 = SCALE * math.log2(math.e)


def mm(a, b):
    return jnp.dot(a, b, preferred_element_type=F32)


def mm_nt(a, b):
    return lax.dot_general(a, b, (((1,), (1,)), ((), ())), preferred_element_type=F32)


def sigmoid(v):
    return 1.0 / (1.0 + jnp.exp(-v))


def peer(**coords):
    return dict(device_id=coords, device_id_type=MESH)


def split3(v):
    hi = v.astype(BF16)
    rest = v - hi.astype(F32)
    mid = rest.astype(BF16)
    return hi, mid, (rest - mid.astype(F32)).astype(BF16)


def exact(dot, a, b):
    if a.dtype == BF16:
        hi, mid, lo = split3(b)
        return (dot(a, hi) + dot(a, mid)) + dot(a, lo)
    hi, mid, lo = split3(a)
    return (dot(hi, b) + dot(mid, b)) + dot(lo, b)


def conv(x, halo, taps):
    width = taps.shape[0]
    rows = x.shape[0]
    full = jnp.concatenate([halo[EDGE - 8:], x], axis=0)
    total = None
    for tap in range(width):
        start = 8 - (width - 1) + tap
        term = taps[tap:tap + 1] * full[start:start + rows]
        total = term if total is None else total + term
    return total


def conv_back(grads, after, taps):
    width = taps.shape[0]
    rows = grads.shape[0]
    padded = jnp.concatenate([grads, after], axis=0)
    total = None
    for tap in range(width):
        offset = width - 1 - tap
        term = taps[tap:tap + 1] * padded[offset:offset + rows]
        total = term if total is None else total + term
    return total


def iota(shape, axis):
    return lax.broadcasted_iota(jnp.int32, shape, axis)


def block_kernel(n, m, x_hbm, bc_hbm, w_hbm, wbc_hbm, ld_hbm, skip_ref, q_hbm, k_hbm, v_hbm, dm_hbm,
                 mixed_ref, dq_ref, dk_out, dv_out, dx_ref, dbc_out, dla_ref,
                 x_ref, dm_ref, q_ref, w_ref, bc3, wbc3, ld_ref, bcs, kva, xh, bch, bcn,
                 xb_ref, sl_ref, col_ref, xt_ref, dme_ref, y_ref, gx_ref, att_ref,
                 bcv, bcsl, bcsn, bt, ct, rowp, dec, rdec, inner, innert, dinner, dbc, dbcb, net_ref, fin_ref,
                 tf, tb, of, ob, rf, rb, af, ab, sf, sb, mf, mb, s_in, g_in,
                 s_ref, eb_ref, ds_ref, kt, vt, ek, eq, dka, dva, part, landy, landz, acc,
                 gh, gn, bb, nb,
                 ls, zs, zr, fs, fr, hs, hr, ofs, ofr, obs, obr, es, er,
                 cfs, cfr, cbs, cbr, mfs, mfr, mbs, mbr, pys, pyr, pzs, pzr, xs, xr, bs, br, ns, nr):
    me = lax.axis_index("seq")
    my = lax.axis_index("head")
    odd = lax.rem(me, 2)
    is_odd = odd == 1
    mate = me + 1 - 2 * odd
    level = me // 2
    levels = n // 2
    rows, wide = x_ref.shape
    width = k_hbm.shape[1]
    heads = wide // D
    pairs = heads // 2
    share = pairs // 2
    kv_heads = width // D
    ratio = heads // kv_heads
    length = n * rows
    nxt = lax.rem(me + 1, n)
    prv = lax.rem(me + n - 1, n)
    up = lax.rem(me + 2, n)
    down = lax.rem(me + n - 2, n)

    barrier = pltpu.get_barrier_semaphore()
    count = 0
    for off in range(1, n):
        pl.semaphore_signal(barrier, inc=1, **peer(seq=lax.rem(me + off, n), head=my))
        count += 1
    for off in range(1, m):
        for to in (me, nxt, prv):
            pl.semaphore_signal(barrier, inc=1, **peer(seq=to, head=lax.rem(my + off, m)))
            count += 1

    loads = [
        (k_hbm, kva.at[me, :, pl.ds(0, width)]), (v_hbm, kva.at[me, :, pl.ds(width, width)]),
        (ld_hbm, ld_ref), (bc_hbm, bc3), (wbc_hbm, wbc3), (w_hbm, w_ref), (x_hbm, x_ref),
        (dm_hbm, dm_ref), (q_hbm, q_ref),
    ]
    loads = [pltpu.make_async_copy(src, dst, ls.at[i]) for i, (src, dst) in enumerate(loads)]
    for cp in loads:
        cp.start()

    t_i = iota((rows, rows), 0)
    s_i = iota((rows, rows), 1)
    lower = jnp.where(t_i >= s_i, 1.0, 0.0).astype(BF16)
    loads[2].wait()
    cum = exact(mm_nt, lower, ld_ref[...])
    parts = split3(cum)
    ident = jnp.where(iota((heads, heads), 0) == iota((heads, heads), 1), 1.0, 0.0).astype(BF16)
    cum_rows = (mm_nt(ident, parts[0]) + mm_nt(ident, parts[1])) + mm_nt(ident, parts[2])
    for h in range(heads):
        rowp[h // 2, :, (h % 2) * D:(h % 2) * D + D] = cum_rows[h:h + 1]

    cross = max(levels // 4, 1)
    early = level < cross
    for off in range(1, n):
        fill = me + off < n
        if off == 1:
            fill = jnp.logical_and(fill, jnp.logical_or(is_odd, jnp.logical_not(early)))

        @pl.when(fill)
        def _():
            kva[lax.rem(me + off, n)] = jnp.zeros(kva.shape[1:], kva.dtype)

    big = -(2.0 ** 100)
    e_i = iota((rows, D), 1)
    r_i = iota((rows, D), 0)
    inside = jnp.where((r_i == e_i) & (e_i > 0), big, 0.0).astype(BF16)
    outside = jnp.where(e_i == 0, big, 0.0).astype(BF16)
    for j in range(n):
        later = jnp.where(me < j, outside, jnp.zeros_like(outside))
        ek[j * rows:(j + 1) * rows] = jnp.where(me == j, inside, later)
    reach = jnp.where((e_i > r_i) | (e_i == 0), 1.0, 0.0).astype(BF16)
    eq[:rows] = reach
    eq[rows:] = reach
    vt[D:] = jnp.ones((vt.shape[0] - D, length), BF16)

    for i in (0, 1, 3, 4, 5, 6):
        loads[i].wait()
    bcs[:, :D] = bc3[...].astype(F32)[:, 0, :].astype(BF16)
    bcs[:, D:] = bc3[...].astype(F32)[:, 1, :].astype(BF16)
    wbc = jnp.concatenate([wbc3[...].astype(F32)[:, 0, :], wbc3[...].astype(F32)[:, 1, :]], axis=1)
    pl.semaphore_wait(barrier, count)

    def halo(slot, src, dst, to):
        return pltpu.make_async_remote_copy(
            src_ref=src, dst_ref=dst, send_sem=hs.at[slot], recv_sem=hr.at[slot],
            **peer(seq=to, head=my))

    last = pl.ds(rows - EDGE, EDGE)
    cx = halo(0, x_ref.at[last], xh, nxt)
    cb = halo(1, bcs.at[last], bch, nxt)
    cn = halo(2, bcs.at[pl.ds(0, EDGE)], bcn, prv)

    @pl.when(me < n - 1)
    def _():
        cb.start()
        cx.start()

    @pl.when(me > 0)
    def _():
        cn.start()

    par = odd

    def rise(blk):
        return pltpu.make_async_remote_copy(
            src_ref=kva.at[blk], dst_ref=kva.at[blk], send_sem=zs.at[blk], recv_sem=zr.at[blk],
            **peer(seq=up, head=my))

    def over(blk):
        return pltpu.make_async_remote_copy(
            src_ref=kva.at[blk], dst_ref=kva.at[blk], send_sem=fs.at[blk], recv_sem=fr.at[blk],
            **peer(seq=mate, head=my))

    not_top = level < levels - 1

    @pl.when(not_top)
    def _():
        rise(me).start()

    @pl.when(jnp.logical_or(odd == 0, early))
    def _():
        over(me).start()

    def relay(k):
        if k == 0:
            @pl.when(early)
            def _():
                over(mate).wait_recv()
                rise(mate).start()
            return

        @pl.when(level >= k)
        def _():
            far = level - k
            mine = 2 * far + par
            rise(mine).wait_recv()

            @pl.when(not_top)
            def _():
                rise(mine).start()

            @pl.when(far >= cross)
            def _():
                over(mine).start()

            @pl.when(far < cross)
            def _():
                other = 2 * far + 1 - par
                rise(other).wait_recv()

                @pl.when(not_top)
                def _():
                    rise(other).start()

    def relayed():
        @pl.when(jnp.logical_and(odd == 1, jnp.logical_not(early)))
        def _():
            over(mate).wait_recv()

        for k in range(1, levels):
            @pl.when(jnp.logical_and(level >= k, level - k >= cross))
            def _():
                over(2 * (level - k) + 1 - par).wait_recv()

    def relay_sent():
        @pl.when(not_top)
        def _():
            rise(me).wait_send()

        @pl.when(jnp.logical_or(odd == 0, early))
        def _():
            over(me).wait_send()

        @pl.when(early)
        def _():
            rise(mate).wait_send()

        for k in range(1, levels):
            far = level - k

            @pl.when(jnp.logical_and(level >= k, not_top))
            def _():
                rise(2 * far + par).wait_send()

            @pl.when(jnp.logical_and(level >= k, far >= cross))
            def _():
                over(2 * far + par).wait_send()

            @pl.when(jnp.logical_and(jnp.logical_and(level >= k, far < cross), not_top))
            def _():
                rise(2 * far + 1 - par).wait_send()

    @pl.when(me == 0)
    def _():
        xh[...] = jnp.zeros(xh.shape, xh.dtype)
        bch[...] = jnp.zeros(bch.shape, bch.dtype)

    @pl.when(me == n - 1)
    def _():
        bcn[...] = jnp.zeros(bcn.shape, bcn.dtype)

    loads[7].wait()
    loads[8].wait()

    @pl.when(me > 0)
    def _():
        cb.wait_recv()
        cx.wait_recv()

    @pl.when(me < n - 1)
    def _():
        cn.wait_recv()

    def slope(pre, sig):
        return sig * (1.0 + pre * (1.0 - sig))

    pre = conv(bcs[...].astype(F32), bch[...].astype(F32), wbc)
    sig = sigmoid(pre)
    act = (pre * sig).astype(BF16)
    bcv[...] = act
    bcsl[...] = slope(pre, sig)
    pre = conv(bcn[...].astype(F32), bcs[rows - EDGE:].astype(F32), wbc)
    bcsn[...] = slope(pre, sigmoid(pre))
    act = act.astype(F32)
    bt[...] = jnp.transpose(act[:, :D]).astype(BF16)
    ct[...] = jnp.transpose(act[:, D:]).astype(BF16)
    b = bcv[:, :D]
    c = bcv[:, D:]
    own_inner = mm_nt(c, b)
    own_innert = mm_nt(b, c)
    for a in range(2):
        inner[:, a * D:(a + 1) * D] = own_inner
        innert[:, a * D:(a + 1) * D] = own_innert
    dinner[...] = jnp.zeros_like(dinner)
    dbc[...] = jnp.zeros_like(dbc)

    def trade(i, which):
        src, dst, send, recv = ((tf, rf, ofs, ofr), (tb, rb, obs, obr))[which]
        return pltpu.make_async_remote_copy(
            src_ref=src.at[i], dst_ref=dst.at[i], send_sem=send.at[i], recv_sem=recv.at[i],
            **peer(seq=mate, head=my))

    bottom = level == 0
    top_level = level == levels - 1
    send_tf = jnp.logical_not(jnp.logical_and(is_odd, top_level))
    send_tb = jnp.logical_or(is_odd, jnp.logical_not(bottom))
    recv_tf = jnp.logical_or(is_odd, jnp.logical_not(top_level))
    recv_tb = jnp.logical_not(jnp.logical_and(is_odd, bottom))
    give_f = recv_tb
    take_f = send_tb
    give_b = recv_tf
    take_b = send_tf
    base = odd * share

    @pl.when(jnp.logical_not(recv_tf))
    def _():
        rf[...] = jnp.zeros(rf.shape, rf.dtype)

    @pl.when(jnp.logical_not(recv_tb))
    def _():
        rb[...] = jnp.zeros(rb.shape, rb.dtype)

    @pl.when(jnp.logical_not(take_f))
    def _():
        s_in[pl.ds(share - base, share)] = jnp.zeros((share, D, W), BF16)

    @pl.when(jnp.logical_not(take_b))
    def _():
        g_in[pl.ds(share - base, share)] = jnp.zeros((share, D, W), BF16)

    def wide_of(p):
        return pl.ds(pl.multiple_of(p * W, W), W)

    def own(i):
        p = lax.rem(i + (1 - odd) * share, pairs)
        lanes = wide_of(p)
        pre = conv(x_ref[:, lanes].astype(F32), xh[:, lanes].astype(F32), w_ref[:, lanes].astype(F32))
        sig = sigmoid(pre)
        xb = (pre * sig).astype(BF16)
        xb_ref[:, lanes] = xb
        sl_ref[:, lanes] = slope(pre, sig)
        pick = jnp.where(iota((heads, W), 0) == 2 * p + iota((heads, W), 1) // D, 1.0, 0.0).astype(BF16)
        col = (mm(parts[0], pick) + mm(parts[1], pick)) + mm(parts[2], pick)
        col_ref[:, lanes] = col
        final = col[rows - 1:]
        dec[p] = jnp.exp(final)
        xt = (xb.astype(F32) * jnp.exp(final - col)).astype(BF16)
        dme = (dm_ref[:, lanes].astype(F32) * jnp.exp(col)).astype(BF16)
        xt_ref[:, lanes] = xt
        dme_ref[:, lanes] = dme
        own_f = mm(bt[...], xt)
        own_b = mm(ct[...], dme)

        @pl.when(i < share)
        def _():
            tf[i] = own_f.astype(BF16)
            tb[i] = own_b.astype(BF16)

            @pl.when(send_tf)
            def _():
                trade(i, 0).start()

            @pl.when(send_tb)
            def _():
                trade(i, 1).start()

        @pl.when(i >= share)
        def _():
            of[i - share] = own_f
            ob[i - share] = own_b

    def skips(p):
        return jnp.where(iota((1, W), 1) < D, skip_ref[2 * p], skip_ref[2 * p + 1])

    t_w = iota((rows, W), 0)
    s_w = lax.rem(iota((rows, W), 1), D)

    def within(p):
        lanes = wide_of(p)
        xb = xb_ref[:, lanes]
        dm = dm_ref[:, lanes]
        gap = col_ref[:, lanes] - rowp[p]
        fade = jnp.exp(jnp.where(t_w >= s_w, gap, -1e30))
        fadet = jnp.exp(jnp.where(s_w >= t_w, -gap, -1e30))
        mix = (inner[...] * fade).astype(BF16)
        mixt = (innert[...] * fadet).astype(BF16)
        skip = skips(p)
        total = None
        ys, gs = [], []
        for a in range(2):
            cols = slice(a * D, (a + 1) * D)
            ys.append(mm(mix[:, cols], xb[:, cols]))
            gs.append(mm(mixt[:, cols], dm[:, cols]))
            term = mm_nt(dm[:, cols], xb[:, cols]) * fade[:, cols]
            total = term if total is None else total + term
        dinner[...] += total
        y_ref[:, lanes] = jnp.concatenate(ys, axis=1) + skip * xb.astype(F32)
        gx_ref[:, lanes] = jnp.concatenate(gs, axis=1) + skip * dm.astype(F32)

    def unit(i, carry):
        @pl.when(i < pairs)
        def _():
            own(i)

        @pl.when(i >= pairs)
        def _():
            within(i - pairs)

        return carry

    done = 0
    relay(0)
    for k in range(1, levels):
        upto = 2 * pairs * k // levels
        lax.fori_loop(done, upto, unit, 0)
        done = upto
        relay(k)

    lax.fori_loop(done, 2 * pairs, unit, 0)

    swap = pltpu.make_async_remote_copy(
        src_ref=dec.at[pl.ds((1 - odd) * share, share)], dst_ref=rdec, send_sem=es, recv_sem=er,
        **peer(seq=mate, head=my))
    swap.start()
    relayed()
    swap.wait()

    def copy(stage, landing, send, recv, i, to):
        return pltpu.make_async_remote_copy(
            src_ref=stage.at[i], dst_ref=landing.at[i], send_sem=send.at[i], recv_sem=recv.at[i],
            **peer(seq=to, head=my))

    def give(stage, out, send, recv, i, start):
        return pltpu.make_async_remote_copy(
            src_ref=stage.at[i], dst_ref=out.at[start + i], send_sem=send.at[i],
            recv_sem=recv.at[i], **peer(seq=mate, head=my))

    def ahead(i, x):
        mine, other = of[i], rf[i].astype(F32)
        even_f, odd_f = jnp.where(is_odd, other, mine), jnp.where(is_odd, mine, other)
        even_d = jnp.where(is_odd, rdec[i], dec[base + i])
        odd_d = jnp.where(is_odd, dec[base + i], rdec[i])
        middle = even_d * x + even_f
        return jnp.where(is_odd, middle, x), jnp.where(is_odd, x, middle), odd_d * middle + odd_f

    def behind(i, x):
        mine, other = ob[i], rb[i].astype(F32)
        even_b, odd_b = jnp.where(is_odd, other, mine), jnp.where(is_odd, mine, other)
        even_d = jnp.where(is_odd, rdec[i], dec[base + i])
        odd_d = jnp.where(is_odd, dec[base + i], rdec[i])
        middle = odd_d * x + odd_b
        return jnp.where(is_odd, x, middle), jnp.where(is_odd, middle, x), even_d * middle + even_b

    def hop(i, join, landing, stage, send, recv, to, first, last, out, gift, gsend, grecv, which, arrives, gives):
        @pl.when(first)
        def _():
            landing[i] = jnp.zeros(landing.shape[1:], landing.dtype)

        @pl.when(jnp.logical_not(first))
        def _():
            copy(stage, landing, send, recv, i, to).wait_recv()

        @pl.when(arrives)
        def _():
            trade(i, which).wait_recv()

        mine, other, on = join(i, landing[i].astype(F32))
        stage[i] = on.astype(BF16)

        @pl.when(jnp.logical_not(last))
        def _():
            copy(stage, landing, send, recv, i, to).start()

        out[base + i] = mine.astype(BF16)
        gift[i] = other.astype(BF16)

        @pl.when(gives)
        def _():
            give(gift, out, gsend, grecv, i, base).start()

    def pass_over(kv, j):
        return pltpu.make_async_remote_copy(
            src_ref=part.at[kv, 2 * j + 1 - par], dst_ref=landy.at[kv, j], send_sem=pys.at[kv, j],
            recv_sem=pyr.at[kv, j], **peer(seq=mate, head=my))

    def pass_down(kv, j):
        return pltpu.make_async_remote_copy(
            src_ref=part.at[kv, 2 * j + par], dst_ref=landz.at[kv, j], send_sem=pzs.at[kv, j],
            recv_sem=pzr.at[kv, j], **peer(seq=down, head=my))

    def sends_over(j):
        return jnp.logical_or(j < level, jnp.logical_and(j == level, is_odd))

    def takes_over(j):
        return jnp.logical_or(j < level, jnp.logical_and(j == level, odd == 0))

    def gather_down(kv, j):
        acc[...] = part[kv, 2 * j + par].astype(F32)

        @pl.when(takes_over(j))
        def _():
            pass_over(kv, j).wait_recv()
            acc[...] += landy[kv, j].astype(F32)

        @pl.when(not_top)
        def _():
            pass_down(kv, j).wait_recv()
            acc[...] += landz[kv, j].astype(F32)

        @pl.when(j < level)
        def _():
            part[kv, 2 * j + par] = acc[...].astype(BF16)
            pass_down(kv, j).start()

        @pl.when(j == level)
        def _():
            cols = slice(kv * D, kv * D + D)
            dk_out[:, cols] = acc[:, :D]
            dv_out[:, cols] = acc[:, D:]

    slots = 2 * pairs

    def slot_of(kv):
        ready = (kv + 1) * (ratio // 2) - 1
        return ready + (2 if kv < kv_heads - 1 else 5) + 3 * (levels - 1 - level)

    def gathers(t):
        for kv in range(kv_heads):
            j = t - slot_of(kv)

            @pl.when(jnp.logical_and(j >= 0, j <= level))
            def _():
                gather_down(kv, j)

    def lanes_of(h):
        return pl.ds(pl.multiple_of(h * D, D), D)

    tile = W if length % W == 0 else D
    many = tile // rows

    def attend(p):
        h = 2 * p
        kv = h // ratio
        first, second = lanes_of(h), lanes_of(h + 1)
        k_cols, v_cols = lanes_of(kv), lanes_of(kv_heads + kv)

        @pl.when(lax.rem(h, ratio) == 0)
        def _():
            kt[...] = jnp.transpose(kva[:, :, k_cols].reshape(length, D).astype(F32)).astype(BF16)
            vt[:D] = jnp.transpose(kva[:, :, v_cols].reshape(length, D).astype(F32)).astype(BF16)
            dka[...] = jnp.zeros_like(dka)
            dva[...] = jnp.zeros_like(dva)

        q = jnp.concatenate([q_ref[:, first], q_ref[:, second]], axis=0)
        dm = jnp.concatenate([dm_ref[:, first], dm_ref[:, second]], axis=0)
        qe = jnp.concatenate([q, eq[...]], axis=1)
        top = None
        for j in range(length // tile):
            at = slice(j * tile, (j + 1) * tile)
            k = kva[j * many:(j + 1) * many, :, k_cols].reshape(tile, D)
            s = mm_nt(jnp.concatenate([k, ek[at]], axis=1), qe)
            s_ref[at] = s
            high = jnp.max(s.reshape(tile // 8, 8, 2 * rows), axis=0)
            top = high if top is None else jnp.maximum(top, high)
        top = jnp.max(top, axis=0, keepdims=True) * LOG2
        for j in range(length // tile):
            at = slice(j * tile, (j + 1) * tile)
            e = jnp.exp2(s_ref[at] * LOG2 - top)
            s_ref[at] = e
            eb_ref[at] = e.astype(BF16)
        out_t = mm(vt[...], eb_ref[...])
        inv = 1.0 / out_t[D:D + 1]
        out_t = out_t[:D] * inv
        out = jnp.transpose(out_t)
        att_ref[:, first] = out[:rows]
        att_ref[:, second] = out[rows:]
        delta = jnp.sum(jnp.transpose(dm.astype(F32)) * out_t, axis=0, keepdims=True)
        for j in range(length // tile):
            at = slice(j * tile, (j + 1) * tile)
            v = kva[j * many:(j + 1) * many, :, v_cols].reshape(tile, D)
            ds_ref[at] = (s_ref[at] * (mm_nt(v, dm) - delta)).astype(BF16)
        dq = jnp.transpose(mm(kt[...], ds_ref[...]) * (inv * SCALE))
        dq_ref[:, first] = dq[:rows]
        dq_ref[:, second] = dq[rows:]
        inv_col = jnp.transpose(jnp.broadcast_to(inv, (D, 2 * rows)))
        dka[...] += mm(ds_ref[...], (q.astype(F32) * inv_col).astype(BF16))
        dva[...] += mm(eb_ref[...], (dm.astype(F32) * inv_col).astype(BF16))

        @pl.when(lax.rem(h, ratio) == ratio - 2)
        def _():
            part[kv, :, :, :D] = (dka[...] * SCALE).astype(BF16).reshape(n, rows, D)
            part[kv, :, :, D:] = dva[...].astype(BF16).reshape(n, rows, D)
            for j in range(levels):
                @pl.when(sends_over(j))
                def _():
                    pass_over(kv, j).start()

    def step(t, carry):
        f = t - level
        g = t - (levels - 1 - level)

        @pl.when(jnp.logical_and(f >= 0, f < share))
        def _():
            hop(f, ahead, af, sf, cfs, cfr, up, level == 0, level == levels - 1, s_in, mf, mfs, mfr,
                0, recv_tf, give_f)

        @pl.when(jnp.logical_and(g >= 0, g < share))
        def _():
            hop(g, behind, ab, sb, cbs, cbr, down, level == levels - 1, level == 0, g_in, mb, mbs, mbr,
                1, recv_tb, give_b)

        @pl.when(t < pairs)
        def _():
            attend(t)
            gathers(t)

        return carry

    lax.fori_loop(0, max(levels - 1 + share, pairs), step, 0)

    ones = jnp.ones((EDGE, D), BF16)

    def through(i, carry):
        p = lax.rem(i + base, pairs)
        lanes = wide_of(p)

        @pl.when(jnp.logical_and(i >= share, take_f))
        def _():
            give(mf, s_in, mfs, mfr, i - share, share - base).wait_recv()

        @pl.when(jnp.logical_and(i >= share, take_b))
        def _():
            give(mb, g_in, mbs, mbr, i - share, share - base).wait_recv()

        state = s_in[p]
        grad = g_in[p]
        xf = xb_ref[:, lanes].astype(F32)
        dmf = dm_ref[:, lanes].astype(F32)
        col = col_ref[:, lanes]
        final = col[rows - 1:]
        back = jnp.exp(final - col) * mm(b, grad)
        y = y_ref[:, lanes] + jnp.exp(col) * mm(c, state)
        mixed_ref[:, lanes] = (y + att_ref[:, lanes]).astype(BF16)
        gx = gx_ref[:, lanes] + back
        net = dmf * y - xf * gx
        hi = net.astype(BF16)
        lo = (net - hi.astype(F32)).astype(BF16)
        inside = jnp.sum(xf * back, axis=0, keepdims=True) + jnp.exp(final) * jnp.sum(
            state.astype(F32) * grad.astype(F32), axis=0, keepdims=True)
        for a in range(2):
            cols = slice(a * D, (a + 1) * D)
            sums = mm_nt(ones, hi[:, cols]) + mm_nt(ones, lo[:, cols])
            net_ref[pl.ds(2 * p + a, 1)] = sums[:1]
            fin_ref[pl.ds(2 * p + a, 1)] = inside[:, cols]
        dbc[:, D:] += mm_nt(dme_ref[:, lanes], state)
        dbc[:, :D] += mm_nt(xt_ref[:, lanes], grad)
        g = gx * sl_ref[:, lanes]
        gh[:, lanes] = g[:EDGE].astype(BF16)
        dx_ref[:, lanes] = conv_back(g, jnp.zeros((8, W), F32), w_ref[:, lanes].astype(F32))
        gathers(pairs + i)
        return carry

    lax.fori_loop(0, pairs, through, 0)
    di = dinner[...]
    dbcb[:, D:] = (dbc[:, D:] + mm(di.astype(BF16), b)).astype(BF16)
    dbcb[:, :D] = (dbc[:, :D] + mm(jnp.transpose(di).astype(BF16), c)).astype(BF16)

    def remote(src, dst, send, recv, seq, head):
        return pltpu.make_async_remote_copy(
            src_ref=src, dst_ref=dst, send_sem=send, recv_sem=recv, **peer(seq=seq, head=head))

    def across(off):
        return remote(dbcb, bb.at[off], bs.at[off], br.at[off], me, lax.rem(my + off, m))

    def before(off):
        return remote(dbcb.at[pl.ds(0, EDGE)], nb.at[off], ns.at[off], nr.at[off], prv,
                      lax.rem(my + off, m))

    edge = remote(gh, gn, xs, xr, prv, my)
    for off in range(1, m):
        across(off).start()

    @pl.when(me > 0)
    def _():
        edge.start()
        for off in range(m):
            before(off).start()

    dla_ref[...] = exact(mm, net_ref[...], lower) + exact(mm, fin_ref[...], jnp.ones((D, rows), BF16))

    for kv in range(kv_heads):
        for j in range(levels):
            @pl.when(jnp.logical_and(j <= level, slot_of(kv) + j >= slots))
            def _():
                gather_down(kv, j)

    @pl.when(me < n - 1)
    def _():
        edge.wait_recv()
        after = jnp.concatenate([jnp.zeros((8, wide), F32), gn[:8].astype(F32)], axis=0)
        taps = w_ref[...].astype(F32)
        fix = None
        for tap in range(taps.shape[0]):
            offset = taps.shape[0] - 1 - tap
            term = taps[tap:tap + 1] * after[offset:offset + 8]
            fix = term if fix is None else fix + term
        dx_ref[rows - 8:] += fix
        for off in range(m):
            before(off).wait_recv()

    @pl.when(me == n - 1)
    def _():
        nb[...] = jnp.zeros(nb.shape, nb.dtype)

    total = dbcb[...].astype(F32)
    for off in range(1, m):
        across(off).wait_recv()
        total += bb[off].astype(F32)
    follow = nb[0].astype(F32)
    for off in range(1, m):
        follow += nb[off].astype(F32)
    dbc_out[...] = conv_back(total * bcsl[...], (follow * bcsn[...])[:8], wbc)

    for off in range(1, m):
        across(off).wait_send()

    @pl.when(me > 0)
    def _():
        edge.wait_send()
        for off in range(m):
            before(off).wait_send()

    for kv in range(kv_heads):
        for j in range(levels):
            @pl.when(sends_over(j))
            def _():
                pass_over(kv, j).wait_send()

            @pl.when(j < level)
            def _():
                pass_down(kv, j).wait_send()

    def drain(i, carry):
        @pl.when(not_top)
        def _():
            copy(sf, af, cfs, cfr, i, up).wait_send()

        @pl.when(level > 0)
        def _():
            copy(sb, ab, cbs, cbr, i, down).wait_send()

        @pl.when(send_tf)
        def _():
            trade(i, 0).wait_send()

        @pl.when(send_tb)
        def _():
            trade(i, 1).wait_send()

        @pl.when(give_f)
        def _():
            give(mf, s_in, mfs, mfr, i, base).wait_send()

        @pl.when(give_b)
        def _():
            give(mb, g_in, mbs, mbr, i, base).wait_send()

        return carry

    lax.fori_loop(0, share, drain, 0)
    relay_sent()

    @pl.when(me < n - 1)
    def _():
        cb.wait_send()
        cx.wait_send()

    @pl.when(me > 0)
    def _():
        cn.wait_send()


def block_part(n, m, x_in, bc_in, conv_x, conv_bc, log_decay, skip, queries, keys, values, d_mixed):
    rows, wide = x_in.shape
    width = keys.shape[1]
    heads = wide // D
    pairs = heads // 2
    share = pairs // 2
    kv_heads = width // D
    length = n * rows
    taps = conv_x.shape[0]
    dma = pltpu.SemaphoreType.DMA
    shape = jax.ShapeDtypeStruct

    def v(dims, dtype=F32):
        return pltpu.VMEM(dims, dtype)

    def stay(a):
        return pltpu.with_memory_space_constraint(a, pltpu.HBM)

    state = (share, D, W)
    return pl.pallas_call(
        functools.partial(block_kernel, n, m),
        out_shape=(
            shape((rows, wide), BF16), shape((rows, wide), F32), shape((rows, width), F32),
            shape((rows, width), F32), shape((rows, wide), F32), shape((rows, W), F32),
            shape((heads, rows), F32)),
        in_specs=[HBM] * 5 + [SMEM] + [HBM] * 4,
        out_specs=(VMEM,) * 7,
        scratch_shapes=[
            v((rows, wide), BF16), v((rows, wide), BF16), v((rows, wide), BF16), v((taps, wide), BF16),
            v(bc_in.shape, BF16), v(conv_bc.shape, BF16), v((heads, rows)), v((rows, W), BF16),
            v((n, rows, 2 * width), BF16), v((EDGE, wide), BF16), v((EDGE, W), BF16), v((EDGE, W), BF16),
            v((rows, wide), BF16), v((rows, wide)), v((rows, wide)), v((rows, wide), BF16),
            v((rows, wide), BF16), v((rows, wide)), v((rows, wide)), v((rows, wide)),
            v((rows, W), BF16), v((rows, W)), v((EDGE, W)), v((D, rows), BF16), v((D, rows), BF16),
            v((pairs, 1, W)), v((pairs, 1, W)), v((share, 1, W)), v((rows, W)), v((rows, W)),
            v((rows, rows)), v((rows, W)), v((rows, W), BF16), v((heads, rows)), v((heads, rows)),
            v(state, BF16), v(state, BF16), v(state), v(state),
            *[v(state, BF16) for _ in range(8)],
            v((pairs, D, W), BF16), v((pairs, D, W), BF16),
            v((length, W)), v((length, W), BF16), v((length, W), BF16), v((D, length), BF16),
            v((D + EDGE, length), BF16), v((length, D), BF16), v((2 * rows, D), BF16), v((length, D)),
            v((length, D)), v((kv_heads, n, rows, W), BF16), v((kv_heads, n // 2, rows, W), BF16),
            v((kv_heads, n // 2, rows, W), BF16), v((rows, W)),
            v((EDGE, wide), BF16), v((EDGE, wide), BF16), v((m, rows, W), BF16), v((m, EDGE, W), BF16),
            dma((9,)), dma((n,)), dma((n,)), dma((n,)), dma((n,)), dma((3,)), dma((3,)),
            dma((share,)), dma((share,)), dma((share,)), dma((share,)), dma, dma,
            *[dma((share,)) for _ in range(8)],
            *[dma((kv_heads, n // 2)) for _ in range(4)], dma, dma, dma((m,)), dma((m,)), dma((m,)), dma((m,))],
        compiler_params=pltpu.CompilerParams(
            collective_id=0, has_side_effects=True, vmem_limit_bytes=40 * 2**20),
        name="block",
    )(*map(stay, (x_in, bc_in, conv_x, conv_bc, log_decay.T)), skip,
      *map(stay, (queries, keys, values, d_mixed)))


def write_kernel(mixed, dq, dk, dv, dx, dbc, dla, mixed_o, dq_o, dk_o, dv_o, dx_o, dbc_o, dla_o, dbc3, sem):
    copies = [(dq, dq_o), (dx, dx_o), (mixed, mixed_o), (dk, dk_o), (dv, dv_o), (dla, dla_o), (dbc3, dbc_o)]
    copies = [pltpu.make_async_copy(src, dst, sem.at[i]) for i, (src, dst) in enumerate(copies)]
    for cp in copies[:-1]:
        cp.start()
    dbc3[:, 0, :] = dbc[:, :D]
    dbc3[:, 1, :] = dbc[:, D:]
    copies[-1].start()
    for cp in copies:
        cp.wait()


def write_part(mixed, dq, dk, dv, dx, dbc, dla):
    rows = dbc.shape[0]
    outs = tuple(jax.ShapeDtypeStruct(a.shape, a.dtype) for a in (mixed, dq, dk, dv, dx))
    outs += (jax.ShapeDtypeStruct((rows, 2, D), F32), jax.ShapeDtypeStruct(dla.shape, F32))
    return pl.pallas_call(
        write_kernel,
        out_shape=outs,
        in_specs=[VMEM] * 7,
        out_specs=(HBM,) * 7,
        scratch_shapes=[pltpu.VMEM((rows, 2, D), F32), pltpu.SemaphoreType.DMA((7,))],
        compiler_params=pltpu.CompilerParams(vmem_limit_bytes=2 * 2**20),
        name="write",
    )(mixed, dq, dk, dv, dx, dbc, dla)


def shards(n, m, *args):
    *outs, dla = write_part(*block_part(n, m, *args))
    return (*outs, dla.T)


def solution(mesh):
    n, m = mesh.shape["seq"], mesh.shape["head"]
    grid = P("seq", "head")
    part = P("seq", None, None)
    in_specs = (grid, part, P(None, "head"), P(), grid, P("head"), grid, grid, grid, grid)
    out_specs = (grid, grid, grid, grid, grid, part, grid)
    return jax.shard_map(functools.partial(shards, n, m), mesh=mesh, in_specs=in_specs,
                         out_specs=out_specs, check_vma=False)
```

```python
import functools
import math

import jax
import jax.numpy as jnp
from jax import lax
from jax.experimental import pallas as pl
from jax.experimental.pallas import tpu as pltpu
from jax.sharding import PartitionSpec as P

D = 128
W = 2 * D
EDGE = 16
F32 = jnp.float32
BF16 = jnp.bfloat16
MESH = pl.DeviceIdType.MESH
VMEM = pl.BlockSpec(memory_space=pltpu.VMEM)
HBM = pl.BlockSpec(memory_space=pltpu.HBM)
SMEM = pl.BlockSpec(memory_space=pltpu.SMEM)
SCALE = D ** (-0.5)
LOG2 = SCALE * math.log2(math.e)


def mm(a, b):
    return jnp.dot(a, b, preferred_element_type=F32)


def mm_nt(a, b):
    return lax.dot_general(a, b, (((1,), (1,)), ((), ())), preferred_element_type=F32)


def sigmoid(v):
    return 1.0 / (1.0 + jnp.exp(-v))


def peer(**coords):
    return dict(device_id=coords, device_id_type=MESH)


def split3(v):
    hi = v.astype(BF16)
    rest = v - hi.astype(F32)
    mid = rest.astype(BF16)
    return hi, mid, (rest - mid.astype(F32)).astype(BF16)


def exact(dot, a, b):
    if a.dtype == BF16:
        hi, mid, lo = split3(b)
        return (dot(a, hi) + dot(a, mid)) + dot(a, lo)
    hi, mid, lo = split3(a)
    return (dot(hi, b) + dot(mid, b)) + dot(lo, b)


def conv(x, halo, taps):
    width = taps.shape[0]
    rows = x.shape[0]
    full = jnp.concatenate([halo[EDGE - 8:], x], axis=0)
    total = None
    for tap in range(width):
        start = 8 - (width - 1) + tap
        term = taps[tap:tap + 1] * full[start:start + rows]
        total = term if total is None else total + term
    return total


def conv_back(grads, after, taps):
    width = taps.shape[0]
    rows = grads.shape[0]
    padded = jnp.concatenate([grads, after], axis=0)
    total = None
    for tap in range(width):
        offset = width - 1 - tap
        term = taps[tap:tap + 1] * padded[offset:offset + rows]
        total = term if total is None else total + term
    return total


def iota(shape, axis):
    return lax.broadcasted_iota(jnp.int32, shape, axis)


def block_kernel(n, m, x_hbm, bc_hbm, w_hbm, wbc_hbm, ld_hbm, skip_ref, q_hbm, k_hbm, v_hbm, dm_hbm,
                 mixed_ref, dq_ref, dk_out, dv_out, dx_ref, dbc_out, dla_ref,
                 x_ref, dm_ref, q_ref, w_ref, bc3, wbc3, ld_ref, bcs, kva, xh, bch, bcn,
                 xb_ref, sl_ref, col_ref, xt_ref, dme_ref, y_ref, gx_ref, att_ref,
                 bcv, bcsl, bcsn, bt, ct, rowp, dec, rdec, inner, innert, dinner, dbc, dbcb, net_ref, fin_ref,
                 of, ob, sm, gm, af, ab, sf, sb, mf, mb, xf_ref, xg_ref,
                 s_ref, eb_ref, ds_ref, kt, vt, ek, eq, dka, dva, part, landy, landz, acc,
                 gh, gn, bb, nb,
                 ls, zs, zr, fs, fr, hs, hr, es, er,
                 cfs, cfr, cbs, cbr, mfs, mfr, mbs, mbr, pys, pyr, pzs, pzr, xs, xr, bs, br, ns, nr):
    me = lax.axis_index("seq")
    my = lax.axis_index("head")
    odd = lax.rem(me, 2)
    is_odd = odd == 1
    mate = me + 1 - 2 * odd
    level = me // 2
    levels = n // 2
    rows, wide = x_ref.shape
    width = k_hbm.shape[1]
    heads = wide // D
    pairs = heads // 2
    kv_heads = width // D
    ratio = heads // kv_heads
    length = n * rows
    nxt = lax.rem(me + 1, n)
    prv = lax.rem(me + n - 1, n)
    up = lax.rem(me + 2, n)
    down = lax.rem(me + n - 2, n)

    barrier = pltpu.get_barrier_semaphore()
    count = 0
    for off in range(1, n):
        pl.semaphore_signal(barrier, inc=1, **peer(seq=lax.rem(me + off, n), head=my))
        count += 1
    for off in range(1, m):
        for to in (me, nxt, prv):
            pl.semaphore_signal(barrier, inc=1, **peer(seq=to, head=lax.rem(my + off, m)))
            count += 1

    loads = [(ld_hbm, ld_ref)]
    for kv in range(kv_heads):
        lanes = pl.ds(kv * D, D)
        loads.append((k_hbm.at[:, lanes], kva.at[kv, me, :, pl.ds(0, D)]))
        loads.append((v_hbm.at[:, lanes], kva.at[kv, me, :, pl.ds(D, D)]))
    loads += [
        (bc_hbm, bc3), (wbc_hbm, wbc3), (w_hbm, w_ref), (x_hbm, x_ref), (dm_hbm, dm_ref), (q_hbm, q_ref)]
    loads = [pltpu.make_async_copy(src, dst, ls.at[i]) for i, (src, dst) in enumerate(loads)]
    for cp in loads:
        cp.start()

    t_i = iota((rows, rows), 0)
    s_i = iota((rows, rows), 1)
    lower = jnp.where(t_i >= s_i, 1.0, 0.0).astype(BF16)
    loads[0].wait()
    cum = exact(mm_nt, lower, ld_ref[...])
    parts = split3(cum)
    ident = jnp.where(iota((heads, heads), 0) == iota((heads, heads), 1), 1.0, 0.0).astype(BF16)
    cum_rows = (mm_nt(ident, parts[0]) + mm_nt(ident, parts[1])) + mm_nt(ident, parts[2])
    for h in range(heads):
        rowp[h // 2, :, (h % 2) * D:(h % 2) * D + D] = cum_rows[h:h + 1]

    def column(p, first):
        pick = jnp.where(iota((heads, W), 0) == 2 * p + iota((heads, W), 1) // D, 1.0, 0.0).astype(BF16)
        return (mm(parts[0][first:], pick) + mm(parts[1][first:], pick)) + mm(parts[2][first:], pick)

    def decay(p, carry):
        dec[p] = jnp.exp(column(p, rows - EDGE)[EDGE - 1:])
        return carry

    lax.fori_loop(0, pairs, decay, 0)

    cross = max(levels // 4, 1)
    early = level < cross
    for off in range(1, n):
        fill = me + off < n
        if off == 1:
            fill = jnp.logical_and(fill, jnp.logical_or(is_odd, jnp.logical_not(early)))

        @pl.when(fill)
        def _():
            for kv in range(kv_heads):
                kva[kv, lax.rem(me + off, n)] = jnp.zeros(kva.shape[2:], kva.dtype)

    big = -(2.0 ** 100)
    e_i = iota((rows, D), 1)
    r_i = iota((rows, D), 0)
    inside = jnp.where((r_i == e_i) & (e_i > 0), big, 0.0).astype(BF16)
    outside = jnp.where(e_i == 0, big, 0.0).astype(BF16)
    for j in range(n):
        later = jnp.where(me < j, outside, jnp.zeros_like(outside))
        ek[j * rows:(j + 1) * rows] = jnp.where(me == j, inside, later)
    reach = jnp.where((e_i > r_i) | (e_i == 0), 1.0, 0.0).astype(BF16)
    eq[:rows] = reach
    eq[rows:] = reach
    vt[D:] = jnp.ones((vt.shape[0] - D, length), BF16)

    for cp in loads[1:-2]:
        cp.wait()
    bcs[:, :D] = bc3[...].astype(F32)[:, 0, :].astype(BF16)
    bcs[:, D:] = bc3[...].astype(F32)[:, 1, :].astype(BF16)
    wbc = jnp.concatenate([wbc3[...].astype(F32)[:, 0, :], wbc3[...].astype(F32)[:, 1, :]], axis=1)
    pl.semaphore_wait(barrier, count)

    def halo(slot, src, dst, to):
        return pltpu.make_async_remote_copy(
            src_ref=src, dst_ref=dst, send_sem=hs.at[slot], recv_sem=hr.at[slot],
            **peer(seq=to, head=my))

    last = pl.ds(rows - EDGE, EDGE)
    cx = halo(0, x_ref.at[last], xh, nxt)
    cb = halo(1, bcs.at[last], bch, nxt)
    cn = halo(2, bcs.at[pl.ds(0, EDGE)], bcn, prv)

    swap = pltpu.make_async_remote_copy(
        src_ref=dec, dst_ref=rdec, send_sem=es, recv_sem=er, **peer(seq=mate, head=my))
    swap.start()

    @pl.when(me < n - 1)
    def _():
        cb.start()
        cx.start()

    @pl.when(me > 0)
    def _():
        cn.start()

    par = odd

    def rise(kv, blk):
        return pltpu.make_async_remote_copy(
            src_ref=kva.at[kv, blk], dst_ref=kva.at[kv, blk], send_sem=zs.at[kv, blk],
            recv_sem=zr.at[kv, blk], **peer(seq=up, head=my))

    def over(kv, blk):
        return pltpu.make_async_remote_copy(
            src_ref=kva.at[kv, blk], dst_ref=kva.at[kv, blk], send_sem=fs.at[kv, blk],
            recv_sem=fr.at[kv, blk], **peer(seq=mate, head=my))

    not_top = level < levels - 1
    crosses = jnp.logical_or(odd == 0, early)
    for kv in range(kv_heads):
        @pl.when(not_top)
        def _():
            rise(kv, me).start()

        @pl.when(crosses)
        def _():
            over(kv, me).start()

    def relay_first(kv):
        @pl.when(early)
        def _():
            over(kv, mate).wait_recv()
            rise(kv, mate).start()

    def relay_mine(kv, k):
        @pl.when(level >= k)
        def _():
            blk = 2 * (level - k) + par
            rise(kv, blk).wait_recv()

            @pl.when(not_top)
            def _():
                rise(kv, blk).start()

            @pl.when(level - k >= cross)
            def _():
                over(kv, blk).start()

    def relay_other(kv, k):
        @pl.when(jnp.logical_and(level >= k, level - k < cross))
        def _():
            blk = 2 * (level - k) + 1 - par
            rise(kv, blk).wait_recv()

            @pl.when(not_top)
            def _():
                rise(kv, blk).start()

    def relayed(kv):
        @pl.when(jnp.logical_and(odd == 1, jnp.logical_not(early)))
        def _():
            over(kv, mate).wait_recv()

        for k in range(1, levels):
            @pl.when(jnp.logical_and(level >= k, level - k >= cross))
            def _():
                over(kv, 2 * (level - k) + 1 - par).wait_recv()

    def relay_sent(kv):
        @pl.when(not_top)
        def _():
            rise(kv, me).wait_send()

        @pl.when(crosses)
        def _():
            over(kv, me).wait_send()

        @pl.when(early)
        def _():
            rise(kv, mate).wait_send()

        for k in range(1, levels):
            far = level - k

            @pl.when(jnp.logical_and(level >= k, not_top))
            def _():
                rise(kv, 2 * far + par).wait_send()

            @pl.when(jnp.logical_and(level >= k, far >= cross))
            def _():
                over(kv, 2 * far + par).wait_send()

            @pl.when(jnp.logical_and(jnp.logical_and(level >= k, far < cross), not_top))
            def _():
                rise(kv, 2 * far + 1 - par).wait_send()

    def event(kv, k):
        if k == 0:
            relay_first(kv)
        else:
            relay_other(kv, k)
        if k < levels - 1:
            relay_mine(kv, k + 1)

    events = [functools.partial(event, kv, k) for k in range(levels) for kv in range(kv_heads)]
    events.pop(0)()

    @pl.when(me == 0)
    def _():
        xh[...] = jnp.zeros(xh.shape, xh.dtype)
        bch[...] = jnp.zeros(bch.shape, bch.dtype)

    @pl.when(me == n - 1)
    def _():
        bcn[...] = jnp.zeros(bcn.shape, bcn.dtype)

    loads[-2].wait()
    loads[-1].wait()

    @pl.when(me > 0)
    def _():
        cb.wait_recv()
        cx.wait_recv()

    @pl.when(me < n - 1)
    def _():
        cn.wait_recv()

    def slope(pre, sig):
        return sig * (1.0 + pre * (1.0 - sig))

    pre = conv(bcs[...].astype(F32), bch[...].astype(F32), wbc)
    sig = sigmoid(pre)
    act = (pre * sig).astype(BF16)
    bcv[...] = act
    bcsl[...] = slope(pre, sig)
    pre = conv(bcn[...].astype(F32), bcs[rows - EDGE:].astype(F32), wbc)
    bcsn[...] = slope(pre, sigmoid(pre))
    act = act.astype(F32)
    bt[...] = jnp.transpose(act[:, :D]).astype(BF16)
    ct[...] = jnp.transpose(act[:, D:]).astype(BF16)
    b = bcv[:, :D]
    c = bcv[:, D:]
    own_inner = mm_nt(c, b)
    own_innert = mm_nt(b, c)
    for a in range(2):
        inner[:, a * D:(a + 1) * D] = own_inner
        innert[:, a * D:(a + 1) * D] = own_innert
    dinner[...] = jnp.zeros_like(dinner)
    dbc[...] = jnp.zeros_like(dbc)

    bottom = level == 0
    top_level = level == levels - 1
    give_f = jnp.logical_or(odd == 0, jnp.logical_not(bottom))
    take_f = jnp.logical_or(is_odd, jnp.logical_not(bottom))
    give_b = jnp.logical_or(is_odd, jnp.logical_not(top_level))
    take_b = jnp.logical_or(odd == 0, jnp.logical_not(top_level))

    @pl.when(jnp.logical_not(take_f))
    def _():
        xf_ref[...] = jnp.zeros(xf_ref.shape, BF16)

    @pl.when(jnp.logical_not(take_b))
    def _():
        xg_ref[...] = jnp.zeros(xg_ref.shape, BF16)

    def wide_of(p):
        return pl.ds(pl.multiple_of(p * W, W), W)

    def own(p):
        lanes = wide_of(p)
        pre = conv(x_ref[:, lanes].astype(F32), xh[:, lanes].astype(F32), w_ref[:, lanes].astype(F32))
        sig = sigmoid(pre)
        xb = (pre * sig).astype(BF16)
        xb_ref[:, lanes] = xb
        sl_ref[:, lanes] = slope(pre, sig)
        col = column(p, 0)
        col_ref[:, lanes] = col
        final = col[rows - 1:]
        xt = (xb.astype(F32) * jnp.exp(final - col)).astype(BF16)
        dme = (dm_ref[:, lanes].astype(F32) * jnp.exp(col)).astype(BF16)
        xt_ref[:, lanes] = xt
        dme_ref[:, lanes] = dme
        of[p] = mm(bt[...], xt)
        ob[p] = mm(ct[...], dme)

        @pl.when(bottom)
        def _():
            hop_f(p)

        @pl.when(top_level)
        def _():
            hop_b(p)

    def skips(p):
        return jnp.where(iota((1, W), 1) < D, skip_ref[2 * p], skip_ref[2 * p + 1])

    t_w = iota((rows, W), 0)
    s_w = lax.rem(iota((rows, W), 1), D)

    def within(p):
        lanes = wide_of(p)
        xb = xb_ref[:, lanes]
        dm = dm_ref[:, lanes]
        gap = col_ref[:, lanes] - rowp[p]
        fade = jnp.exp(jnp.where(t_w >= s_w, gap, -1e30))
        fadet = jnp.exp(jnp.where(s_w >= t_w, -gap, -1e30))
        mix = (inner[...] * fade).astype(BF16)
        mixt = (innert[...] * fadet).astype(BF16)
        skip = skips(p)
        total = None
        ys, gs = [], []
        for a in range(2):
            cols = slice(a * D, (a + 1) * D)
            ys.append(mm(mix[:, cols], xb[:, cols]))
            gs.append(mm(mixt[:, cols], dm[:, cols]))
            term = mm_nt(dm[:, cols], xb[:, cols]) * fade[:, cols]
            total = term if total is None else total + term
        dinner[...] += total
        y_ref[:, lanes] = jnp.concatenate(ys, axis=1) + skip * xb.astype(F32)
        gx_ref[:, lanes] = jnp.concatenate(gs, axis=1) + skip * dm.astype(F32)

    def unit(i, carry):
        @pl.when(i < pairs)
        def _():
            own(i)

        @pl.when(i >= pairs)
        def _():
            within(i - pairs)

        return carry

    def copy(stage, landing, send, recv, i, to):
        return pltpu.make_async_remote_copy(
            src_ref=stage.at[i], dst_ref=landing.at[i], send_sem=send.at[i], recv_sem=recv.at[i],
            **peer(seq=to, head=my))

    def climb(i):
        return copy(sf, af, cfs, cfr, i, up)

    def descend(i):
        return copy(sb, ab, cbs, cbr, i, down)

    def give(i, which):
        src, dst, send, recv = ((mf, xf_ref, mfs, mfr), (mb, xg_ref, mbs, mbr))[which]
        return copy(src, dst, send, recv, i, mate)

    def decays(i):
        mine, other = dec[i], rdec[i]
        return jnp.where(is_odd, other, mine), jnp.where(is_odd, mine, other)

    def hop_f(i):
        @pl.when(bottom)
        def _():
            af[i] = jnp.zeros(af.shape[1:], BF16)

        @pl.when(jnp.logical_not(bottom))
        def _():
            climb(i).wait_recv()

        even_d, odd_d = decays(i)
        x = af[i].astype(F32)
        mine = of[i]
        near = even_d * x
        mf[i] = jnp.where(is_odd, x, near + mine).astype(BF16)
        sm[i] = jnp.where(is_odd, near, x)

        @pl.when(not_top)
        def _():
            sf[i] = (odd_d * near + jnp.where(is_odd, 1.0, odd_d) * mine).astype(BF16)
            climb(i).start()

        @pl.when(give_f)
        def _():
            give(i, 0).start()

    def hop_b(i):
        @pl.when(top_level)
        def _():
            ab[i] = jnp.zeros(ab.shape[1:], BF16)

        @pl.when(not_top)
        def _():
            descend(i).wait_recv()

        even_d, odd_d = decays(i)
        x = ab[i].astype(F32)
        mine = ob[i]
        near = odd_d * x
        mb[i] = jnp.where(is_odd, near + mine, x).astype(BF16)
        gm[i] = jnp.where(is_odd, x, near)

        @pl.when(jnp.logical_not(bottom))
        def _():
            sb[i] = (even_d * near + jnp.where(is_odd, even_d, 1.0) * mine).astype(BF16)
            descend(i).start()

        @pl.when(give_b)
        def _():
            give(i, 1).start()

    def hops(t):
        f = t - 2 * (level - 1)
        g = t - 2 * (levels - 2 - level)

        @pl.when(jnp.logical_and(jnp.logical_not(bottom), jnp.logical_and(f >= 0, f < pairs)))
        def _():
            hop_f(f)

        @pl.when(jnp.logical_and(not_top, jnp.logical_and(g >= 0, g < pairs)))
        def _():
            hop_b(g)

    swap.wait()
    slow = 2 * (levels - 2)
    done = 0
    early_events = max(len(events) - slow, 0)
    for i in range(early_events):
        events.pop(0)()
        upto = pairs * (i + 1) // early_events
        lax.fori_loop(done, upto, unit, 0)
        done = upto
    lax.fori_loop(done, pairs, unit, 0)
    done = pairs
    for t in range(slow):
        hops(t)
        upto = pairs + pairs * (t + 1) // slow
        lax.fori_loop(done, upto, unit, 0)
        done = upto
        if t < slow - 1 and len(events) > kv_heads - 1:
            events.pop(0)()
    while len(events) > kv_heads - 1:
        events.pop(0)()
    relayed(0)
    rest = range(1, kv_heads)

    def plain(kv):
        return kv < kv_heads - 1

    def swap_over(kv):
        return pltpu.make_async_remote_copy(
            src_ref=part.at[kv, mate], dst_ref=landy.at[kv, 0], send_sem=pys.at[kv, 0],
            recv_sem=pyr.at[kv, 0], **peer(seq=mate, head=my))

    def pass_both(kv, j):
        return pltpu.make_async_remote_copy(
            src_ref=part.at[kv, pl.ds(2 * j, 2)], dst_ref=landz.at[kv, j], send_sem=pzs.at[kv, j],
            recv_sem=pzr.at[kv, j], **peer(seq=down, head=my))

    def pass_over(kv, j):
        return pltpu.make_async_remote_copy(
            src_ref=part.at[kv, 2 * j + 1 - par], dst_ref=landy.at[kv, j], send_sem=pys.at[kv, j],
            recv_sem=pyr.at[kv, j], **peer(seq=mate, head=my))

    def pass_down(kv, j):
        return pltpu.make_async_remote_copy(
            src_ref=part.at[kv, 2 * j + par], dst_ref=landz.at[kv, j, 0], send_sem=pzs.at[kv, j],
            recv_sem=pzr.at[kv, j], **peer(seq=down, head=my))

    def sends_over(j):
        return jnp.logical_or(j < level, jnp.logical_and(j == level, is_odd))

    def takes_over(j):
        return jnp.logical_or(j < level, jnp.logical_and(j == level, odd == 0))

    def result(kv, total):
        cols = slice(kv * D, kv * D + D)
        dk_out[:, cols] = total[:, :D]
        dv_out[:, cols] = total[:, D:]

    def gather_down(kv, j):
        if plain(kv):
            @pl.when(not_top)
            def _():
                pass_both(kv, j).wait_recv()
                both = pl.ds(2 * j, 2)
                part[kv, both] = (part[kv, both].astype(F32) + landz[kv, j].astype(F32)).astype(BF16)

            @pl.when(j < level)
            def _():
                pass_both(kv, j).start()

            @pl.when(j == level)
            def _():
                swap_over(kv).start()

            return

        acc[...] = part[kv, 2 * j + par].astype(F32)

        @pl.when(takes_over(j))
        def _():
            pass_over(kv, j).wait_recv()
            acc[...] += landy[kv, j].astype(F32)

        @pl.when(not_top)
        def _():
            pass_down(kv, j).wait_recv()
            acc[...] += landz[kv, j, 0].astype(F32)

        @pl.when(j < level)
        def _():
            part[kv, 2 * j + par] = acc[...].astype(BF16)
            pass_down(kv, j).start()

        @pl.when(j == level)
        def _():
            result(kv, acc[...])

    def gathered(kv):
        if plain(kv):
            swap_over(kv).wait_recv()
            result(kv, part[kv, me].astype(F32) + landy[kv, 0].astype(F32))

    def gather_sent(kv):
        if plain(kv):
            swap_over(kv).wait_send()
        for j in range(levels):
            if not plain(kv):
                @pl.when(sends_over(j))
                def _():
                    pass_over(kv, j).wait_send()

            @pl.when(j < level)
            def _():
                (pass_both if plain(kv) else pass_down)(kv, j).wait_send()

    slots = 2 * pairs

    def slot_of(kv):
        ready = (kv + 1) * (ratio // 2) - 1
        behind = levels - 1 - level
        if plain(kv):
            return ready + 3 * behind, jnp.where(behind == 0, 0, 2)
        return ready + 4 + 4 * behind, 1

    def gathers(t):
        for kv in range(kv_heads):
            first, pace = slot_of(kv)
            for j in range(levels):
                @pl.when(jnp.logical_and(j <= level, first + pace * j == t))
                def _():
                    gather_down(kv, j)

    def lanes_of(h):
        return pl.ds(pl.multiple_of(h * D, D), D)

    tile = W if length % W == 0 else D
    many = tile // rows

    def attend(p):
        h = 2 * p
        kv = h // ratio
        first, second = lanes_of(h), lanes_of(h + 1)

        @pl.when(lax.rem(h, ratio) == 0)
        def _():
            kt[...] = jnp.transpose(kva[kv, :, :, :D].reshape(length, D).astype(F32)).astype(BF16)
            vt[:D] = jnp.transpose(kva[kv, :, :, D:].reshape(length, D).astype(F32)).astype(BF16)
            dka[...] = jnp.zeros_like(dka)
            dva[...] = jnp.zeros_like(dva)

        q = jnp.concatenate([q_ref[:, first], q_ref[:, second]], axis=0)
        dm = jnp.concatenate([dm_ref[:, first], dm_ref[:, second]], axis=0)
        qe = jnp.concatenate([q, eq[...]], axis=1)
        top = None
        for j in range(length // tile):
            at = slice(j * tile, (j + 1) * tile)
            k = kva[kv, j * many:(j + 1) * many, :, :D].reshape(tile, D)
            s = mm_nt(jnp.concatenate([k, ek[at]], axis=1), qe)
            s_ref[at] = s
            high = jnp.max(s.reshape(tile // 8, 8, 2 * rows), axis=0)
            top = high if top is None else jnp.maximum(top, high)
        top = jnp.max(top, axis=0, keepdims=True) * LOG2
        for j in range(length // tile):
            at = slice(j * tile, (j + 1) * tile)
            e = jnp.exp2(s_ref[at] * LOG2 - top)
            s_ref[at] = e
            eb_ref[at] = e.astype(BF16)
        out_t = mm(vt[...], eb_ref[...])
        inv = 1.0 / out_t[D:D + 1]
        out_t = out_t[:D] * inv
        out = jnp.transpose(out_t)
        att_ref[:, first] = out[:rows]
        att_ref[:, second] = out[rows:]
        delta = jnp.sum(jnp.transpose(dm.astype(F32)) * out_t, axis=0, keepdims=True)
        for j in range(length // tile):
            at = slice(j * tile, (j + 1) * tile)
            v = kva[kv, j * many:(j + 1) * many, :, D:].reshape(tile, D)
            ds_ref[at] = (s_ref[at] * (mm_nt(v, dm) - delta)).astype(BF16)
        dq = jnp.transpose(mm(kt[...], ds_ref[...]) * (inv * SCALE))
        dq_ref[:, first] = dq[:rows]
        dq_ref[:, second] = dq[rows:]
        inv_col = jnp.transpose(jnp.broadcast_to(inv, (D, 2 * rows)))
        dka[...] += mm(ds_ref[...], (q.astype(F32) * inv_col).astype(BF16))
        dva[...] += mm(eb_ref[...], (dm.astype(F32) * inv_col).astype(BF16))

        @pl.when(lax.rem(h, ratio) == ratio - 2)
        def _():
            part[kv, :, :, :D] = (dka[...] * SCALE).astype(BF16).reshape(n, rows, D)
            part[kv, :, :, D:] = dva[...].astype(BF16).reshape(n, rows, D)

        @pl.when(p == (kv_heads * ratio) // 2 - 1)
        def _():
            for j in range(levels):
                @pl.when(sends_over(j))
                def _():
                    pass_over(kv_heads - 1, j).start()

    def step(t, carry):
        for kv in rest:
            @pl.when(t == kv * (ratio // 2))
            def _():
                events[kv - 1]()
                relayed(kv)

        hops(slow + t)
        attend(t)
        gathers(t)
        return carry

    lax.fori_loop(0, pairs, step, 0)

    ones = jnp.ones((EDGE, D), BF16)

    def edge(i):
        return copy(gh, gn, xs, xr, i, prv)

    def through(i, carry):
        p = i
        lanes = wide_of(p)

        @pl.when(take_f)
        def _():
            give(p, 0).wait_recv()

        @pl.when(take_b)
        def _():
            give(p, 1).wait_recv()

        state = (sm[p] + xf_ref[p].astype(F32)).astype(BF16)
        grad = (gm[p] + xg_ref[p].astype(F32)).astype(BF16)
        xf = xb_ref[:, lanes].astype(F32)
        dmf = dm_ref[:, lanes].astype(F32)
        col = col_ref[:, lanes]
        final = col[rows - 1:]
        back = jnp.exp(final - col) * mm(b, grad)
        y = y_ref[:, lanes] + jnp.exp(col) * mm(c, state)
        mixed_ref[:, lanes] = (y + att_ref[:, lanes]).astype(BF16)
        gx = gx_ref[:, lanes] + back
        net = dmf * y - xf * gx
        hi = net.astype(BF16)
        lo = (net - hi.astype(F32)).astype(BF16)
        inside = jnp.sum(xf * back, axis=0, keepdims=True) + jnp.exp(final) * jnp.sum(
            state.astype(F32) * grad.astype(F32), axis=0, keepdims=True)
        for a in range(2):
            cols = slice(a * D, (a + 1) * D)
            sums = mm_nt(ones, hi[:, cols]) + mm_nt(ones, lo[:, cols])
            net_ref[pl.ds(2 * p + a, 1)] = sums[:1]
            fin_ref[pl.ds(2 * p + a, 1)] = inside[:, cols]
        dbc[:, D:] += mm_nt(dme_ref[:, lanes], state)
        dbc[:, :D] += mm_nt(xt_ref[:, lanes], grad)
        g = gx * sl_ref[:, lanes]
        gh[p] = g[:EDGE].astype(BF16)

        @pl.when(me > 0)
        def _():
            edge(p).start()

        dx_ref[:, lanes] = conv_back(g, jnp.zeros((8, W), F32), w_ref[:, lanes].astype(F32))
        gathers(pairs + i)
        return carry

    lax.fori_loop(0, pairs, through, 0)
    di = dinner[...]
    dbcb[:, D:] = (dbc[:, D:] + mm(di.astype(BF16), b)).astype(BF16)
    dbcb[:, :D] = (dbc[:, :D] + mm(jnp.transpose(di).astype(BF16), c)).astype(BF16)

    def remote(src, dst, send, recv, seq, head):
        return pltpu.make_async_remote_copy(
            src_ref=src, dst_ref=dst, send_sem=send, recv_sem=recv, **peer(seq=seq, head=head))

    def across(off):
        return remote(dbcb, bb.at[off], bs.at[off], br.at[off], me, lax.rem(my + off, m))

    def before(off):
        return remote(dbcb.at[pl.ds(0, EDGE)], nb.at[off], ns.at[off], nr.at[off], prv,
                      lax.rem(my + off, m))

    for off in range(1, m):
        across(off).start()

    @pl.when(me > 0)
    def _():
        for off in range(m):
            before(off).start()

    dla_ref[...] = exact(mm, net_ref[...], lower) + exact(mm, fin_ref[...], jnp.ones((D, rows), BF16))

    for kv in range(kv_heads):
        first, pace = slot_of(kv)
        for j in range(levels):
            @pl.when(jnp.logical_and(j <= level, first + pace * j >= slots))
            def _():
                gather_down(kv, j)

    @pl.when(me < n - 1)
    def _():
        def finish(i, carry):
            lanes = wide_of(i)
            edge(i).wait_recv()
            after = jnp.concatenate([jnp.zeros((8, W), F32), gn[i].astype(F32)[:8]], axis=0)
            taps = w_ref[:, lanes].astype(F32)
            fix = None
            for tap in range(taps.shape[0]):
                offset = taps.shape[0] - 1 - tap
                term = taps[tap:tap + 1] * after[offset:offset + 8]
                fix = term if fix is None else fix + term
            dx_ref[rows - 8:, lanes] += fix
            return carry

        lax.fori_loop(0, pairs, finish, 0)
        for off in range(m):
            before(off).wait_recv()

    @pl.when(me == n - 1)
    def _():
        nb[...] = jnp.zeros(nb.shape, nb.dtype)

    total = dbcb[...].astype(F32)
    for off in range(1, m):
        across(off).wait_recv()
        total += bb[off].astype(F32)
    follow = nb[0].astype(F32)
    for off in range(1, m):
        follow += nb[off].astype(F32)
    dbc_out[...] = conv_back(total * bcsl[...], (follow * bcsn[...])[:8], wbc)

    for kv in range(kv_heads):
        gathered(kv)

    for off in range(1, m):
        across(off).wait_send()

    @pl.when(me > 0)
    def _():
        def edge_sent(i, carry):
            edge(i).wait_send()
            return carry

        lax.fori_loop(0, pairs, edge_sent, 0)
        for off in range(m):
            before(off).wait_send()

    for kv in range(kv_heads):
        gather_sent(kv)

    def drain(i, carry):
        @pl.when(not_top)
        def _():
            climb(i).wait_send()

        @pl.when(level > 0)
        def _():
            descend(i).wait_send()

        @pl.when(give_f)
        def _():
            give(i, 0).wait_send()

        @pl.when(give_b)
        def _():
            give(i, 1).wait_send()

        return carry

    lax.fori_loop(0, pairs, drain, 0)
    for kv in range(kv_heads):
        relay_sent(kv)

    @pl.when(me < n - 1)
    def _():
        cb.wait_send()
        cx.wait_send()

    @pl.when(me > 0)
    def _():
        cn.wait_send()


def block_part(n, m, x_in, bc_in, conv_x, conv_bc, log_decay, skip, queries, keys, values, d_mixed):
    rows, wide = x_in.shape
    width = keys.shape[1]
    heads = wide // D
    pairs = heads // 2
    kv_heads = width // D
    length = n * rows
    taps = conv_x.shape[0]
    dma = pltpu.SemaphoreType.DMA
    shape = jax.ShapeDtypeStruct

    def v(dims, dtype=F32):
        return pltpu.VMEM(dims, dtype)

    def stay(a):
        return pltpu.with_memory_space_constraint(a, pltpu.HBM)

    state = (pairs, D, W)
    return pl.pallas_call(
        functools.partial(block_kernel, n, m),
        out_shape=(
            shape((rows, wide), BF16), shape((rows, wide), F32), shape((rows, width), F32),
            shape((rows, width), F32), shape((rows, wide), F32), shape((rows, W), F32),
            shape((heads, rows), F32)),
        in_specs=[HBM] * 5 + [SMEM] + [HBM] * 4,
        out_specs=(VMEM,) * 7,
        scratch_shapes=[
            v((rows, wide), BF16), v((rows, wide), BF16), v((rows, wide), BF16), v((taps, wide), BF16),
            v(bc_in.shape, BF16), v(conv_bc.shape, BF16), v((heads, rows)), v((rows, W), BF16),
            v((kv_heads, n, rows, W), BF16), v((EDGE, wide), BF16), v((EDGE, W), BF16), v((EDGE, W), BF16),
            v((rows, wide), BF16), v((rows, wide)), v((rows, wide)), v((rows, wide), BF16),
            v((rows, wide), BF16), v((rows, wide)), v((rows, wide)), v((rows, wide)),
            v((rows, W), BF16), v((rows, W)), v((EDGE, W)), v((D, rows), BF16), v((D, rows), BF16),
            v((pairs, 1, W)), v((pairs, 1, W)), v((pairs, 1, W)), v((rows, W)), v((rows, W)),
            v((rows, rows)), v((rows, W)), v((rows, W), BF16), v((heads, rows)), v((heads, rows)),
            *[v(state) for _ in range(4)], *[v(state, BF16) for _ in range(8)],
            v((length, W)), v((length, W), BF16), v((length, W), BF16), v((D, length), BF16),
            v((D + EDGE, length), BF16), v((length, D), BF16), v((2 * rows, D), BF16), v((length, D)),
            v((length, D)), v((kv_heads, n, rows, W), BF16), v((kv_heads, n // 2, rows, W), BF16),
            v((kv_heads, n // 2, 2, rows, W), BF16), v((rows, W)),
            v((pairs, EDGE, W), BF16), v((pairs, EDGE, W), BF16), v((m, rows, W), BF16), v((m, EDGE, W), BF16),
            dma((2 * kv_heads + 7,)), *[dma((kv_heads, n)) for _ in range(4)], dma((3,)), dma((3,)),
            dma, dma, *[dma((pairs,)) for _ in range(8)],
            *[dma((kv_heads, n // 2)) for _ in range(4)], dma((pairs,)), dma((pairs,)), dma((m,)), dma((m,)), dma((m,)), dma((m,))],
        compiler_params=pltpu.CompilerParams(
            collective_id=0, has_side_effects=True, vmem_limit_bytes=40 * 2**20),
        name="block",
    )(*map(stay, (x_in, bc_in, conv_x, conv_bc, log_decay.T)), skip,
      *map(stay, (queries, keys, values, d_mixed)))


def write_kernel(mixed, dq, dk, dv, dx, dbc, dla, mixed_o, dq_o, dk_o, dv_o, dx_o, dbc_o, dla_o, dbc3, sem):
    copies = [(dq, dq_o), (dx, dx_o), (mixed, mixed_o), (dk, dk_o), (dv, dv_o), (dla, dla_o), (dbc3, dbc_o)]
    copies = [pltpu.make_async_copy(src, dst, sem.at[i]) for i, (src, dst) in enumerate(copies)]
    for cp in copies[:-1]:
        cp.start()
    dbc3[:, 0, :] = dbc[:, :D]
    dbc3[:, 1, :] = dbc[:, D:]
    copies[-1].start()
    for cp in copies:
        cp.wait()


def write_part(mixed, dq, dk, dv, dx, dbc, dla):
    rows = dbc.shape[0]
    outs = tuple(jax.ShapeDtypeStruct(a.shape, a.dtype) for a in (mixed, dq, dk, dv, dx))
    outs += (jax.ShapeDtypeStruct((rows, 2, D), F32), jax.ShapeDtypeStruct(dla.shape, F32))
    return pl.pallas_call(
        write_kernel,
        out_shape=outs,
        in_specs=[VMEM] * 7,
        out_specs=(HBM,) * 7,
        scratch_shapes=[pltpu.VMEM((rows, 2, D), F32), pltpu.SemaphoreType.DMA((7,))],
        compiler_params=pltpu.CompilerParams(vmem_limit_bytes=2 * 2**20),
        name="write",
    )(mixed, dq, dk, dv, dx, dbc, dla)


def shards(n, m, *args):
    *outs, dla = write_part(*block_part(n, m, *args))
    return (*outs, dla.T)


def solution(mesh):
    n, m = mesh.shape["seq"], mesh.shape["head"]
    grid = P("seq", "head")
    part = P("seq", None, None)
    in_specs = (grid, part, P(None, "head"), P(), grid, P("head"), grid, grid, grid, grid)
    out_specs = (grid, grid, grid, grid, grid, part, grid)
    return jax.shard_map(functools.partial(shards, n, m), mesh=mesh, in_specs=in_specs,
                         out_specs=out_specs, check_vma=False)
```

```python
import functools
import math

import jax
import jax.numpy as jnp
from jax import lax
from jax.experimental import pallas as pl
from jax.experimental.pallas import tpu as pltpu
from jax.sharding import PartitionSpec as P

D = 128
W = 2 * D
EDGE = 16
SLACK = 2
F32 = jnp.float32
BF16 = jnp.bfloat16
MESH = pl.DeviceIdType.MESH
VMEM = pl.BlockSpec(memory_space=pltpu.VMEM)
HBM = pl.BlockSpec(memory_space=pltpu.HBM)
SMEM = pl.BlockSpec(memory_space=pltpu.SMEM)
SCALE = D ** (-0.5)
LOG2 = SCALE * math.log2(math.e)


def mm(a, b):
    return jnp.dot(a, b, preferred_element_type=F32)


def mm_nt(a, b):
    return lax.dot_general(a, b, (((1,), (1,)), ((), ())), preferred_element_type=F32)


def sigmoid(v):
    return 1.0 / (1.0 + jnp.exp(-v))


def peer(**coords):
    return dict(device_id=coords, device_id_type=MESH)


def split3(v):
    hi = v.astype(BF16)
    rest = v - hi.astype(F32)
    mid = rest.astype(BF16)
    return hi, mid, (rest - mid.astype(F32)).astype(BF16)


def exact(dot, a, b):
    if a.dtype == BF16:
        hi, mid, lo = split3(b)
        return (dot(a, hi) + dot(a, mid)) + dot(a, lo)
    hi, mid, lo = split3(a)
    return (dot(hi, b) + dot(mid, b)) + dot(lo, b)


def conv(x, halo, taps):
    width = taps.shape[0]
    rows = x.shape[0]
    full = jnp.concatenate([halo[EDGE - 8:], x], axis=0)
    total = None
    for tap in range(width):
        start = 8 - (width - 1) + tap
        term = taps[tap:tap + 1] * full[start:start + rows]
        total = term if total is None else total + term
    return total


def conv_back(grads, after, taps):
    width = taps.shape[0]
    rows = grads.shape[0]
    padded = jnp.concatenate([grads, after], axis=0)
    total = None
    for tap in range(width):
        offset = width - 1 - tap
        term = taps[tap:tap + 1] * padded[offset:offset + rows]
        total = term if total is None else total + term
    return total


def iota(shape, axis):
    return lax.broadcasted_iota(jnp.int32, shape, axis)


def block_kernel(n, m, x_hbm, bc_hbm, w_hbm, wbc_hbm, ld_hbm, skip_ref, q_hbm, k_hbm, v_hbm, dm_hbm,
                 mixed_ref, dq_ref, dk_out, dv_out, dx_ref, dbc_out, dla_ref,
                 x_ref, dm_ref, q_ref, w_ref, bc3, wbc3, ld_ref, bcs, kva, xh, bch, bcn,
                 xb_ref, sl_ref, col_ref, xt_ref, dme_ref, y_ref, gx_ref, att_ref,
                 bcv, bcsl, bcsn, bt, ct, rowp, dec, rdec, inner, innert, dinner, dbc, dbcb, net_ref, fin_ref,
                 of, ob, sm, gm, af, ab, sf, sb, mf, mb, xf_ref, xg_ref,
                 s_ref, eb_ref, ds_ref, kt, vt, ek, eq, dka, dva, part, landy, landz, acc,
                 gh, gn, bb, nb,
                 ls, zs, zr, fs, fr, hs, hr, es, er,
                 cfs, cfr, cbs, cbr, mfs, mfr, mbs, mbr, pys, pyr, pzs, pzr, xs, xr, bs, br, ns, nr):
    me = lax.axis_index("seq")
    my = lax.axis_index("head")
    odd = lax.rem(me, 2)
    is_odd = odd == 1
    mate = me + 1 - 2 * odd
    level = me // 2
    levels = n // 2
    rows, wide = x_ref.shape
    width = k_hbm.shape[1]
    heads = wide // D
    pairs = heads // 2
    kv_heads = width // D
    ratio = heads // kv_heads
    length = n * rows
    nxt = lax.rem(me + 1, n)
    prv = lax.rem(me + n - 1, n)
    up = lax.rem(me + 2, n)
    down = lax.rem(me + n - 2, n)

    barrier = pltpu.get_barrier_semaphore()
    count = 0
    for off in range(1, n):
        pl.semaphore_signal(barrier, inc=1, **peer(seq=lax.rem(me + off, n), head=my))
        count += 1
    for off in range(1, m):
        for to in (me, nxt, prv):
            pl.semaphore_signal(barrier, inc=1, **peer(seq=to, head=lax.rem(my + off, m)))
            count += 1

    loads = [(ld_hbm, ld_ref)]
    for kv in range(kv_heads):
        lanes = pl.ds(kv * D, D)
        loads.append((k_hbm.at[:, lanes], kva.at[kv, me, :, pl.ds(0, D)]))
        loads.append((v_hbm.at[:, lanes], kva.at[kv, me, :, pl.ds(D, D)]))
    loads += [
        (bc_hbm, bc3), (wbc_hbm, wbc3), (w_hbm, w_ref), (x_hbm, x_ref), (dm_hbm, dm_ref), (q_hbm, q_ref)]
    loads = [pltpu.make_async_copy(src, dst, ls.at[i]) for i, (src, dst) in enumerate(loads)]
    for cp in loads:
        cp.start()

    t_i = iota((rows, rows), 0)
    s_i = iota((rows, rows), 1)
    lower = jnp.where(t_i >= s_i, 1.0, 0.0).astype(BF16)
    loads[0].wait()
    cum = exact(mm_nt, lower, ld_ref[...])
    parts = split3(cum)
    ident = jnp.where(iota((heads, heads), 0) == iota((heads, heads), 1), 1.0, 0.0).astype(BF16)
    cum_rows = (mm_nt(ident, parts[0]) + mm_nt(ident, parts[1])) + mm_nt(ident, parts[2])
    for h in range(heads):
        rowp[h // 2, :, (h % 2) * D:(h % 2) * D + D] = cum_rows[h:h + 1]

    def column(p, first):
        pick = jnp.where(iota((heads, W), 0) == 2 * p + iota((heads, W), 1) // D, 1.0, 0.0).astype(BF16)
        return (mm(parts[0][first:], pick) + mm(parts[1][first:], pick)) + mm(parts[2][first:], pick)

    def decay(p, carry):
        dec[p] = jnp.exp(column(p, rows - EDGE)[EDGE - 1:])
        return carry

    lax.fori_loop(0, pairs, decay, 0)

    cross = max(levels // 2, 1)
    early = level < cross
    for off in range(1, n):
        fill = me + off < n
        if off == 1:
            fill = jnp.logical_and(fill, jnp.logical_or(is_odd, jnp.logical_not(early)))

        @pl.when(fill)
        def _():
            for kv in range(kv_heads):
                kva[kv, lax.rem(me + off, n)] = jnp.zeros(kva.shape[2:], kva.dtype)

    big = -(2.0 ** 100)
    e_i = iota((rows, D), 1)
    r_i = iota((rows, D), 0)
    inside = jnp.where((r_i == e_i) & (e_i > 0), big, 0.0).astype(BF16)
    outside = jnp.where(e_i == 0, big, 0.0).astype(BF16)
    for j in range(n):
        later = jnp.where(me < j, outside, jnp.zeros_like(outside))
        ek[j * rows:(j + 1) * rows] = jnp.where(me == j, inside, later)
    reach = jnp.where((e_i > r_i) | (e_i == 0), 1.0, 0.0).astype(BF16)
    eq[:rows] = reach
    eq[rows:] = reach
    vt[D:] = jnp.ones((vt.shape[0] - D, length), BF16)

    for cp in loads[1:-2]:
        cp.wait()
    bcs[:, :D] = bc3[...].astype(F32)[:, 0, :].astype(BF16)
    bcs[:, D:] = bc3[...].astype(F32)[:, 1, :].astype(BF16)
    wbc = jnp.concatenate([wbc3[...].astype(F32)[:, 0, :], wbc3[...].astype(F32)[:, 1, :]], axis=1)
    pl.semaphore_wait(barrier, count)

    def halo(slot, src, dst, to):
        return pltpu.make_async_remote_copy(
            src_ref=src, dst_ref=dst, send_sem=hs.at[slot], recv_sem=hr.at[slot],
            **peer(seq=to, head=my))

    last = pl.ds(rows - EDGE, EDGE)
    cx = halo(0, x_ref.at[last], xh, nxt)
    cb = halo(1, bcs.at[last], bch, nxt)
    cn = halo(2, bcs.at[pl.ds(0, EDGE)], bcn, prv)

    swap = pltpu.make_async_remote_copy(
        src_ref=dec, dst_ref=rdec, send_sem=es, recv_sem=er, **peer(seq=mate, head=my))
    swap.start()

    @pl.when(me < n - 1)
    def _():
        cb.start()
        cx.start()

    @pl.when(me > 0)
    def _():
        cn.start()

    par = odd

    def rise(kv, blk):
        return pltpu.make_async_remote_copy(
            src_ref=kva.at[kv, blk], dst_ref=kva.at[kv, blk], send_sem=zs.at[kv, blk],
            recv_sem=zr.at[kv, blk], **peer(seq=up, head=my))

    def over(kv, blk):
        return pltpu.make_async_remote_copy(
            src_ref=kva.at[kv, blk], dst_ref=kva.at[kv, blk], send_sem=fs.at[kv, blk],
            recv_sem=fr.at[kv, blk], **peer(seq=mate, head=my))

    not_top = level < levels - 1
    crosses = jnp.logical_or(odd == 0, early)
    for kv in range(kv_heads):
        @pl.when(not_top)
        def _():
            rise(kv, me).start()

        @pl.when(crosses)
        def _():
            over(kv, me).start()

    def relay_first(kv):
        @pl.when(early)
        def _():
            over(kv, mate).wait_recv()
            rise(kv, mate).start()

    def relay_mine(kv, k):
        @pl.when(level >= k)
        def _():
            blk = 2 * (level - k) + par
            rise(kv, blk).wait_recv()

            @pl.when(not_top)
            def _():
                rise(kv, blk).start()

            @pl.when(level - k >= cross)
            def _():
                over(kv, blk).start()

    def relay_other(kv, k):
        @pl.when(jnp.logical_and(level >= k, level - k < cross))
        def _():
            blk = 2 * (level - k) + 1 - par
            rise(kv, blk).wait_recv()

            @pl.when(not_top)
            def _():
                rise(kv, blk).start()

    def relayed(kv):
        @pl.when(jnp.logical_and(odd == 1, jnp.logical_not(early)))
        def _():
            over(kv, mate).wait_recv()

        for k in range(1, levels):
            @pl.when(jnp.logical_and(level >= k, level - k >= cross))
            def _():
                over(kv, 2 * (level - k) + 1 - par).wait_recv()

    def relay_sent(kv):
        @pl.when(not_top)
        def _():
            rise(kv, me).wait_send()

        @pl.when(crosses)
        def _():
            over(kv, me).wait_send()

        @pl.when(early)
        def _():
            rise(kv, mate).wait_send()

        for k in range(1, levels):
            far = level - k

            @pl.when(jnp.logical_and(level >= k, not_top))
            def _():
                rise(kv, 2 * far + par).wait_send()

            @pl.when(jnp.logical_and(level >= k, far >= cross))
            def _():
                over(kv, 2 * far + par).wait_send()

            @pl.when(jnp.logical_and(jnp.logical_and(level >= k, far < cross), not_top))
            def _():
                rise(kv, 2 * far + 1 - par).wait_send()

    def event(kv, k):
        if k == 0:
            relay_first(kv)
        else:
            relay_other(kv, k)
        if k < levels - 1:
            relay_mine(kv, k + 1)

    events = [functools.partial(event, kv, k) for k in range(levels) for kv in range(kv_heads)]

    @pl.when(me == 0)
    def _():
        xh[...] = jnp.zeros(xh.shape, xh.dtype)
        bch[...] = jnp.zeros(bch.shape, bch.dtype)

    @pl.when(me == n - 1)
    def _():
        bcn[...] = jnp.zeros(bcn.shape, bcn.dtype)

    loads[-2].wait()
    loads[-1].wait()

    def wide_of(p):
        return pl.ds(pl.multiple_of(p * W, W), W)

    def prepare(p, carry):
        lanes = wide_of(p)
        sl_ref[:, lanes] = conv(
            x_ref[:, lanes].astype(F32), jnp.zeros((EDGE, W), F32), w_ref[:, lanes].astype(F32))
        col = column(p, 0)
        col_ref[:, lanes] = col
        dme_ref[:, lanes] = (dm_ref[:, lanes].astype(F32) * jnp.exp(col)).astype(BF16)
        return carry

    lax.fori_loop(0, pairs, prepare, 0)
    events.pop(0)()

    @pl.when(me > 0)
    def _():
        cb.wait_recv()
        cx.wait_recv()

    @pl.when(me < n - 1)
    def _():
        cn.wait_recv()

    def slope(pre, sig):
        return sig * (1.0 + pre * (1.0 - sig))

    pre = conv(bcs[...].astype(F32), bch[...].astype(F32), wbc)
    sig = sigmoid(pre)
    act = (pre * sig).astype(BF16)
    bcv[...] = act
    bcsl[...] = slope(pre, sig)
    pre = conv(bcn[...].astype(F32), bcs[rows - EDGE:].astype(F32), wbc)
    bcsn[...] = slope(pre, sigmoid(pre))
    act = act.astype(F32)
    bt[...] = jnp.transpose(act[:, :D]).astype(BF16)
    ct[...] = jnp.transpose(act[:, D:]).astype(BF16)
    b = bcv[:, :D]
    c = bcv[:, D:]
    own_inner = mm_nt(c, b)
    own_innert = mm_nt(b, c)
    for a in range(2):
        inner[:, a * D:(a + 1) * D] = own_inner
        innert[:, a * D:(a + 1) * D] = own_innert
    dinner[...] = jnp.zeros_like(dinner)
    dbc[...] = jnp.zeros_like(dbc)

    bottom = level == 0
    top_level = level == levels - 1
    give_f = jnp.logical_or(odd == 0, jnp.logical_not(bottom))
    take_f = jnp.logical_or(is_odd, jnp.logical_not(bottom))
    give_b = jnp.logical_or(is_odd, jnp.logical_not(top_level))
    take_b = jnp.logical_or(odd == 0, jnp.logical_not(top_level))

    @pl.when(jnp.logical_not(take_f))
    def _():
        xf_ref[...] = jnp.zeros(xf_ref.shape, BF16)

    @pl.when(jnp.logical_not(take_b))
    def _():
        xg_ref[...] = jnp.zeros(xg_ref.shape, BF16)

    def own(p):
        lanes = wide_of(p)
        pre = sl_ref[:, lanes]
        fix = conv(jnp.zeros((8, W), F32), xh[:, lanes].astype(F32), w_ref[:, lanes].astype(F32))
        pre = jnp.concatenate([pre[:8] + fix, pre[8:]], axis=0)
        sig = sigmoid(pre)
        xb = (pre * sig).astype(BF16)
        xb_ref[:, lanes] = xb
        sl_ref[:, lanes] = slope(pre, sig)
        col = col_ref[:, lanes]
        dme = dme_ref[:, lanes]
        final = col[rows - 1:]
        xt = (xb.astype(F32) * jnp.exp(final - col)).astype(BF16)
        xt_ref[:, lanes] = xt
        of[p] = mm(bt[...], xt)
        ob[p] = mm(ct[...], dme)

        @pl.when(bottom)
        def _():
            hop_f(p)

        @pl.when(top_level)
        def _():
            hop_b(p)

    def skips(p):
        return jnp.where(iota((1, W), 1) < D, skip_ref[2 * p], skip_ref[2 * p + 1])

    t_w = iota((rows, W), 0)
    s_w = lax.rem(iota((rows, W), 1), D)

    def within(p):
        lanes = wide_of(p)
        xb = xb_ref[:, lanes]
        dm = dm_ref[:, lanes]
        gap = col_ref[:, lanes] - rowp[p]
        fade = jnp.exp(jnp.where(t_w >= s_w, gap, -1e30))
        fadet = jnp.exp(jnp.where(s_w >= t_w, -gap, -1e30))
        mix = (inner[...] * fade).astype(BF16)
        mixt = (innert[...] * fadet).astype(BF16)
        skip = skips(p)
        total = None
        ys, gs = [], []
        for a in range(2):
            cols = slice(a * D, (a + 1) * D)
            ys.append(mm(mix[:, cols], xb[:, cols]))
            gs.append(mm(mixt[:, cols], dm[:, cols]))
            term = mm_nt(dm[:, cols], xb[:, cols]) * fade[:, cols]
            total = term if total is None else total + term
        dinner[...] += total
        y_ref[:, lanes] = jnp.concatenate(ys, axis=1) + skip * xb.astype(F32)
        gx_ref[:, lanes] = jnp.concatenate(gs, axis=1) + skip * dm.astype(F32)

    def copy(stage, landing, send, recv, i, to):
        return pltpu.make_async_remote_copy(
            src_ref=stage.at[i], dst_ref=landing.at[i], send_sem=send.at[i], recv_sem=recv.at[i],
            **peer(seq=to, head=my))

    def climb(i):
        return copy(sf, af, cfs, cfr, i, up)

    def descend(i):
        return copy(sb, ab, cbs, cbr, i, down)

    def give(i, which):
        src, dst, send, recv = ((mf, xf_ref, mfs, mfr), (mb, xg_ref, mbs, mbr))[which]
        return copy(src, dst, send, recv, i, mate)

    def decays(i):
        mine, other = dec[i], rdec[i]
        return jnp.where(is_odd, other, mine), jnp.where(is_odd, mine, other)

    def hop_f(i):
        @pl.when(bottom)
        def _():
            af[i] = jnp.zeros(af.shape[1:], BF16)

        @pl.when(jnp.logical_not(bottom))
        def _():
            climb(i).wait_recv()

        even_d, odd_d = decays(i)
        x = af[i].astype(F32)
        mine = of[i]
        near = even_d * x
        mf[i] = jnp.where(is_odd, x, near + mine).astype(BF16)
        sm[i] = jnp.where(is_odd, near, x)

        @pl.when(not_top)
        def _():
            sf[i] = (odd_d * near + jnp.where(is_odd, 1.0, odd_d) * mine).astype(BF16)
            climb(i).start()

        @pl.when(give_f)
        def _():
            give(i, 0).start()

    def hop_b(i):
        @pl.when(top_level)
        def _():
            ab[i] = jnp.zeros(ab.shape[1:], BF16)

        @pl.when(not_top)
        def _():
            descend(i).wait_recv()

        even_d, odd_d = decays(i)
        x = ab[i].astype(F32)
        mine = ob[i]
        near = odd_d * x
        mb[i] = jnp.where(is_odd, near + mine, x).astype(BF16)
        gm[i] = jnp.where(is_odd, x, near)

        @pl.when(jnp.logical_not(bottom))
        def _():
            sb[i] = (even_d * near + jnp.where(is_odd, even_d, 1.0) * mine).astype(BF16)
            descend(i).start()

        @pl.when(give_b)
        def _():
            give(i, 1).start()

    def hops(t):
        f = t - 2 * (level - 1) - jnp.where(top_level, SLACK, 0)
        g = t - 2 * (levels - 2 - level) - jnp.where(bottom, SLACK, 0)

        @pl.when(jnp.logical_and(jnp.logical_not(bottom), jnp.logical_and(f >= 0, f < pairs)))
        def _():
            hop_f(f)

        @pl.when(jnp.logical_and(not_top, jnp.logical_and(g >= 0, g < pairs)))
        def _():
            hop_b(g)

    swap.wait()
    slow = 2 * (levels - 2)
    early_events = max(len(events) - slow, 1)

    def first_phase(t, carry):
        for i in range(early_events):
            @pl.when(t == pairs * i // early_events)
            def _():
                events[i]()

        own(t)
        return carry

    lax.fori_loop(0, pairs, first_phase, 0)
    middle = events[early_events:len(events) - (kv_heads - 1)]

    def second_phase(t, carry):
        def inner(i, carry):
            within(i)
            return carry

        hops(t)
        lax.fori_loop(pairs * t // slow, pairs * (t + 1) // slow, inner, 0)
        for i in range(min(slow - 1, len(middle))):
            @pl.when(t == i)
            def _():
                middle[i]()

        return carry

    lax.fori_loop(0, slow, second_phase, 0)
    for late in middle[slow - 1:]:
        late()
    events = events[len(events) - (kv_heads - 1):]
    relayed(0)
    rest = range(1, kv_heads)

    def plain(kv):
        return kv < kv_heads - 1

    def swap_over(kv):
        return pltpu.make_async_remote_copy(
            src_ref=part.at[kv, mate], dst_ref=landy.at[kv, 0], send_sem=pys.at[kv, 0],
            recv_sem=pyr.at[kv, 0], **peer(seq=mate, head=my))

    def pass_both(kv, j):
        return pltpu.make_async_remote_copy(
            src_ref=part.at[kv, pl.ds(2 * j, 2)], dst_ref=landz.at[kv, j], send_sem=pzs.at[kv, j],
            recv_sem=pzr.at[kv, j], **peer(seq=down, head=my))

    def pass_over(kv, j):
        return pltpu.make_async_remote_copy(
            src_ref=part.at[kv, 2 * j + 1 - par], dst_ref=landy.at[kv, j], send_sem=pys.at[kv, j],
            recv_sem=pyr.at[kv, j], **peer(seq=mate, head=my))

    def pass_down(kv, j):
        return pltpu.make_async_remote_copy(
            src_ref=part.at[kv, 2 * j + par], dst_ref=landz.at[kv, j, 0], send_sem=pzs.at[kv, j],
            recv_sem=pzr.at[kv, j], **peer(seq=down, head=my))

    def sends_over(j):
        return jnp.logical_or(j < level, jnp.logical_and(j == level, is_odd))

    def takes_over(j):
        return jnp.logical_or(j < level, jnp.logical_and(j == level, odd == 0))

    def result(kv, total):
        cols = slice(kv * D, kv * D + D)
        dk_out[:, cols] = total[:, :D]
        dv_out[:, cols] = total[:, D:]

    def gather_down(kv, j):
        if plain(kv):
            pass_both(kv, j).wait_recv()
            both = pl.ds(2 * j, 2)
            part[kv, both] = (part[kv, both].astype(F32) + landz[kv, j].astype(F32)).astype(BF16)

            @pl.when(j < level)
            def _():
                pass_both(kv, j).start()

            @pl.when(j == level)
            def _():
                swap_over(kv).start()

            return

        acc[...] = part[kv, 2 * j + par].astype(F32)

        @pl.when(takes_over(j))
        def _():
            pass_over(kv, j).wait_recv()
            acc[...] += landy[kv, j].astype(F32)

        @pl.when(not_top)
        def _():
            pass_down(kv, j).wait_recv()
            acc[...] += landz[kv, j, 0].astype(F32)

        @pl.when(j < level)
        def _():
            part[kv, 2 * j + par] = acc[...].astype(BF16)
            pass_down(kv, j).start()

        @pl.when(j == level)
        def _():
            result(kv, acc[...])

    def gathered(kv):
        if plain(kv):
            swap_over(kv).wait_recv()
            result(kv, part[kv, me].astype(F32) + landy[kv, 0].astype(F32))

    def gather_sent(kv):
        if plain(kv):
            swap_over(kv).wait_send()
        for j in range(levels):
            if not plain(kv):
                @pl.when(sends_over(j))
                def _():
                    pass_over(kv, j).wait_send()

            @pl.when(j < level)
            def _():
                (pass_both if plain(kv) else pass_down)(kv, j).wait_send()

    lag = min(8, pairs)
    slots = pairs + lag

    def slot_of(kv):
        ready = (kv + 1) * (ratio // 2) - 1
        behind = levels - 1 - level
        if plain(kv):
            return ready + 3 * behind, 2
        return ready + 4 + 4 * behind, 1

    def gathers(t):
        for kv in range(kv_heads):
            first, pace = slot_of(kv)
            if plain(kv):
                @pl.when(jnp.logical_and(top_level, t == first))
                def _():
                    def launch(j, carry):
                        @pl.when(j < level)
                        def _():
                            pass_both(kv, j).start()

                        return carry

                    lax.fori_loop(0, levels, launch, 0)
                    swap_over(kv).start()

            since = t - first
            j = since // pace
            fits = jnp.logical_and(since >= 0, jnp.logical_and(j <= level, since == j * pace))
            if plain(kv):
                fits = jnp.logical_and(fits, not_top)

            @pl.when(fits)
            def _():
                gather_down(kv, j)

    def lanes_of(h):
        return pl.ds(pl.multiple_of(h * D, D), D)

    tile = W if length % W == 0 else D
    many = tile // rows

    def attend(p):
        h = 2 * p
        kv = h // ratio
        first, second = lanes_of(h), lanes_of(h + 1)

        @pl.when(lax.rem(h, ratio) == 0)
        def _():
            kt[...] = jnp.transpose(kva[kv, :, :, :D].reshape(length, D).astype(F32)).astype(BF16)
            vt[:D] = jnp.transpose(kva[kv, :, :, D:].reshape(length, D).astype(F32)).astype(BF16)
            dka[...] = jnp.zeros_like(dka)
            dva[...] = jnp.zeros_like(dva)

        q = jnp.concatenate([q_ref[:, first], q_ref[:, second]], axis=0)
        dm = jnp.concatenate([dm_ref[:, first], dm_ref[:, second]], axis=0)
        qe = jnp.concatenate([q, eq[...]], axis=1)
        top = None
        for j in range(length // tile):
            at = slice(j * tile, (j + 1) * tile)
            k = kva[kv, j * many:(j + 1) * many, :, :D].reshape(tile, D)
            s = mm_nt(jnp.concatenate([k, ek[at]], axis=1), qe)
            s_ref[at] = s
            high = jnp.max(s.reshape(tile // 8, 8, 2 * rows), axis=0)
            top = high if top is None else jnp.maximum(top, high)
        top = jnp.max(top, axis=0, keepdims=True) * LOG2
        for j in range(length // tile):
            at = slice(j * tile, (j + 1) * tile)
            e = jnp.exp2(s_ref[at] * LOG2 - top)
            s_ref[at] = e
            eb_ref[at] = e.astype(BF16)
        out_t = mm(vt[...], eb_ref[...])
        inv = 1.0 / out_t[D:D + 1]
        out_t = out_t[:D] * inv
        out = jnp.transpose(out_t)
        att_ref[:, first] = out[:rows]
        att_ref[:, second] = out[rows:]
        delta = jnp.sum(jnp.transpose(dm.astype(F32)) * out_t, axis=0, keepdims=True)
        for j in range(length // tile):
            at = slice(j * tile, (j + 1) * tile)
            v = kva[kv, j * many:(j + 1) * many, :, D:].reshape(tile, D)
            ds_ref[at] = (s_ref[at] * (mm_nt(v, dm) - delta)).astype(BF16)
        dq = jnp.transpose(mm(kt[...], ds_ref[...]) * (inv * SCALE))
        dq_ref[:, first] = dq[:rows]
        dq_ref[:, second] = dq[rows:]
        inv_col = jnp.transpose(jnp.broadcast_to(inv, (D, 2 * rows)))
        dka[...] += mm(ds_ref[...], (q.astype(F32) * inv_col).astype(BF16))
        dva[...] += mm(eb_ref[...], (dm.astype(F32) * inv_col).astype(BF16))

        @pl.when(lax.rem(h, ratio) == ratio - 2)
        def _():
            part[kv, :, :, :D] = (dka[...] * SCALE).astype(BF16).reshape(n, rows, D)
            part[kv, :, :, D:] = dva[...].astype(BF16).reshape(n, rows, D)

        @pl.when(p == (kv_heads * ratio) // 2 - 1)
        def _():
            for j in range(levels):
                @pl.when(sends_over(j))
                def _():
                    pass_over(kv_heads - 1, j).start()

    ones = jnp.ones((EDGE, D), BF16)

    def edge(i):
        return copy(gh, gn, xs, xr, i, prv)

    def through(p):
        lanes = wide_of(p)

        @pl.when(take_f)
        def _():
            give(p, 0).wait_recv()

        @pl.when(take_b)
        def _():
            give(p, 1).wait_recv()

        state = (sm[p] + xf_ref[p].astype(F32)).astype(BF16)
        grad = (gm[p] + xg_ref[p].astype(F32)).astype(BF16)
        xf = xb_ref[:, lanes].astype(F32)
        dmf = dm_ref[:, lanes].astype(F32)
        col = col_ref[:, lanes]
        final = col[rows - 1:]
        back = jnp.exp(final - col) * mm(b, grad)
        y = y_ref[:, lanes] + jnp.exp(col) * mm(c, state)
        mixed_ref[:, lanes] = (y + att_ref[:, lanes]).astype(BF16)
        gx = gx_ref[:, lanes] + back
        net = dmf * y - xf * gx
        hi = net.astype(BF16)
        lo = (net - hi.astype(F32)).astype(BF16)
        inside = jnp.sum(xf * back, axis=0, keepdims=True) + jnp.exp(final) * jnp.sum(
            state.astype(F32) * grad.astype(F32), axis=0, keepdims=True)
        for a in range(2):
            cols = slice(a * D, (a + 1) * D)
            sums = mm_nt(ones, hi[:, cols]) + mm_nt(ones, lo[:, cols])
            net_ref[pl.ds(2 * p + a, 1)] = sums[:1]
            fin_ref[pl.ds(2 * p + a, 1)] = inside[:, cols]
        dbc[:, D:] += mm_nt(dme_ref[:, lanes], state)
        dbc[:, :D] += mm_nt(xt_ref[:, lanes], grad)
        g = gx * sl_ref[:, lanes]
        gh[p] = g[:EDGE].astype(BF16)

        @pl.when(me > 0)
        def _():
            edge(p).start()

        dx_ref[:, lanes] = conv_back(g, jnp.zeros((8, W), F32), w_ref[:, lanes].astype(F32))

    def step(t, carry):
        for kv in rest:
            @pl.when(t == kv * (ratio // 2))
            def _():
                events[kv - 1]()
                relayed(kv)

        hops(slow + t)
        attend(t)
        gathers(t)
        return carry

    lax.fori_loop(0, pairs, step, 0)

    def last_hops(t, carry):
        hops(t)
        return carry

    lax.fori_loop(slow + pairs, slow + pairs + SLACK, last_hops, 0)

    def finish_through(i, carry):
        through(pairs - lag + i)
        gathers(pairs + i)
        return carry

    lax.fori_loop(0, lag, finish_through, 0)
    di = dinner[...]
    dbcb[:, D:] = (dbc[:, D:] + mm(di.astype(BF16), b)).astype(BF16)
    dbcb[:, :D] = (dbc[:, :D] + mm(jnp.transpose(di).astype(BF16), c)).astype(BF16)

    def remote(src, dst, send, recv, seq, head):
        return pltpu.make_async_remote_copy(
            src_ref=src, dst_ref=dst, send_sem=send, recv_sem=recv, **peer(seq=seq, head=head))

    def across(off):
        return remote(dbcb, bb.at[off], bs.at[off], br.at[off], me, lax.rem(my + off, m))

    def before(off):
        return remote(dbcb.at[pl.ds(0, EDGE)], nb.at[off], ns.at[off], nr.at[off], prv,
                      lax.rem(my + off, m))

    for off in range(1, m):
        across(off).start()

    @pl.when(me > 0)
    def _():
        for off in range(m):
            before(off).start()

    dla_ref[...] = exact(mm, net_ref[...], lower) + exact(mm, fin_ref[...], jnp.ones((D, rows), BF16))

    for kv in range(kv_heads):
        first, pace = slot_of(kv)

        def leftover(j, carry):
            later = jnp.logical_and(j <= level, first + pace * j >= slots)
            if plain(kv):
                later = jnp.logical_and(later, not_top)

            @pl.when(later)
            def _():
                gather_down(kv, j)

            return carry

        lax.fori_loop(0, levels, leftover, 0)

    @pl.when(me < n - 1)
    def _():
        def finish(i, carry):
            lanes = wide_of(i)
            edge(i).wait_recv()
            after = jnp.concatenate([jnp.zeros((8, W), F32), gn[i].astype(F32)[:8]], axis=0)
            taps = w_ref[:, lanes].astype(F32)
            fix = None
            for tap in range(taps.shape[0]):
                offset = taps.shape[0] - 1 - tap
                term = taps[tap:tap + 1] * after[offset:offset + 8]
                fix = term if fix is None else fix + term
            dx_ref[rows - 8:, lanes] += fix
            return carry

        lax.fori_loop(0, pairs, finish, 0)
        for off in range(m):
            before(off).wait_recv()

    @pl.when(me == n - 1)
    def _():
        nb[...] = jnp.zeros(nb.shape, nb.dtype)

    total = dbcb[...].astype(F32)
    for off in range(1, m):
        across(off).wait_recv()
        total += bb[off].astype(F32)
    follow = nb[0].astype(F32)
    for off in range(1, m):
        follow += nb[off].astype(F32)
    dbc_out[...] = conv_back(total * bcsl[...], (follow * bcsn[...])[:8], wbc)

    for kv in range(kv_heads):
        gathered(kv)

    for off in range(1, m):
        across(off).wait_send()

    @pl.when(me > 0)
    def _():
        def edge_sent(i, carry):
            edge(i).wait_send()
            return carry

        lax.fori_loop(0, pairs, edge_sent, 0)
        for off in range(m):
            before(off).wait_send()

    for kv in range(kv_heads):
        gather_sent(kv)

    def drain(i, carry):
        @pl.when(not_top)
        def _():
            climb(i).wait_send()

        @pl.when(level > 0)
        def _():
            descend(i).wait_send()

        @pl.when(give_f)
        def _():
            give(i, 0).wait_send()

        @pl.when(give_b)
        def _():
            give(i, 1).wait_send()

        return carry

    lax.fori_loop(0, pairs, drain, 0)
    for kv in range(kv_heads):
        relay_sent(kv)

    @pl.when(me < n - 1)
    def _():
        cb.wait_send()
        cx.wait_send()

    @pl.when(me > 0)
    def _():
        cn.wait_send()


def block_part(n, m, x_in, bc_in, conv_x, conv_bc, log_decay, skip, queries, keys, values, d_mixed):
    rows, wide = x_in.shape
    width = keys.shape[1]
    heads = wide // D
    pairs = heads // 2
    kv_heads = width // D
    length = n * rows
    taps = conv_x.shape[0]
    dma = pltpu.SemaphoreType.DMA
    shape = jax.ShapeDtypeStruct

    def v(dims, dtype=F32):
        return pltpu.VMEM(dims, dtype)

    def stay(a):
        return pltpu.with_memory_space_constraint(a, pltpu.HBM)

    state = (pairs, D, W)
    return pl.pallas_call(
        functools.partial(block_kernel, n, m),
        out_shape=(
            shape((rows, wide), BF16), shape((rows, wide), F32), shape((rows, width), F32),
            shape((rows, width), F32), shape((rows, wide), F32), shape((rows, W), F32),
            shape((heads, rows), F32)),
        in_specs=[HBM] * 5 + [SMEM] + [HBM] * 4,
        out_specs=(VMEM,) * 7,
        scratch_shapes=[
            v((rows, wide), BF16), v((rows, wide), BF16), v((rows, wide), BF16), v((taps, wide), BF16),
            v(bc_in.shape, BF16), v(conv_bc.shape, BF16), v((heads, rows)), v((rows, W), BF16),
            v((kv_heads, n, rows, W), BF16), v((EDGE, wide), BF16), v((EDGE, W), BF16), v((EDGE, W), BF16),
            v((rows, wide), BF16), v((rows, wide)), v((rows, wide)), v((rows, wide), BF16),
            v((rows, wide), BF16), v((rows, wide)), v((rows, wide)), v((rows, wide)),
            v((rows, W), BF16), v((rows, W)), v((EDGE, W)), v((D, rows), BF16), v((D, rows), BF16),
            v((pairs, 1, W)), v((pairs, 1, W)), v((pairs, 1, W)), v((rows, W)), v((rows, W)),
            v((rows, rows)), v((rows, W)), v((rows, W), BF16), v((heads, rows)), v((heads, rows)),
            *[v(state) for _ in range(4)], *[v(state, BF16) for _ in range(8)],
            v((length, W)), v((length, W), BF16), v((length, W), BF16), v((D, length), BF16),
            v((D + EDGE, length), BF16), v((length, D), BF16), v((2 * rows, D), BF16), v((length, D)),
            v((length, D)), v((kv_heads, n, rows, W), BF16), v((kv_heads, n // 2, rows, W), BF16),
            v((kv_heads, n // 2, 2, rows, W), BF16), v((rows, W)),
            v((pairs, EDGE, W), BF16), v((pairs, EDGE, W), BF16), v((m, rows, W), BF16), v((m, EDGE, W), BF16),
            dma((2 * kv_heads + 7,)), *[dma((kv_heads, n)) for _ in range(4)], dma((3,)), dma((3,)),
            dma, dma, *[dma((pairs,)) for _ in range(8)],
            *[dma((kv_heads, n // 2)) for _ in range(4)], dma((pairs,)), dma((pairs,)), dma((m,)), dma((m,)), dma((m,)), dma((m,))],
        compiler_params=pltpu.CompilerParams(
            collective_id=0, has_side_effects=True, vmem_limit_bytes=40 * 2**20),
        name="block",
    )(*map(stay, (x_in, bc_in, conv_x, conv_bc, log_decay.T, skip, queries, keys, values, d_mixed)))


def write_kernel(mixed, dq, dk, dv, dx, dbc, dla, mixed_o, dq_o, dk_o, dv_o, dx_o, dbc_o, dla_o, dbc3, sem):
    quarter = dq.shape[0] // 4
    copies = [(a.at[pl.ds(i * quarter, quarter)], b.at[pl.ds(i * quarter, quarter)])
              for a, b in ((dq, dq_o), (dx, dx_o), (mixed, mixed_o)) for i in range(4)]
    copies += [(dk, dk_o), (dv, dv_o), (dla, dla_o), (dbc3, dbc_o)]
    copies = [pltpu.make_async_copy(src, dst, sem.at[i]) for i, (src, dst) in enumerate(copies)]
    for cp in copies[:-1]:
        cp.start()
    dbc3[:, 0, :] = dbc[:, :D]
    dbc3[:, 1, :] = dbc[:, D:]
    copies[-1].start()
    for cp in copies:
        cp.wait()


def write_part(mixed, dq, dk, dv, dx, dbc, dla):
    rows = dbc.shape[0]
    outs = tuple(jax.ShapeDtypeStruct(a.shape, a.dtype) for a in (mixed, dq, dk, dv, dx))
    outs += (jax.ShapeDtypeStruct((rows, 2, D), F32), jax.ShapeDtypeStruct(dla.shape, F32))
    return pl.pallas_call(
        write_kernel,
        out_shape=outs,
        in_specs=[VMEM] * 7,
        out_specs=(HBM,) * 7,
        scratch_shapes=[pltpu.VMEM((rows, 2, D), F32), pltpu.SemaphoreType.DMA((16,))],
        compiler_params=pltpu.CompilerParams(vmem_limit_bytes=2 * 2**20),
        name="write",
    )(mixed, dq, dk, dv, dx, dbc, dla)


def shards(n, m, *args):
    *outs, dla = write_part(*block_part(n, m, *args))
    return (*outs, dla.T)


def solution(mesh):
    n, m = mesh.shape["seq"], mesh.shape["head"]
    grid = P("seq", "head")
    part = P("seq", None, None)
    in_specs = (grid, part, P(None, "head"), P(), grid, P("head"), grid, grid, grid, grid)
    out_specs = (grid, grid, grid, grid, grid, part, grid)
    return jax.shard_map(functools.partial(shards, n, m), mesh=mesh, in_specs=in_specs,
                         out_specs=out_specs, check_vma=False)
```

```python
import functools
import math

import jax
import jax.numpy as jnp
from jax import lax
from jax.experimental import pallas as pl
from jax.experimental.pallas import tpu as pltpu
from jax.sharding import PartitionSpec as P

D = 128
W = 2 * D
EDGE = 16
SLACK = 2
HEAD = 0
F32 = jnp.float32
BF16 = jnp.bfloat16
MESH = pl.DeviceIdType.MESH
VMEM = pl.BlockSpec(memory_space=pltpu.VMEM)
HBM = pl.BlockSpec(memory_space=pltpu.HBM)
SMEM = pl.BlockSpec(memory_space=pltpu.SMEM)
SCALE = D ** (-0.5)
LOG2 = SCALE * math.log2(math.e)


def mm(a, b):
    return jnp.dot(a, b, preferred_element_type=F32)


def mm_nt(a, b):
    return lax.dot_general(a, b, (((1,), (1,)), ((), ())), preferred_element_type=F32)


def sigmoid(v):
    return 1.0 / (1.0 + jnp.exp(-v))


def peer(**coords):
    return dict(device_id=coords, device_id_type=MESH)


def split3(v):
    hi = v.astype(BF16)
    rest = v - hi.astype(F32)
    mid = rest.astype(BF16)
    return hi, mid, (rest - mid.astype(F32)).astype(BF16)


def exact(dot, a, b):
    if a.dtype == BF16:
        hi, mid, lo = split3(b)
        return (dot(a, hi) + dot(a, mid)) + dot(a, lo)
    hi, mid, lo = split3(a)
    return (dot(hi, b) + dot(mid, b)) + dot(lo, b)


def conv(x, halo, taps):
    width = taps.shape[0]
    rows = x.shape[0]
    full = jnp.concatenate([halo[EDGE - 8:], x], axis=0)
    total = None
    for tap in range(width):
        start = 8 - (width - 1) + tap
        term = taps[tap:tap + 1] * full[start:start + rows]
        total = term if total is None else total + term
    return total


def conv_back(grads, after, taps):
    width = taps.shape[0]
    rows = grads.shape[0]
    padded = jnp.concatenate([grads, after], axis=0)
    total = None
    for tap in range(width):
        offset = width - 1 - tap
        term = taps[tap:tap + 1] * padded[offset:offset + rows]
        total = term if total is None else total + term
    return total


def iota(shape, axis):
    return lax.broadcasted_iota(jnp.int32, shape, axis)


def block_kernel(n, m, x_hbm, bc_hbm, w_hbm, wbc_hbm, ld_hbm, skip_ref, q_hbm, k_hbm, v_hbm, dm_hbm,
                 mixed_ref, dq_ref, dk_out, dv_out, dx_ref, dbc_out, dla_ref,
                 x_ref, dm_ref, q_ref, w_ref, bc3, wbc3, ld_ref, bcs, kva, xh, bch, bcn,
                 xb_ref, sl_ref, col_ref, xt_ref, dme_ref, y_ref, gx_ref, att_ref,
                 bcv, bcsl, bcsn, bt, ct, rowp, dec, rdec, inner, innert, dinner, dbc, dbcb, net_ref, fin_ref,
                 of, ob, sm, gm, af, ab, sf, sb, mf, mb, xf_ref, xg_ref,
                 s_ref, eb_ref, ds_ref, kt, vt, ek, eq, dka, dva, part, landy, landz, acc,
                 gh, gn, bb, nb,
                 ls, zs, zr, fs, fr, hs, hr, es, er,
                 cfs, cfr, cbs, cbr, mfs, mfr, mbs, mbr, pys, pyr, pzs, pzr, xs, xr, bs, br, ns, nr):
    me = lax.axis_index("seq")
    my = lax.axis_index("head")
    odd = lax.rem(me, 2)
    is_odd = odd == 1
    mate = me + 1 - 2 * odd
    level = me // 2
    levels = n // 2
    rows, wide = x_ref.shape
    width = k_hbm.shape[1]
    heads = wide // D
    pairs = heads // 2
    kv_heads = width // D
    ratio = heads // kv_heads
    length = n * rows
    nxt = lax.rem(me + 1, n)
    prv = lax.rem(me + n - 1, n)
    up = lax.rem(me + 2, n)
    down = lax.rem(me + n - 2, n)

    barrier = pltpu.get_barrier_semaphore()
    count = 0
    for off in range(1, n):
        pl.semaphore_signal(barrier, inc=1, **peer(seq=lax.rem(me + off, n), head=my))
        count += 1
    for off in range(1, m):
        for to in (me, nxt, prv):
            pl.semaphore_signal(barrier, inc=1, **peer(seq=to, head=lax.rem(my + off, m)))
            count += 1

    loads = [(ld_hbm, ld_ref)]
    for kv in range(kv_heads):
        lanes = pl.ds(kv * D, D)
        loads.append((k_hbm.at[:, lanes], kva.at[kv, me, :, pl.ds(0, D)]))
        loads.append((v_hbm.at[:, lanes], kva.at[kv, me, :, pl.ds(D, D)]))
    loads += [
        (bc_hbm, bc3), (wbc_hbm, wbc3), (w_hbm, w_ref), (x_hbm, x_ref), (dm_hbm, dm_ref), (q_hbm, q_ref)]
    loads = [pltpu.make_async_copy(src, dst, ls.at[i]) for i, (src, dst) in enumerate(loads)]
    for cp in loads:
        cp.start()

    t_i = iota((rows, rows), 0)
    s_i = iota((rows, rows), 1)
    lower = jnp.where(t_i >= s_i, 1.0, 0.0).astype(BF16)
    loads[0].wait()
    cum = exact(mm_nt, lower, ld_ref[...])
    parts = split3(cum)
    ident = jnp.where(iota((heads, heads), 0) == iota((heads, heads), 1), 1.0, 0.0).astype(BF16)
    cum_rows = (mm_nt(ident, parts[0]) + mm_nt(ident, parts[1])) + mm_nt(ident, parts[2])
    for h in range(heads):
        rowp[h // 2, :, (h % 2) * D:(h % 2) * D + D] = cum_rows[h:h + 1]

    def column(p, first):
        pick = jnp.where(iota((heads, W), 0) == 2 * p + iota((heads, W), 1) // D, 1.0, 0.0).astype(BF16)
        return (mm(parts[0][first:], pick) + mm(parts[1][first:], pick)) + mm(parts[2][first:], pick)

    def decay(p, carry):
        dec[p] = jnp.exp(column(p, rows - EDGE)[EDGE - 1:])
        return carry

    lax.fori_loop(0, pairs, decay, 0)

    cross = max(levels // 2, 1)
    early = level < cross
    for off in range(1, n):
        fill = me + off < n
        if off == 1:
            fill = jnp.logical_and(fill, jnp.logical_or(is_odd, jnp.logical_not(early)))

        @pl.when(fill)
        def _():
            for kv in range(kv_heads):
                kva[kv, lax.rem(me + off, n)] = jnp.zeros(kva.shape[2:], kva.dtype)

    big = -(2.0 ** 100)
    e_i = iota((rows, D), 1)
    r_i = iota((rows, D), 0)
    inside = jnp.where((r_i == e_i) & (e_i > 0), big, 0.0).astype(BF16)
    outside = jnp.where(e_i == 0, big, 0.0).astype(BF16)
    for j in range(n):
        later = jnp.where(me < j, outside, jnp.zeros_like(outside))
        ek[j * rows:(j + 1) * rows] = jnp.where(me == j, inside, later)
    reach = jnp.where((e_i > r_i) | (e_i == 0), 1.0, 0.0).astype(BF16)
    eq[:rows] = reach
    eq[rows:] = reach
    vt[D:] = jnp.ones((vt.shape[0] - D, length), BF16)

    for cp in loads[1:-2]:
        cp.wait()
    bcs[:, :D] = bc3[...].astype(F32)[:, 0, :].astype(BF16)
    bcs[:, D:] = bc3[...].astype(F32)[:, 1, :].astype(BF16)
    wbc = jnp.concatenate([wbc3[...].astype(F32)[:, 0, :], wbc3[...].astype(F32)[:, 1, :]], axis=1)
    pl.semaphore_wait(barrier, count)

    def halo(slot, src, dst, to):
        return pltpu.make_async_remote_copy(
            src_ref=src, dst_ref=dst, send_sem=hs.at[slot], recv_sem=hr.at[slot],
            **peer(seq=to, head=my))

    last = pl.ds(rows - EDGE, EDGE)
    cx = halo(0, x_ref.at[last], xh, nxt)
    cb = halo(1, bcs.at[last], bch, nxt)
    cn = halo(2, bcs.at[pl.ds(0, EDGE)], bcn, prv)

    swap = pltpu.make_async_remote_copy(
        src_ref=dec, dst_ref=rdec, send_sem=es, recv_sem=er, **peer(seq=mate, head=my))
    swap.start()

    @pl.when(me < n - 1)
    def _():
        cb.start()
        cx.start()

    @pl.when(me > 0)
    def _():
        cn.start()

    par = odd

    def rise(kv, blk):
        return pltpu.make_async_remote_copy(
            src_ref=kva.at[kv, blk], dst_ref=kva.at[kv, blk], send_sem=zs.at[kv, blk],
            recv_sem=zr.at[kv, blk], **peer(seq=up, head=my))

    def over(kv, blk):
        return pltpu.make_async_remote_copy(
            src_ref=kva.at[kv, blk], dst_ref=kva.at[kv, blk], send_sem=fs.at[kv, blk],
            recv_sem=fr.at[kv, blk], **peer(seq=mate, head=my))

    not_top = level < levels - 1
    crosses = jnp.logical_or(odd == 0, early)
    for kv in range(kv_heads):
        @pl.when(not_top)
        def _():
            rise(kv, me).start()

        @pl.when(crosses)
        def _():
            over(kv, me).start()

    def relay_first(kv):
        @pl.when(early)
        def _():
            over(kv, mate).wait_recv()
            rise(kv, mate).start()

    def relay_mine(kv, k):
        @pl.when(level >= k)
        def _():
            blk = 2 * (level - k) + par
            rise(kv, blk).wait_recv()

            @pl.when(not_top)
            def _():
                rise(kv, blk).start()

            @pl.when(level - k >= cross)
            def _():
                over(kv, blk).start()

    def relay_other(kv, k):
        @pl.when(jnp.logical_and(level >= k, level - k < cross))
        def _():
            blk = 2 * (level - k) + 1 - par
            rise(kv, blk).wait_recv()

            @pl.when(not_top)
            def _():
                rise(kv, blk).start()

    def relayed(kv):
        @pl.when(jnp.logical_and(odd == 1, jnp.logical_not(early)))
        def _():
            over(kv, mate).wait_recv()

        for k in range(1, levels):
            @pl.when(jnp.logical_and(level >= k, level - k >= cross))
            def _():
                over(kv, 2 * (level - k) + 1 - par).wait_recv()

    def relay_sent(kv):
        @pl.when(not_top)
        def _():
            rise(kv, me).wait_send()

        @pl.when(crosses)
        def _():
            over(kv, me).wait_send()

        @pl.when(early)
        def _():
            rise(kv, mate).wait_send()

        for k in range(1, levels):
            far = level - k

            @pl.when(jnp.logical_and(level >= k, not_top))
            def _():
                rise(kv, 2 * far + par).wait_send()

            @pl.when(jnp.logical_and(level >= k, far >= cross))
            def _():
                over(kv, 2 * far + par).wait_send()

            @pl.when(jnp.logical_and(jnp.logical_and(level >= k, far < cross), not_top))
            def _():
                rise(kv, 2 * far + 1 - par).wait_send()

    def event(kv, k):
        if k == 0:
            relay_first(kv)
        else:
            relay_other(kv, k)
        if k < levels - 1:
            relay_mine(kv, k + 1)

    events = [functools.partial(event, kv, k) for k in range(levels) for kv in range(kv_heads)]

    @pl.when(me == 0)
    def _():
        xh[...] = jnp.zeros(xh.shape, xh.dtype)
        bch[...] = jnp.zeros(bch.shape, bch.dtype)

    @pl.when(me == n - 1)
    def _():
        bcn[...] = jnp.zeros(bcn.shape, bcn.dtype)

    loads[-2].wait()
    loads[-1].wait()

    def wide_of(p):
        return pl.ds(pl.multiple_of(p * W, W), W)

    def prepare(p, carry):
        lanes = wide_of(p)
        sl_ref[:, lanes] = conv(
            x_ref[:, lanes].astype(F32), jnp.zeros((EDGE, W), F32), w_ref[:, lanes].astype(F32))
        col = column(p, 0)
        col_ref[:, lanes] = col
        dme_ref[:, lanes] = (dm_ref[:, lanes].astype(F32) * jnp.exp(col)).astype(BF16)
        return carry

    lax.fori_loop(0, pairs, prepare, 0)
    events.pop(0)()

    @pl.when(me > 0)
    def _():
        cb.wait_recv()
        cx.wait_recv()

    @pl.when(me < n - 1)
    def _():
        cn.wait_recv()

    def slope(pre, sig):
        return sig * (1.0 + pre * (1.0 - sig))

    pre = conv(bcs[...].astype(F32), bch[...].astype(F32), wbc)
    sig = sigmoid(pre)
    act = (pre * sig).astype(BF16)
    bcv[...] = act
    bcsl[...] = slope(pre, sig)
    pre = conv(bcn[...].astype(F32), bcs[rows - EDGE:].astype(F32), wbc)
    bcsn[...] = slope(pre, sigmoid(pre))
    act = act.astype(F32)
    bt[...] = jnp.transpose(act[:, :D]).astype(BF16)
    ct[...] = jnp.transpose(act[:, D:]).astype(BF16)
    b = bcv[:, :D]
    c = bcv[:, D:]
    own_inner = mm_nt(c, b)
    own_innert = mm_nt(b, c)
    for a in range(2):
        inner[:, a * D:(a + 1) * D] = own_inner
        innert[:, a * D:(a + 1) * D] = own_innert
    dinner[...] = jnp.zeros_like(dinner)
    dbc[...] = jnp.zeros_like(dbc)

    bottom = level == 0
    top_level = level == levels - 1
    give_f = jnp.logical_or(odd == 0, jnp.logical_not(bottom))
    take_f = jnp.logical_or(is_odd, jnp.logical_not(bottom))
    give_b = jnp.logical_or(is_odd, jnp.logical_not(top_level))
    take_b = jnp.logical_or(odd == 0, jnp.logical_not(top_level))

    @pl.when(jnp.logical_not(take_f))
    def _():
        xf_ref[...] = jnp.zeros(xf_ref.shape, BF16)

    @pl.when(jnp.logical_not(take_b))
    def _():
        xg_ref[...] = jnp.zeros(xg_ref.shape, BF16)

    def own(p):
        lanes = wide_of(p)
        pre = sl_ref[:, lanes]
        fix = conv(jnp.zeros((8, W), F32), xh[:, lanes].astype(F32), w_ref[:, lanes].astype(F32))
        pre = jnp.concatenate([pre[:8] + fix, pre[8:]], axis=0)
        sig = sigmoid(pre)
        xb = (pre * sig).astype(BF16)
        xb_ref[:, lanes] = xb
        sl_ref[:, lanes] = slope(pre, sig)
        col = col_ref[:, lanes]
        dme = dme_ref[:, lanes]
        final = col[rows - 1:]
        xt = (xb.astype(F32) * jnp.exp(final - col)).astype(BF16)
        xt_ref[:, lanes] = xt
        of[p] = mm(bt[...], xt)
        ob[p] = mm(ct[...], dme)

        @pl.when(bottom)
        def _():
            hop_f(p)

        @pl.when(top_level)
        def _():
            hop_b(p)

    def skips(p):
        return jnp.where(iota((1, W), 1) < D, skip_ref[2 * p], skip_ref[2 * p + 1])

    t_w = iota((rows, W), 0)
    s_w = lax.rem(iota((rows, W), 1), D)

    def within(p):
        lanes = wide_of(p)
        xb = xb_ref[:, lanes]
        dm = dm_ref[:, lanes]
        gap = col_ref[:, lanes] - rowp[p]
        fade = jnp.exp(jnp.where(t_w >= s_w, gap, -1e30))
        fadet = jnp.exp(jnp.where(s_w >= t_w, -gap, -1e30))
        mix = (inner[...] * fade).astype(BF16)
        mixt = (innert[...] * fadet).astype(BF16)
        skip = skips(p)
        total = None
        ys, gs = [], []
        for a in range(2):
            cols = slice(a * D, (a + 1) * D)
            ys.append(mm(mix[:, cols], xb[:, cols]))
            gs.append(mm(mixt[:, cols], dm[:, cols]))
            term = mm_nt(dm[:, cols], xb[:, cols]) * fade[:, cols]
            total = term if total is None else total + term
        dinner[...] += total
        y_ref[:, lanes] = jnp.concatenate(ys, axis=1) + skip * xb.astype(F32)
        gx_ref[:, lanes] = jnp.concatenate(gs, axis=1) + skip * dm.astype(F32)

    def copy(stage, landing, send, recv, i, to):
        return pltpu.make_async_remote_copy(
            src_ref=stage.at[i], dst_ref=landing.at[i], send_sem=send.at[i], recv_sem=recv.at[i],
            **peer(seq=to, head=my))

    def climb(i):
        return copy(sf, af, cfs, cfr, i, up)

    def descend(i):
        return copy(sb, ab, cbs, cbr, i, down)

    def give(i, which):
        src, dst, send, recv = ((mf, xf_ref, mfs, mfr), (mb, xg_ref, mbs, mbr))[which]
        return copy(src, dst, send, recv, i, mate)

    def decays(i):
        mine, other = dec[i], rdec[i]
        return jnp.where(is_odd, other, mine), jnp.where(is_odd, mine, other)

    def hop_f(i):
        @pl.when(bottom)
        def _():
            af[i] = jnp.zeros(af.shape[1:], BF16)

        @pl.when(jnp.logical_not(bottom))
        def _():
            climb(i).wait_recv()

        even_d, odd_d = decays(i)
        x = af[i].astype(F32)
        mine = of[i]
        near = even_d * x
        mf[i] = jnp.where(is_odd, x, near + mine).astype(BF16)
        sm[i] = jnp.where(is_odd, near, x)

        @pl.when(not_top)
        def _():
            sf[i] = (odd_d * near + jnp.where(is_odd, 1.0, odd_d) * mine).astype(BF16)
            climb(i).start()

        @pl.when(give_f)
        def _():
            give(i, 0).start()

    def hop_b(i):
        @pl.when(top_level)
        def _():
            ab[i] = jnp.zeros(ab.shape[1:], BF16)

        @pl.when(not_top)
        def _():
            descend(i).wait_recv()

        even_d, odd_d = decays(i)
        x = ab[i].astype(F32)
        mine = ob[i]
        near = odd_d * x
        mb[i] = jnp.where(is_odd, near + mine, x).astype(BF16)
        gm[i] = jnp.where(is_odd, x, near)

        @pl.when(jnp.logical_not(bottom))
        def _():
            sb[i] = (even_d * near + jnp.where(is_odd, even_d, 1.0) * mine).astype(BF16)
            descend(i).start()

        @pl.when(give_b)
        def _():
            give(i, 1).start()

    def hops(t):
        f = t - 2 * (level - 1) - jnp.where(top_level, SLACK, 0)
        g = t - 2 * (levels - 2 - level) - jnp.where(bottom, SLACK, 0)

        @pl.when(jnp.logical_and(jnp.logical_not(bottom), jnp.logical_and(f >= 0, f < pairs)))
        def _():
            hop_f(f)

        @pl.when(jnp.logical_and(not_top, jnp.logical_and(g >= 0, g < pairs)))
        def _():
            hop_b(g)

    swap.wait()
    slow = 2 * (levels - 2)
    early_events = max(len(events) - slow, 1)

    def first_phase(t, carry):
        for i in range(early_events):
            @pl.when(t == pairs * i // early_events)
            def _():
                events[i]()

        own(t)
        ahead = t - (pairs - 2 * HEAD + 1)

        @pl.when(jnp.logical_and(ahead >= 0, lax.rem(ahead, 2) == 0))
        def _():
            hops(ahead // 2)

        return carry

    lax.fori_loop(0, pairs, first_phase, 0)
    middle = events[early_events:len(events) - (kv_heads - 1)]

    def second_phase(t, carry):
        def inner(i, carry):
            within(i)
            return carry

        hops(HEAD + t)
        lax.fori_loop(pairs * t // slow, pairs * (t + 1) // slow, inner, 0)
        for i in range(min(slow - 1, len(middle))):
            @pl.when(t == i)
            def _():
                middle[i]()

        return carry

    lax.fori_loop(0, slow, second_phase, 0)
    for late in middle[slow - 1:]:
        late()
    events = events[len(events) - (kv_heads - 1):]
    relayed(0)
    rest = range(1, kv_heads)

    def plain(kv):
        return kv < kv_heads - 1

    def swap_over(kv):
        return pltpu.make_async_remote_copy(
            src_ref=part.at[kv, mate], dst_ref=landy.at[kv, 0], send_sem=pys.at[kv, 0],
            recv_sem=pyr.at[kv, 0], **peer(seq=mate, head=my))

    def pass_both(kv, j):
        return pltpu.make_async_remote_copy(
            src_ref=part.at[kv, pl.ds(2 * j, 2)], dst_ref=landz.at[kv, j], send_sem=pzs.at[kv, j],
            recv_sem=pzr.at[kv, j], **peer(seq=down, head=my))

    def pass_over(kv, j):
        return pltpu.make_async_remote_copy(
            src_ref=part.at[kv, 2 * j + 1 - par], dst_ref=landy.at[kv, j], send_sem=pys.at[kv, j],
            recv_sem=pyr.at[kv, j], **peer(seq=mate, head=my))

    def pass_down(kv, j):
        return pltpu.make_async_remote_copy(
            src_ref=part.at[kv, 2 * j + par], dst_ref=landz.at[kv, j, 0], send_sem=pzs.at[kv, j],
            recv_sem=pzr.at[kv, j], **peer(seq=down, head=my))

    def sends_over(j):
        return jnp.logical_or(j < level, jnp.logical_and(j == level, is_odd))

    def takes_over(j):
        return jnp.logical_or(j < level, jnp.logical_and(j == level, odd == 0))

    def result(kv, total):
        cols = slice(kv * D, kv * D + D)
        dk_out[:, cols] = total[:, :D]
        dv_out[:, cols] = total[:, D:]

    def gather_down(kv, j):
        if plain(kv):
            pass_both(kv, j).wait_recv()
            both = pl.ds(2 * j, 2)
            part[kv, both] = (part[kv, both].astype(F32) + landz[kv, j].astype(F32)).astype(BF16)

            @pl.when(j < level)
            def _():
                pass_both(kv, j).start()

            @pl.when(j == level)
            def _():
                swap_over(kv).start()

            return

        acc[...] = part[kv, 2 * j + par].astype(F32)

        @pl.when(takes_over(j))
        def _():
            pass_over(kv, j).wait_recv()
            acc[...] += landy[kv, j].astype(F32)

        @pl.when(not_top)
        def _():
            pass_down(kv, j).wait_recv()
            acc[...] += landz[kv, j, 0].astype(F32)

        @pl.when(j < level)
        def _():
            part[kv, 2 * j + par] = acc[...].astype(BF16)
            pass_down(kv, j).start()

        @pl.when(j == level)
        def _():
            result(kv, acc[...])

    def gathered(kv):
        if plain(kv):
            swap_over(kv).wait_recv()
            result(kv, part[kv, me].astype(F32) + landy[kv, 0].astype(F32))

    def gather_sent(kv):
        if plain(kv):
            swap_over(kv).wait_send()
        for j in range(levels):
            if not plain(kv):
                @pl.when(sends_over(j))
                def _():
                    pass_over(kv, j).wait_send()

            @pl.when(j < level)
            def _():
                (pass_both if plain(kv) else pass_down)(kv, j).wait_send()

    lag = min(8, pairs)
    slots = pairs + lag

    def slot_of(kv):
        ready = (kv + 1) * (ratio // 2) - 1
        behind = levels - 1 - level
        if plain(kv):
            return ready + 3 * behind, 2
        return ready + 4 + 4 * behind, 1

    def gathers(t):
        for kv in range(kv_heads):
            first, pace = slot_of(kv)
            if plain(kv):
                @pl.when(jnp.logical_and(top_level, t == first))
                def _():
                    def launch(j, carry):
                        @pl.when(j < level)
                        def _():
                            pass_both(kv, j).start()

                        return carry

                    lax.fori_loop(0, levels, launch, 0)
                    swap_over(kv).start()

            since = t - first
            j = since // pace
            fits = jnp.logical_and(since >= 0, jnp.logical_and(j <= level, since == j * pace))
            if plain(kv):
                fits = jnp.logical_and(fits, not_top)

            @pl.when(fits)
            def _():
                gather_down(kv, j)

    def lanes_of(h):
        return pl.ds(pl.multiple_of(h * D, D), D)

    tile = W if length % W == 0 else D
    many = tile // rows

    def attend(p):
        h = 2 * p
        kv = h // ratio
        first, second = lanes_of(h), lanes_of(h + 1)

        @pl.when(lax.rem(h, ratio) == 0)
        def _():
            kt[...] = jnp.transpose(kva[kv, :, :, :D].reshape(length, D).astype(F32)).astype(BF16)
            vt[:D] = jnp.transpose(kva[kv, :, :, D:].reshape(length, D).astype(F32)).astype(BF16)
            dka[...] = jnp.zeros_like(dka)
            dva[...] = jnp.zeros_like(dva)

        q = jnp.concatenate([q_ref[:, first], q_ref[:, second]], axis=0)
        dm = jnp.concatenate([dm_ref[:, first], dm_ref[:, second]], axis=0)
        qe = jnp.concatenate([q, eq[...]], axis=1)
        top = None
        for j in range(length // tile):
            at = slice(j * tile, (j + 1) * tile)
            k = kva[kv, j * many:(j + 1) * many, :, :D].reshape(tile, D)
            s = mm_nt(jnp.concatenate([k, ek[at]], axis=1), qe)
            s_ref[at] = s
            high = jnp.max(s.reshape(tile // 8, 8, 2 * rows), axis=0)
            top = high if top is None else jnp.maximum(top, high)
        top = jnp.max(top, axis=0, keepdims=True) * LOG2
        for j in range(length // tile):
            at = slice(j * tile, (j + 1) * tile)
            e = jnp.exp2(s_ref[at] * LOG2 - top)
            s_ref[at] = e
            eb_ref[at] = e.astype(BF16)
        out_t = mm(vt[...], eb_ref[...])
        inv = 1.0 / out_t[D:D + 1]
        out_t = out_t[:D] * inv
        out = jnp.transpose(out_t)
        att_ref[:, first] = out[:rows]
        att_ref[:, second] = out[rows:]
        delta = jnp.sum(jnp.transpose(dm.astype(F32)) * out_t, axis=0, keepdims=True)
        for j in range(length // tile):
            at = slice(j * tile, (j + 1) * tile)
            v = kva[kv, j * many:(j + 1) * many, :, D:].reshape(tile, D)
            ds_ref[at] = (s_ref[at] * (mm_nt(v, dm) - delta)).astype(BF16)
        dq = jnp.transpose(mm(kt[...], ds_ref[...]) * (inv * SCALE))
        dq_ref[:, first] = dq[:rows]
        dq_ref[:, second] = dq[rows:]
        inv_col = jnp.transpose(jnp.broadcast_to(inv, (D, 2 * rows)))
        dka[...] += mm(ds_ref[...], (q.astype(F32) * inv_col).astype(BF16))
        dva[...] += mm(eb_ref[...], (dm.astype(F32) * inv_col).astype(BF16))

        @pl.when(lax.rem(h, ratio) == ratio - 2)
        def _():
            part[kv, :, :, :D] = (dka[...] * SCALE).astype(BF16).reshape(n, rows, D)
            part[kv, :, :, D:] = dva[...].astype(BF16).reshape(n, rows, D)

        @pl.when(p == (kv_heads * ratio) // 2 - 1)
        def _():
            for j in range(levels):
                @pl.when(sends_over(j))
                def _():
                    pass_over(kv_heads - 1, j).start()

    ones = jnp.ones((EDGE, D), BF16)

    def edge(i):
        return copy(gh, gn, xs, xr, i, prv)

    def states_of(p):
        @pl.when(take_f)
        def _():
            give(p, 0).wait_recv()

        @pl.when(take_b)
        def _():
            give(p, 1).wait_recv()

    def through(p):
        lanes = wide_of(p)
        state = (sm[p] + xf_ref[p].astype(F32)).astype(BF16)
        grad = (gm[p] + xg_ref[p].astype(F32)).astype(BF16)
        xf = xb_ref[:, lanes].astype(F32)
        dmf = dm_ref[:, lanes].astype(F32)
        col = col_ref[:, lanes]
        final = col[rows - 1:]
        back = jnp.exp(final - col) * mm(b, grad)
        y = y_ref[:, lanes] + jnp.exp(col) * mm(c, state)
        mixed_ref[:, lanes] = (y + att_ref[:, lanes]).astype(BF16)
        gx = gx_ref[:, lanes] + back
        net = dmf * y - xf * gx
        hi = net.astype(BF16)
        lo = (net - hi.astype(F32)).astype(BF16)
        inside = jnp.sum(xf * back, axis=0, keepdims=True) + jnp.exp(final) * jnp.sum(
            state.astype(F32) * grad.astype(F32), axis=0, keepdims=True)
        for a in range(2):
            cols = slice(a * D, (a + 1) * D)
            sums = mm_nt(ones, hi[:, cols]) + mm_nt(ones, lo[:, cols])
            net_ref[pl.ds(2 * p + a, 1)] = sums[:1]
            fin_ref[pl.ds(2 * p + a, 1)] = inside[:, cols]
        dbc[:, D:] += mm_nt(dme_ref[:, lanes], state)
        dbc[:, :D] += mm_nt(xt_ref[:, lanes], grad)
        g = gx * sl_ref[:, lanes]
        gh[p] = g[:EDGE].astype(BF16)
        dx_ref[:, lanes] = conv_back(g, jnp.zeros((8, W), F32), w_ref[:, lanes].astype(F32))

    def step(t, carry):
        for kv in rest:
            @pl.when(t == kv * (ratio // 2))
            def _():
                events[kv - 1]()
                relayed(kv)

        hops(HEAD + slow + t)
        attend(t)
        gathers(t)
        return carry

    lax.fori_loop(0, pairs, step, 0)

    def last_hops(t, carry):
        hops(t)
        return carry

    lax.fori_loop(HEAD + slow + pairs, slow + pairs + SLACK, last_hops, 0)

    def finish_through(i, carry):
        two = (2 * i, 2 * i + 1)
        for p in two:
            states_of(p)
        for p in two:
            through(p)

        @pl.when(me > 0)
        def _():
            for p in two:
                edge(p).start()

        for p in two:
            gathers(pairs + p)
        return carry

    lax.fori_loop(0, pairs // 2, finish_through, 0)
    di = dinner[...]
    dbcb[:, D:] = (dbc[:, D:] + mm(di.astype(BF16), b)).astype(BF16)
    dbcb[:, :D] = (dbc[:, :D] + mm(jnp.transpose(di).astype(BF16), c)).astype(BF16)

    def remote(src, dst, send, recv, seq, head):
        return pltpu.make_async_remote_copy(
            src_ref=src, dst_ref=dst, send_sem=send, recv_sem=recv, **peer(seq=seq, head=head))

    def across(off):
        return remote(dbcb, bb.at[off], bs.at[off], br.at[off], me, lax.rem(my + off, m))

    def before(off):
        return remote(dbcb.at[pl.ds(0, EDGE)], nb.at[off], ns.at[off], nr.at[off], prv,
                      lax.rem(my + off, m))

    for off in range(1, m):
        across(off).start()

    @pl.when(me > 0)
    def _():
        for off in range(m):
            before(off).start()

    dla_ref[...] = exact(mm, net_ref[...], lower) + exact(mm, fin_ref[...], jnp.ones((D, rows), BF16))

    for kv in range(kv_heads):
        first, pace = slot_of(kv)

        def leftover(j, carry):
            later = jnp.logical_and(j <= level, first + pace * j >= slots)
            if plain(kv):
                later = jnp.logical_and(later, not_top)

            @pl.when(later)
            def _():
                gather_down(kv, j)

            return carry

        lax.fori_loop(0, levels, leftover, 0)

    @pl.when(me < n - 1)
    def _():
        def finish(i, carry):
            lanes = wide_of(i)
            edge(i).wait_recv()
            after = jnp.concatenate([jnp.zeros((8, W), F32), gn[i].astype(F32)[:8]], axis=0)
            taps = w_ref[:, lanes].astype(F32)
            fix = None
            for tap in range(taps.shape[0]):
                offset = taps.shape[0] - 1 - tap
                term = taps[tap:tap + 1] * after[offset:offset + 8]
                fix = term if fix is None else fix + term
            dx_ref[rows - 8:, lanes] += fix
            return carry

        lax.fori_loop(0, pairs, finish, 0)
        for off in range(m):
            before(off).wait_recv()

    @pl.when(me == n - 1)
    def _():
        nb[...] = jnp.zeros(nb.shape, nb.dtype)

    total = dbcb[...].astype(F32)
    for off in range(1, m):
        across(off).wait_recv()
        total += bb[off].astype(F32)
    follow = nb[0].astype(F32)
    for off in range(1, m):
        follow += nb[off].astype(F32)
    dbc_out[...] = conv_back(total * bcsl[...], (follow * bcsn[...])[:8], wbc)

    for kv in range(kv_heads):
        gathered(kv)

    for off in range(1, m):
        across(off).wait_send()

    @pl.when(me > 0)
    def _():
        def edge_sent(i, carry):
            edge(i).wait_send()
            return carry

        lax.fori_loop(0, pairs, edge_sent, 0)
        for off in range(m):
            before(off).wait_send()

    for kv in range(kv_heads):
        gather_sent(kv)

    def drain(i, carry):
        @pl.when(not_top)
        def _():
            climb(i).wait_send()

        @pl.when(level > 0)
        def _():
            descend(i).wait_send()

        @pl.when(give_f)
        def _():
            give(i, 0).wait_send()

        @pl.when(give_b)
        def _():
            give(i, 1).wait_send()

        return carry

    lax.fori_loop(0, pairs, drain, 0)
    for kv in range(kv_heads):
        relay_sent(kv)

    @pl.when(me < n - 1)
    def _():
        cb.wait_send()
        cx.wait_send()

    @pl.when(me > 0)
    def _():
        cn.wait_send()


def block_part(n, m, x_in, bc_in, conv_x, conv_bc, log_decay, skip, queries, keys, values, d_mixed):
    rows, wide = x_in.shape
    width = keys.shape[1]
    heads = wide // D
    pairs = heads // 2
    kv_heads = width // D
    length = n * rows
    taps = conv_x.shape[0]
    dma = pltpu.SemaphoreType.DMA
    shape = jax.ShapeDtypeStruct

    def v(dims, dtype=F32):
        return pltpu.VMEM(dims, dtype)

    def stay(a):
        return pltpu.with_memory_space_constraint(a, pltpu.HBM)

    state = (pairs, D, W)
    return pl.pallas_call(
        functools.partial(block_kernel, n, m),
        out_shape=(
            shape((rows, wide), BF16), shape((rows, wide), F32), shape((rows, width), F32),
            shape((rows, width), F32), shape((rows, wide), F32), shape((rows, W), F32),
            shape((heads, rows), F32)),
        in_specs=[HBM] * 5 + [SMEM] + [HBM] * 4,
        out_specs=(VMEM,) * 7,
        scratch_shapes=[
            v((rows, wide), BF16), v((rows, wide), BF16), v((rows, wide), BF16), v((taps, wide), BF16),
            v(bc_in.shape, BF16), v(conv_bc.shape, BF16), v((heads, rows)), v((rows, W), BF16),
            v((kv_heads, n, rows, W), BF16), v((EDGE, wide), BF16), v((EDGE, W), BF16), v((EDGE, W), BF16),
            v((rows, wide), BF16), v((rows, wide)), v((rows, wide)), v((rows, wide), BF16),
            v((rows, wide), BF16), v((rows, wide)), v((rows, wide)), v((rows, wide)),
            v((rows, W), BF16), v((rows, W)), v((EDGE, W)), v((D, rows), BF16), v((D, rows), BF16),
            v((pairs, 1, W)), v((pairs, 1, W)), v((pairs, 1, W)), v((rows, W)), v((rows, W)),
            v((rows, rows)), v((rows, W)), v((rows, W), BF16), v((heads, rows)), v((heads, rows)),
            *[v(state) for _ in range(4)], *[v(state, BF16) for _ in range(8)],
            v((length, W)), v((length, W), BF16), v((length, W), BF16), v((D, length), BF16),
            v((D + EDGE, length), BF16), v((length, D), BF16), v((2 * rows, D), BF16), v((length, D)),
            v((length, D)), v((kv_heads, n, rows, W), BF16), v((kv_heads, n // 2, rows, W), BF16),
            v((kv_heads, n // 2, 2, rows, W), BF16), v((rows, W)),
            v((pairs, EDGE, W), BF16), v((pairs, EDGE, W), BF16), v((m, rows, W), BF16), v((m, EDGE, W), BF16),
            dma((2 * kv_heads + 7,)), *[dma((kv_heads, n)) for _ in range(4)], dma((3,)), dma((3,)),
            dma, dma, *[dma((pairs,)) for _ in range(8)],
            *[dma((kv_heads, n // 2)) for _ in range(4)], dma((pairs,)), dma((pairs,)), dma((m,)), dma((m,)), dma((m,)), dma((m,))],
        compiler_params=pltpu.CompilerParams(
            collective_id=0, has_side_effects=True, vmem_limit_bytes=40 * 2**20),
        name="block",
    )(*map(stay, (x_in, bc_in, conv_x, conv_bc, log_decay.T, skip, queries, keys, values, d_mixed)))


def write_kernel(mixed, dq, dk, dv, dx, dbc, dla, mixed_o, dq_o, dk_o, dv_o, dx_o, dbc_o, dla_o, dbc3, sem):
    quarter = dq.shape[0] // 4
    copies = [(a.at[pl.ds(i * quarter, quarter)], b.at[pl.ds(i * quarter, quarter)])
              for a, b in ((dq, dq_o), (dx, dx_o), (mixed, mixed_o)) for i in range(4)]
    copies += [(dk, dk_o), (dv, dv_o), (dla, dla_o), (dbc3, dbc_o)]
    copies = [pltpu.make_async_copy(src, dst, sem.at[i]) for i, (src, dst) in enumerate(copies)]
    for cp in copies[:-1]:
        cp.start()
    dbc3[:, 0, :] = dbc[:, :D]
    dbc3[:, 1, :] = dbc[:, D:]
    copies[-1].start()
    for cp in copies:
        cp.wait()


def write_part(mixed, dq, dk, dv, dx, dbc, dla):
    rows = dbc.shape[0]
    outs = tuple(jax.ShapeDtypeStruct(a.shape, a.dtype) for a in (mixed, dq, dk, dv, dx))
    outs += (jax.ShapeDtypeStruct((rows, 2, D), F32), jax.ShapeDtypeStruct(dla.shape, F32))
    return pl.pallas_call(
        write_kernel,
        out_shape=outs,
        in_specs=[VMEM] * 7,
        out_specs=(HBM,) * 7,
        scratch_shapes=[pltpu.VMEM((rows, 2, D), F32), pltpu.SemaphoreType.DMA((16,))],
        compiler_params=pltpu.CompilerParams(vmem_limit_bytes=2 * 2**20),
        name="write",
    )(mixed, dq, dk, dv, dx, dbc, dla)


def shards(n, m, *args):
    *outs, dla = write_part(*block_part(n, m, *args))
    return (*outs, dla.T)


def solution(mesh):
    n, m = mesh.shape["seq"], mesh.shape["head"]
    grid = P("seq", "head")
    part = P("seq", None, None)
    in_specs = (grid, part, P(None, "head"), P(), grid, P("head"), grid, grid, grid, grid)
    out_specs = (grid, grid, grid, grid, grid, part, grid)
    return jax.shard_map(functools.partial(shards, n, m), mesh=mesh, in_specs=in_specs,
                         out_specs=out_specs, check_vma=False)
```

```python
import functools
import math

import jax
import jax.numpy as jnp
from jax import lax
from jax.experimental import pallas as pl
from jax.experimental.pallas import tpu as pltpu
from jax.sharding import PartitionSpec as P

D = 128
W = 2 * D
EDGE = 16
SLACK = 1
HEAD = 0
F32 = jnp.float32
BF16 = jnp.bfloat16
MESH = pl.DeviceIdType.MESH
VMEM = pl.BlockSpec(memory_space=pltpu.VMEM)
HBM = pl.BlockSpec(memory_space=pltpu.HBM)
SMEM = pl.BlockSpec(memory_space=pltpu.SMEM)
SCALE = D ** (-0.5)
LOG2 = SCALE * math.log2(math.e)


def mm(a, b):
    return jnp.dot(a, b, preferred_element_type=F32)


def mm_nt(a, b):
    return lax.dot_general(a, b, (((1,), (1,)), ((), ())), preferred_element_type=F32)


def sigmoid(v):
    return 1.0 / (1.0 + jnp.exp(-v))


def peer(**coords):
    return dict(device_id=coords, device_id_type=MESH)


def split3(v):
    hi = v.astype(BF16)
    rest = v - hi.astype(F32)
    mid = rest.astype(BF16)
    return hi, mid, (rest - mid.astype(F32)).astype(BF16)


def exact(dot, a, b):
    if a.dtype == BF16:
        hi, mid, lo = split3(b)
        return (dot(a, hi) + dot(a, mid)) + dot(a, lo)
    hi, mid, lo = split3(a)
    return (dot(hi, b) + dot(mid, b)) + dot(lo, b)


def conv(x, halo, taps):
    width = taps.shape[0]
    rows = x.shape[0]
    full = jnp.concatenate([halo[EDGE - 8:], x], axis=0)
    total = None
    for tap in range(width):
        start = 8 - (width - 1) + tap
        term = taps[tap:tap + 1] * full[start:start + rows]
        total = term if total is None else total + term
    return total


def conv_back(grads, after, taps):
    width = taps.shape[0]
    rows = grads.shape[0]
    padded = jnp.concatenate([grads, after], axis=0)
    total = None
    for tap in range(width):
        offset = width - 1 - tap
        term = taps[tap:tap + 1] * padded[offset:offset + rows]
        total = term if total is None else total + term
    return total


def iota(shape, axis):
    return lax.broadcasted_iota(jnp.int32, shape, axis)


def block_kernel(n, m, x_hbm, bc_hbm, w_hbm, wbc_hbm, ld_hbm, skip_ref, q_hbm, k_hbm, v_hbm, dm_hbm,
                 mixed_ref, dq_ref, dk_out, dv_out, dx_ref, dbc_out, dla_ref,
                 x_ref, dm_ref, q_ref, w_ref, bc3, wbc3, ld_ref, bcs, kva, xh, bch, bcn,
                 xb_ref, sl_ref, col_ref, xt_ref, dme_ref, y_ref, gx_ref, att_ref,
                 bcv, bcsl, bcsn, bt, ct, rowp, dec, rdec, inner, innert, dinner, dbc, dbcb, net_ref, fin_ref,
                 of, ob, sm, gm, af, ab, sf, sb, mf, mb, xf_ref, xg_ref,
                 s_ref, eb_ref, ds_ref, kt, vt, ek, eq, dka, dva, part, landy, landz, acc,
                 gh, gn, bb, nb,
                 ls, zs, zr, fs, fr, hs, hr, es, er,
                 cfs, cfr, cbs, cbr, mfs, mfr, mbs, mbr, pys, pyr, pzs, pzr, xs, xr, bs, br, ns, nr):
    me = lax.axis_index("seq")
    my = lax.axis_index("head")
    odd = lax.rem(me, 2)
    is_odd = odd == 1
    mate = me + 1 - 2 * odd
    level = me // 2
    levels = n // 2
    rows, wide = x_ref.shape
    width = k_hbm.shape[1]
    heads = wide // D
    pairs = heads // 2
    kv_heads = width // D
    ratio = heads // kv_heads
    length = n * rows
    nxt = lax.rem(me + 1, n)
    prv = lax.rem(me + n - 1, n)
    up = lax.rem(me + 2, n)
    down = lax.rem(me + n - 2, n)

    barrier = pltpu.get_barrier_semaphore()
    count = 0
    for off in range(1, n):
        pl.semaphore_signal(barrier, inc=1, **peer(seq=lax.rem(me + off, n), head=my))
        count += 1
    for off in range(1, m):
        for to in (me, nxt, prv):
            pl.semaphore_signal(barrier, inc=1, **peer(seq=to, head=lax.rem(my + off, m)))
            count += 1

    loads = [(ld_hbm, ld_ref)]
    for kv in range(kv_heads):
        lanes = pl.ds(kv * D, D)
        loads.append((k_hbm.at[:, lanes], kva.at[kv, me, :, pl.ds(0, D)]))
        loads.append((v_hbm.at[:, lanes], kva.at[kv, me, :, pl.ds(D, D)]))
    loads += [
        (bc_hbm, bc3), (wbc_hbm, wbc3), (w_hbm, w_ref), (x_hbm, x_ref), (dm_hbm, dm_ref), (q_hbm, q_ref)]
    loads = [pltpu.make_async_copy(src, dst, ls.at[i]) for i, (src, dst) in enumerate(loads)]
    for cp in loads:
        cp.start()

    t_i = iota((rows, rows), 0)
    s_i = iota((rows, rows), 1)
    lower = jnp.where(t_i >= s_i, 1.0, 0.0).astype(BF16)
    loads[0].wait()
    cum = exact(mm_nt, lower, ld_ref[...])
    parts = split3(cum)
    ident = jnp.where(iota((heads, heads), 0) == iota((heads, heads), 1), 1.0, 0.0).astype(BF16)
    cum_rows = (mm_nt(ident, parts[0]) + mm_nt(ident, parts[1])) + mm_nt(ident, parts[2])
    for h in range(heads):
        rowp[h // 2, :, (h % 2) * D:(h % 2) * D + D] = cum_rows[h:h + 1]

    def column(p, first):
        pick = jnp.where(iota((heads, W), 0) == 2 * p + iota((heads, W), 1) // D, 1.0, 0.0).astype(BF16)
        return (mm(parts[0][first:], pick) + mm(parts[1][first:], pick)) + mm(parts[2][first:], pick)

    def decay(p, carry):
        dec[p] = jnp.exp(column(p, rows - EDGE)[EDGE - 1:])
        return carry

    lax.fori_loop(0, pairs, decay, 0)

    cross = max(levels // 4, 1)
    early = level < cross
    for off in range(1, n):
        fill = me + off < n
        if off == 1:
            fill = jnp.logical_and(fill, jnp.logical_or(is_odd, jnp.logical_not(early)))

        @pl.when(fill)
        def _():
            for kv in range(kv_heads):
                kva[kv, lax.rem(me + off, n)] = jnp.zeros(kva.shape[2:], kva.dtype)

    big = -(2.0 ** 100)
    e_i = iota((rows, D), 1)
    r_i = iota((rows, D), 0)
    inside = jnp.where((r_i == e_i) & (e_i > 0), big, 0.0).astype(BF16)
    outside = jnp.where(e_i == 0, big, 0.0).astype(BF16)
    for j in range(n):
        later = jnp.where(me < j, outside, jnp.zeros_like(outside))
        ek[j * rows:(j + 1) * rows] = jnp.where(me == j, inside, later)
    reach = jnp.where((e_i > r_i) | (e_i == 0), 1.0, 0.0).astype(BF16)
    eq[:rows] = reach
    eq[rows:] = reach
    vt[D:] = jnp.ones((vt.shape[0] - D, length), BF16)

    for cp in loads[1:-2]:
        cp.wait()
    bcs[:, :D] = bc3[...].astype(F32)[:, 0, :].astype(BF16)
    bcs[:, D:] = bc3[...].astype(F32)[:, 1, :].astype(BF16)
    wbc = jnp.concatenate([wbc3[...].astype(F32)[:, 0, :], wbc3[...].astype(F32)[:, 1, :]], axis=1)
    pl.semaphore_wait(barrier, count)

    def halo(slot, src, dst, to):
        return pltpu.make_async_remote_copy(
            src_ref=src, dst_ref=dst, send_sem=hs.at[slot], recv_sem=hr.at[slot],
            **peer(seq=to, head=my))

    last = pl.ds(rows - EDGE, EDGE)
    cx = halo(0, x_ref.at[last], xh, nxt)
    cb = halo(1, bcs.at[last], bch, nxt)
    cn = halo(2, bcs.at[pl.ds(0, EDGE)], bcn, prv)

    swap = pltpu.make_async_remote_copy(
        src_ref=dec, dst_ref=rdec, send_sem=es, recv_sem=er, **peer(seq=mate, head=my))
    swap.start()

    @pl.when(me < n - 1)
    def _():
        cb.start()
        cx.start()

    @pl.when(me > 0)
    def _():
        cn.start()

    par = odd

    def rise(kv, blk):
        return pltpu.make_async_remote_copy(
            src_ref=kva.at[kv, blk], dst_ref=kva.at[kv, blk], send_sem=zs.at[kv, blk],
            recv_sem=zr.at[kv, blk], **peer(seq=up, head=my))

    def over(kv, blk):
        return pltpu.make_async_remote_copy(
            src_ref=kva.at[kv, blk], dst_ref=kva.at[kv, blk], send_sem=fs.at[kv, blk],
            recv_sem=fr.at[kv, blk], **peer(seq=mate, head=my))

    not_top = level < levels - 1
    crosses = jnp.logical_or(odd == 0, early)
    for kv in range(kv_heads):
        @pl.when(not_top)
        def _():
            rise(kv, me).start()

        @pl.when(crosses)
        def _():
            over(kv, me).start()

    def relay_first(kv):
        @pl.when(early)
        def _():
            over(kv, mate).wait_recv()
            rise(kv, mate).start()

    def relay_mine(kv, k):
        @pl.when(level >= k)
        def _():
            blk = 2 * (level - k) + par
            rise(kv, blk).wait_recv()

            @pl.when(not_top)
            def _():
                rise(kv, blk).start()

            @pl.when(level - k >= cross)
            def _():
                over(kv, blk).start()

    def relay_other(kv, k):
        @pl.when(jnp.logical_and(level >= k, level - k < cross))
        def _():
            blk = 2 * (level - k) + 1 - par
            rise(kv, blk).wait_recv()

            @pl.when(not_top)
            def _():
                rise(kv, blk).start()

    def relayed(kv):
        @pl.when(jnp.logical_and(odd == 1, jnp.logical_not(early)))
        def _():
            over(kv, mate).wait_recv()

        for k in range(1, levels):
            @pl.when(jnp.logical_and(level >= k, level - k >= cross))
            def _():
                over(kv, 2 * (level - k) + 1 - par).wait_recv()

    def relay_sent(kv):
        @pl.when(not_top)
        def _():
            rise(kv, me).wait_send()

        @pl.when(crosses)
        def _():
            over(kv, me).wait_send()

        @pl.when(early)
        def _():
            rise(kv, mate).wait_send()

        for k in range(1, levels):
            far = level - k

            @pl.when(jnp.logical_and(level >= k, not_top))
            def _():
                rise(kv, 2 * far + par).wait_send()

            @pl.when(jnp.logical_and(level >= k, far >= cross))
            def _():
                over(kv, 2 * far + par).wait_send()

            @pl.when(jnp.logical_and(jnp.logical_and(level >= k, far < cross), not_top))
            def _():
                rise(kv, 2 * far + 1 - par).wait_send()

    def event(kv, k):
        if k == 0:
            relay_first(kv)
        else:
            relay_other(kv, k)
        if k < levels - 1:
            relay_mine(kv, k + 1)

    events = [functools.partial(event, kv, k) for k in range(levels) for kv in range(kv_heads)]

    @pl.when(me == 0)
    def _():
        xh[...] = jnp.zeros(xh.shape, xh.dtype)
        bch[...] = jnp.zeros(bch.shape, bch.dtype)

    @pl.when(me == n - 1)
    def _():
        bcn[...] = jnp.zeros(bcn.shape, bcn.dtype)

    loads[-2].wait()
    loads[-1].wait()

    def wide_of(p):
        return pl.ds(pl.multiple_of(p * W, W), W)

    def prepare(p, carry):
        lanes = wide_of(p)
        sl_ref[:, lanes] = conv(
            x_ref[:, lanes].astype(F32), jnp.zeros((EDGE, W), F32), w_ref[:, lanes].astype(F32))
        col = column(p, 0)
        col_ref[:, lanes] = col
        dme_ref[:, lanes] = (dm_ref[:, lanes].astype(F32) * jnp.exp(col)).astype(BF16)
        return carry

    lax.fori_loop(0, pairs, prepare, 0)
    events.pop(0)()

    @pl.when(me > 0)
    def _():
        cb.wait_recv()
        cx.wait_recv()

    @pl.when(me < n - 1)
    def _():
        cn.wait_recv()

    def slope(pre, sig):
        return sig * (1.0 + pre * (1.0 - sig))

    pre = conv(bcs[...].astype(F32), bch[...].astype(F32), wbc)
    sig = sigmoid(pre)
    act = (pre * sig).astype(BF16)
    bcv[...] = act
    bcsl[...] = slope(pre, sig)
    pre = conv(bcn[...].astype(F32), bcs[rows - EDGE:].astype(F32), wbc)
    bcsn[...] = slope(pre, sigmoid(pre))
    act = act.astype(F32)
    bt[...] = jnp.transpose(act[:, :D]).astype(BF16)
    ct[...] = jnp.transpose(act[:, D:]).astype(BF16)
    b = bcv[:, :D]
    c = bcv[:, D:]
    own_inner = mm_nt(c, b)
    own_innert = mm_nt(b, c)
    for a in range(2):
        inner[:, a * D:(a + 1) * D] = own_inner
        innert[:, a * D:(a + 1) * D] = own_innert
    dinner[...] = jnp.zeros_like(dinner)
    dbc[...] = jnp.zeros_like(dbc)

    bottom = level == 0
    top_level = level == levels - 1
    give_f = jnp.logical_or(odd == 0, jnp.logical_not(bottom))
    take_f = jnp.logical_or(is_odd, jnp.logical_not(bottom))
    give_b = jnp.logical_or(is_odd, jnp.logical_not(top_level))
    take_b = jnp.logical_or(odd == 0, jnp.logical_not(top_level))

    @pl.when(jnp.logical_not(take_f))
    def _():
        xf_ref[...] = jnp.zeros(xf_ref.shape, BF16)

    @pl.when(jnp.logical_not(take_b))
    def _():
        xg_ref[...] = jnp.zeros(xg_ref.shape, BF16)

    def own(p):
        lanes = wide_of(p)
        pre = sl_ref[:, lanes]
        fix = conv(jnp.zeros((8, W), F32), xh[:, lanes].astype(F32), w_ref[:, lanes].astype(F32))
        pre = jnp.concatenate([pre[:8] + fix, pre[8:]], axis=0)
        sig = sigmoid(pre)
        xb = (pre * sig).astype(BF16)
        xb_ref[:, lanes] = xb
        sl_ref[:, lanes] = slope(pre, sig)
        col = col_ref[:, lanes]
        dme = dme_ref[:, lanes]
        final = col[rows - 1:]
        xt = (xb.astype(F32) * jnp.exp(final - col)).astype(BF16)
        xt_ref[:, lanes] = xt
        of[p] = mm(bt[...], xt)
        ob[p] = mm(ct[...], dme)

        @pl.when(bottom)
        def _():
            hop_f(p)

        @pl.when(top_level)
        def _():
            hop_b(p)

    def skips(p):
        return jnp.where(iota((1, W), 1) < D, skip_ref[2 * p], skip_ref[2 * p + 1])

    t_w = iota((rows, W), 0)
    s_w = lax.rem(iota((rows, W), 1), D)

    def within(p):
        lanes = wide_of(p)
        xb = xb_ref[:, lanes]
        dm = dm_ref[:, lanes]
        gap = col_ref[:, lanes] - rowp[p]
        fade = jnp.exp(jnp.where(t_w >= s_w, gap, -1e30))
        fadet = jnp.exp(jnp.where(s_w >= t_w, -gap, -1e30))
        mix = (inner[...] * fade).astype(BF16)
        mixt = (innert[...] * fadet).astype(BF16)
        skip = skips(p)
        total = None
        ys, gs = [], []
        for a in range(2):
            cols = slice(a * D, (a + 1) * D)
            ys.append(mm(mix[:, cols], xb[:, cols]))
            gs.append(mm(mixt[:, cols], dm[:, cols]))
            term = mm_nt(dm[:, cols], xb[:, cols]) * fade[:, cols]
            total = term if total is None else total + term
        dinner[...] += total
        y_ref[:, lanes] = jnp.concatenate(ys, axis=1) + skip * xb.astype(F32)
        gx_ref[:, lanes] = jnp.concatenate(gs, axis=1) + skip * dm.astype(F32)

    def copy(stage, landing, send, recv, i, to):
        return pltpu.make_async_remote_copy(
            src_ref=stage.at[i], dst_ref=landing.at[i], send_sem=send.at[i], recv_sem=recv.at[i],
            **peer(seq=to, head=my))

    def climb(i):
        return copy(sf, af, cfs, cfr, i, up)

    def descend(i):
        return copy(sb, ab, cbs, cbr, i, down)

    def give(i, which):
        src, dst, send, recv = ((mf, xf_ref, mfs, mfr), (mb, xg_ref, mbs, mbr))[which]
        return copy(src, dst, send, recv, i, mate)

    def decays(i):
        mine, other = dec[i], rdec[i]
        return jnp.where(is_odd, other, mine), jnp.where(is_odd, mine, other)

    def hop_f(i):
        @pl.when(bottom)
        def _():
            af[i] = jnp.zeros(af.shape[1:], BF16)

        @pl.when(jnp.logical_not(bottom))
        def _():
            climb(i).wait_recv()

        even_d, odd_d = decays(i)
        x = af[i].astype(F32)
        mine = of[i]
        near = even_d * x
        mf[i] = jnp.where(is_odd, x, near + mine).astype(BF16)
        sm[i] = jnp.where(is_odd, near, x)

        @pl.when(not_top)
        def _():
            sf[i] = (odd_d * near + jnp.where(is_odd, 1.0, odd_d) * mine).astype(BF16)
            climb(i).start()

        @pl.when(give_f)
        def _():
            give(i, 0).start()

    def hop_b(i):
        @pl.when(top_level)
        def _():
            ab[i] = jnp.zeros(ab.shape[1:], BF16)

        @pl.when(not_top)
        def _():
            descend(i).wait_recv()

        even_d, odd_d = decays(i)
        x = ab[i].astype(F32)
        mine = ob[i]
        near = odd_d * x
        mb[i] = jnp.where(is_odd, near + mine, x).astype(BF16)
        gm[i] = jnp.where(is_odd, x, near)

        @pl.when(jnp.logical_not(bottom))
        def _():
            sb[i] = (even_d * near + jnp.where(is_odd, even_d, 1.0) * mine).astype(BF16)
            descend(i).start()

        @pl.when(give_b)
        def _():
            give(i, 1).start()

    def hops(t):
        f = t - 2 * (level - 1) - jnp.where(top_level, SLACK, 0)
        g = t - 2 * (levels - 2 - level) - jnp.where(bottom, SLACK, 0)

        @pl.when(jnp.logical_and(jnp.logical_not(bottom), jnp.logical_and(f >= 0, f < pairs)))
        def _():
            hop_f(f)

        @pl.when(jnp.logical_and(not_top, jnp.logical_and(g >= 0, g < pairs)))
        def _():
            hop_b(g)

    swap.wait()
    slow = 2 * (levels - 2)
    early_events = max(len(events) - slow, 1)

    def first_phase(t, carry):
        for i in range(early_events):
            @pl.when(t == pairs * i // early_events)
            def _():
                events[i]()

        own(t)
        ahead = t - (pairs - 2 * HEAD + 1)

        @pl.when(jnp.logical_and(ahead >= 0, lax.rem(ahead, 2) == 0))
        def _():
            hops(ahead // 2)

        return carry

    lax.fori_loop(0, pairs, first_phase, 0)
    middle = events[early_events:len(events) - (kv_heads - 1)]

    def second_phase(t, carry):
        def inner(i, carry):
            within(i)
            return carry

        hops(HEAD + t)
        lax.fori_loop(pairs * t // slow, pairs * (t + 1) // slow, inner, 0)
        for i in range(min(slow - 1, len(middle))):
            @pl.when(t == i)
            def _():
                middle[i]()

        return carry

    lax.fori_loop(0, slow, second_phase, 0)
    for late in middle[slow - 1:]:
        late()
    events = events[len(events) - (kv_heads - 1):]
    relayed(0)
    rest = range(1, kv_heads)

    def plain(kv):
        return kv < kv_heads - 1

    def swap_over(kv):
        return pltpu.make_async_remote_copy(
            src_ref=part.at[kv, mate], dst_ref=landy.at[kv, 0], send_sem=pys.at[kv, 0],
            recv_sem=pyr.at[kv, 0], **peer(seq=mate, head=my))

    def pass_both(kv, j):
        return pltpu.make_async_remote_copy(
            src_ref=part.at[kv, pl.ds(2 * j, 2)], dst_ref=landz.at[kv, j], send_sem=pzs.at[kv, j],
            recv_sem=pzr.at[kv, j], **peer(seq=down, head=my))

    def pass_over(kv, j):
        return pltpu.make_async_remote_copy(
            src_ref=part.at[kv, 2 * j + 1 - par], dst_ref=landy.at[kv, j], send_sem=pys.at[kv, j],
            recv_sem=pyr.at[kv, j], **peer(seq=mate, head=my))

    def pass_down(kv, j):
        return pltpu.make_async_remote_copy(
            src_ref=part.at[kv, 2 * j + par], dst_ref=landz.at[kv, j, 0], send_sem=pzs.at[kv, j],
            recv_sem=pzr.at[kv, j], **peer(seq=down, head=my))

    def sends_over(j):
        return jnp.logical_or(j < level, jnp.logical_and(j == level, is_odd))

    def takes_over(j):
        return jnp.logical_or(j < level, jnp.logical_and(j == level, odd == 0))

    def result(kv, total):
        cols = slice(kv * D, kv * D + D)
        dk_out[:, cols] = total[:, :D]
        dv_out[:, cols] = total[:, D:]

    def gather_down(kv, j):
        if plain(kv):
            pass_both(kv, j).wait_recv()
            both = pl.ds(2 * j, 2)
            part[kv, both] = (part[kv, both].astype(F32) + landz[kv, j].astype(F32)).astype(BF16)

            @pl.when(j < level)
            def _():
                pass_both(kv, j).start()

            @pl.when(j == level)
            def _():
                swap_over(kv).start()

            return

        acc[...] = part[kv, 2 * j + par].astype(F32)

        @pl.when(takes_over(j))
        def _():
            pass_over(kv, j).wait_recv()
            acc[...] += landy[kv, j].astype(F32)

        @pl.when(not_top)
        def _():
            pass_down(kv, j).wait_recv()
            acc[...] += landz[kv, j, 0].astype(F32)

        @pl.when(j < level)
        def _():
            part[kv, 2 * j + par] = acc[...].astype(BF16)
            pass_down(kv, j).start()

        @pl.when(j == level)
        def _():
            result(kv, acc[...])

    def gathered(kv):
        if plain(kv):
            swap_over(kv).wait_recv()
            result(kv, part[kv, me].astype(F32) + landy[kv, 0].astype(F32))

    def gather_sent(kv):
        if plain(kv):
            swap_over(kv).wait_send()
        for j in range(levels):
            if not plain(kv):
                @pl.when(sends_over(j))
                def _():
                    pass_over(kv, j).wait_send()

            @pl.when(j < level)
            def _():
                (pass_both if plain(kv) else pass_down)(kv, j).wait_send()

    lag = min(8, pairs)
    slots = pairs + lag

    def slot_of(kv):
        ready = (kv + 1) * (ratio // 2) - 1
        behind = levels - 1 - level
        if plain(kv):
            return ready + 3 * behind, 2
        return ready + 4 + 4 * behind, 1

    def gathers(t):
        for kv in range(kv_heads):
            first, pace = slot_of(kv)
            if plain(kv):
                @pl.when(jnp.logical_and(top_level, t == first))
                def _():
                    def launch(j, carry):
                        @pl.when(j < level)
                        def _():
                            pass_both(kv, j).start()

                        return carry

                    lax.fori_loop(0, levels, launch, 0)
                    swap_over(kv).start()

            since = t - first
            j = since // pace
            fits = jnp.logical_and(since >= 0, jnp.logical_and(j <= level, since == j * pace))
            if plain(kv):
                fits = jnp.logical_and(fits, not_top)

            @pl.when(fits)
            def _():
                gather_down(kv, j)

    def lanes_of(h):
        return pl.ds(pl.multiple_of(h * D, D), D)

    tile = W if length % W == 0 else D
    many = tile // rows

    def attend(p):
        h = 2 * p
        kv = h // ratio
        first, second = lanes_of(h), lanes_of(h + 1)

        @pl.when(lax.rem(h, ratio) == 0)
        def _():
            kt[...] = jnp.transpose(kva[kv, :, :, :D].reshape(length, D).astype(F32)).astype(BF16)
            vt[:D] = jnp.transpose(kva[kv, :, :, D:].reshape(length, D).astype(F32)).astype(BF16)
            dka[...] = jnp.zeros_like(dka)
            dva[...] = jnp.zeros_like(dva)

        q = jnp.concatenate([q_ref[:, first], q_ref[:, second]], axis=0)
        dm = jnp.concatenate([dm_ref[:, first], dm_ref[:, second]], axis=0)
        qe = jnp.concatenate([q, eq[...]], axis=1)
        top = None
        for j in range(length // tile):
            at = slice(j * tile, (j + 1) * tile)
            k = kva[kv, j * many:(j + 1) * many, :, :D].reshape(tile, D)
            s = mm_nt(jnp.concatenate([k, ek[at]], axis=1), qe)
            s_ref[at] = s
            high = jnp.max(s.reshape(tile // 8, 8, 2 * rows), axis=0)
            top = high if top is None else jnp.maximum(top, high)
        top = jnp.max(top, axis=0, keepdims=True) * LOG2
        for j in range(length // tile):
            at = slice(j * tile, (j + 1) * tile)
            e = jnp.exp2(s_ref[at] * LOG2 - top)
            s_ref[at] = e
            eb_ref[at] = e.astype(BF16)
        out_t = mm(vt[...], eb_ref[...])
        inv = 1.0 / out_t[D:D + 1]
        out_t = out_t[:D] * inv
        out = jnp.transpose(out_t)
        att_ref[:, first] = out[:rows]
        att_ref[:, second] = out[rows:]
        delta = jnp.sum(jnp.transpose(dm.astype(F32)) * out_t, axis=0, keepdims=True)
        for j in range(length // tile):
            at = slice(j * tile, (j + 1) * tile)
            v = kva[kv, j * many:(j + 1) * many, :, D:].reshape(tile, D)
            ds_ref[at] = (s_ref[at] * (mm_nt(v, dm) - delta)).astype(BF16)
        dq = jnp.transpose(mm(kt[...], ds_ref[...]) * (inv * SCALE))
        dq_ref[:, first] = dq[:rows]
        dq_ref[:, second] = dq[rows:]
        inv_col = jnp.transpose(jnp.broadcast_to(inv, (D, 2 * rows)))
        dka[...] += mm(ds_ref[...], (q.astype(F32) * inv_col).astype(BF16))
        dva[...] += mm(eb_ref[...], (dm.astype(F32) * inv_col).astype(BF16))

        @pl.when(lax.rem(h, ratio) == ratio - 2)
        def _():
            part[kv, :, :, :D] = (dka[...] * SCALE).astype(BF16).reshape(n, rows, D)
            part[kv, :, :, D:] = dva[...].astype(BF16).reshape(n, rows, D)

        @pl.when(p == (kv_heads * ratio) // 2 - 1)
        def _():
            for j in range(levels):
                @pl.when(sends_over(j))
                def _():
                    pass_over(kv_heads - 1, j).start()

    ones = jnp.ones((EDGE, D), BF16)

    def edge(i):
        return copy(gh, gn, xs, xr, i, prv)

    def states_of(p):
        @pl.when(take_f)
        def _():
            give(p, 0).wait_recv()

        @pl.when(take_b)
        def _():
            give(p, 1).wait_recv()

    def through(p):
        lanes = wide_of(p)
        state = (sm[p] + xf_ref[p].astype(F32)).astype(BF16)
        grad = (gm[p] + xg_ref[p].astype(F32)).astype(BF16)
        xf = xb_ref[:, lanes].astype(F32)
        dmf = dm_ref[:, lanes].astype(F32)
        col = col_ref[:, lanes]
        final = col[rows - 1:]
        back = jnp.exp(final - col) * mm(b, grad)
        y = y_ref[:, lanes] + jnp.exp(col) * mm(c, state)
        mixed_ref[:, lanes] = (y + att_ref[:, lanes]).astype(BF16)
        gx = gx_ref[:, lanes] + back
        net = dmf * y - xf * gx
        hi = net.astype(BF16)
        lo = (net - hi.astype(F32)).astype(BF16)
        inside = jnp.sum(xf * back, axis=0, keepdims=True) + jnp.exp(final) * jnp.sum(
            state.astype(F32) * grad.astype(F32), axis=0, keepdims=True)
        for a in range(2):
            cols = slice(a * D, (a + 1) * D)
            sums = mm_nt(ones, hi[:, cols]) + mm_nt(ones, lo[:, cols])
            net_ref[pl.ds(2 * p + a, 1)] = sums[:1]
            fin_ref[pl.ds(2 * p + a, 1)] = inside[:, cols]
        dbc[:, D:] += mm_nt(dme_ref[:, lanes], state)
        dbc[:, :D] += mm_nt(xt_ref[:, lanes], grad)
        g = gx * sl_ref[:, lanes]
        gh[p] = g[:EDGE].astype(BF16)
        dx_ref[:, lanes] = conv_back(g, jnp.zeros((8, W), F32), w_ref[:, lanes].astype(F32))

    def step(t, carry):
        for kv in rest:
            @pl.when(t == kv * (ratio // 2))
            def _():
                events[kv - 1]()
                relayed(kv)

        hops(HEAD + slow + t)
        attend(t)
        gathers(t)
        return carry

    lax.fori_loop(0, pairs, step, 0)

    def last_hops(t, carry):
        hops(t)
        return carry

    lax.fori_loop(HEAD + slow + pairs, slow + pairs + SLACK, last_hops, 0)

    def finish_through(i, carry):
        two = (2 * i, 2 * i + 1)
        for p in two:
            states_of(p)
        for p in two:
            through(p)

        @pl.when(me > 0)
        def _():
            for p in two:
                edge(p).start()

        for p in two:
            gathers(pairs + p)
        return carry

    lax.fori_loop(0, pairs // 2, finish_through, 0)
    di = dinner[...]
    dbcb[:, D:] = (dbc[:, D:] + mm(di.astype(BF16), b)).astype(BF16)
    dbcb[:, :D] = (dbc[:, :D] + mm(jnp.transpose(di).astype(BF16), c)).astype(BF16)

    def remote(src, dst, send, recv, seq, head):
        return pltpu.make_async_remote_copy(
            src_ref=src, dst_ref=dst, send_sem=send, recv_sem=recv, **peer(seq=seq, head=head))

    def across(off):
        return remote(dbcb, bb.at[off], bs.at[off], br.at[off], me, lax.rem(my + off, m))

    def before(off):
        return remote(dbcb.at[pl.ds(0, EDGE)], nb.at[off], ns.at[off], nr.at[off], prv,
                      lax.rem(my + off, m))

    for off in range(1, m):
        across(off).start()

    @pl.when(me > 0)
    def _():
        for off in range(m):
            before(off).start()

    dla_ref[...] = exact(mm, net_ref[...], lower) + exact(mm, fin_ref[...], jnp.ones((D, rows), BF16))

    for kv in range(kv_heads):
        first, pace = slot_of(kv)

        def leftover(j, carry):
            later = jnp.logical_and(j <= level, first + pace * j >= slots)
            if plain(kv):
                later = jnp.logical_and(later, not_top)

            @pl.when(later)
            def _():
                gather_down(kv, j)

            return carry

        lax.fori_loop(0, levels, leftover, 0)

    @pl.when(me < n - 1)
    def _():
        def finish(i, carry):
            lanes = wide_of(i)
            edge(i).wait_recv()
            after = jnp.concatenate([jnp.zeros((8, W), F32), gn[i].astype(F32)[:8]], axis=0)
            taps = w_ref[:, lanes].astype(F32)
            fix = None
            for tap in range(taps.shape[0]):
                offset = taps.shape[0] - 1 - tap
                term = taps[tap:tap + 1] * after[offset:offset + 8]
                fix = term if fix is None else fix + term
            dx_ref[rows - 8:, lanes] += fix
            return carry

        lax.fori_loop(0, pairs, finish, 0)
        for off in range(m):
            before(off).wait_recv()

    @pl.when(me == n - 1)
    def _():
        nb[...] = jnp.zeros(nb.shape, nb.dtype)

    total = dbcb[...].astype(F32)
    for off in range(1, m):
        across(off).wait_recv()
        total += bb[off].astype(F32)
    follow = nb[0].astype(F32)
    for off in range(1, m):
        follow += nb[off].astype(F32)
    dbc_out[...] = conv_back(total * bcsl[...], (follow * bcsn[...])[:8], wbc)

    for kv in range(kv_heads):
        gathered(kv)

    for off in range(1, m):
        across(off).wait_send()

    @pl.when(me > 0)
    def _():
        def edge_sent(i, carry):
            edge(i).wait_send()
            return carry

        lax.fori_loop(0, pairs, edge_sent, 0)
        for off in range(m):
            before(off).wait_send()

    for kv in range(kv_heads):
        gather_sent(kv)

    def drain(i, carry):
        @pl.when(not_top)
        def _():
            climb(i).wait_send()

        @pl.when(level > 0)
        def _():
            descend(i).wait_send()

        @pl.when(give_f)
        def _():
            give(i, 0).wait_send()

        @pl.when(give_b)
        def _():
            give(i, 1).wait_send()

        return carry

    lax.fori_loop(0, pairs, drain, 0)
    for kv in range(kv_heads):
        relay_sent(kv)

    @pl.when(me < n - 1)
    def _():
        cb.wait_send()
        cx.wait_send()

    @pl.when(me > 0)
    def _():
        cn.wait_send()


def block_part(n, m, x_in, bc_in, conv_x, conv_bc, log_decay, skip, queries, keys, values, d_mixed):
    rows, wide = x_in.shape
    width = keys.shape[1]
    heads = wide // D
    pairs = heads // 2
    kv_heads = width // D
    length = n * rows
    taps = conv_x.shape[0]
    dma = pltpu.SemaphoreType.DMA
    shape = jax.ShapeDtypeStruct

    def v(dims, dtype=F32):
        return pltpu.VMEM(dims, dtype)

    def stay(a):
        return pltpu.with_memory_space_constraint(a, pltpu.HBM)

    state = (pairs, D, W)
    return pl.pallas_call(
        functools.partial(block_kernel, n, m),
        out_shape=(
            shape((rows, wide), BF16), shape((rows, wide), F32), shape((rows, width), F32),
            shape((rows, width), F32), shape((rows, wide), F32), shape((rows, W), F32),
            shape((heads, rows), F32)),
        in_specs=[HBM] * 5 + [SMEM] + [HBM] * 4,
        out_specs=(VMEM,) * 7,
        scratch_shapes=[
            v((rows, wide), BF16), v((rows, wide), BF16), v((rows, wide), BF16), v((taps, wide), BF16),
            v(bc_in.shape, BF16), v(conv_bc.shape, BF16), v((heads, rows)), v((rows, W), BF16),
            v((kv_heads, n, rows, W), BF16), v((EDGE, wide), BF16), v((EDGE, W), BF16), v((EDGE, W), BF16),
            v((rows, wide), BF16), v((rows, wide)), v((rows, wide)), v((rows, wide), BF16),
            v((rows, wide), BF16), v((rows, wide)), v((rows, wide)), v((rows, wide)),
            v((rows, W), BF16), v((rows, W)), v((EDGE, W)), v((D, rows), BF16), v((D, rows), BF16),
            v((pairs, 1, W)), v((pairs, 1, W)), v((pairs, 1, W)), v((rows, W)), v((rows, W)),
            v((rows, rows)), v((rows, W)), v((rows, W), BF16), v((heads, rows)), v((heads, rows)),
            *[v(state) for _ in range(4)], *[v(state, BF16) for _ in range(8)],
            v((length, W)), v((length, W), BF16), v((length, W), BF16), v((D, length), BF16),
            v((D + EDGE, length), BF16), v((length, D), BF16), v((2 * rows, D), BF16), v((length, D)),
            v((length, D)), v((kv_heads, n, rows, W), BF16), v((kv_heads, n // 2, rows, W), BF16),
            v((kv_heads, n // 2, 2, rows, W), BF16), v((rows, W)),
            v((pairs, EDGE, W), BF16), v((pairs, EDGE, W), BF16), v((m, rows, W), BF16), v((m, EDGE, W), BF16),
            dma((2 * kv_heads + 7,)), *[dma((kv_heads, n)) for _ in range(4)], dma((3,)), dma((3,)),
            dma, dma, *[dma((pairs,)) for _ in range(8)],
            *[dma((kv_heads, n // 2)) for _ in range(4)], dma((pairs,)), dma((pairs,)), dma((m,)), dma((m,)), dma((m,)), dma((m,))],
        compiler_params=pltpu.CompilerParams(
            collective_id=0, has_side_effects=True, vmem_limit_bytes=40 * 2**20),
        name="block",
    )(*map(stay, (x_in, bc_in, conv_x, conv_bc, log_decay.T, skip, queries, keys, values, d_mixed)))


def write_kernel(mixed, dq, dk, dv, dx, dbc, dla, mixed_o, dq_o, dk_o, dv_o, dx_o, dbc_o, dla_o, dbc3, sem):
    quarter = dq.shape[0] // 4
    copies = [(a.at[pl.ds(i * quarter, quarter)], b.at[pl.ds(i * quarter, quarter)])
              for a, b in ((dq, dq_o), (dx, dx_o), (mixed, mixed_o)) for i in range(4)]
    copies += [(dk, dk_o), (dv, dv_o), (dla, dla_o), (dbc3, dbc_o)]
    copies = [pltpu.make_async_copy(src, dst, sem.at[i]) for i, (src, dst) in enumerate(copies)]
    for cp in copies[:-1]:
        cp.start()
    dbc3[:, 0, :] = dbc[:, :D]
    dbc3[:, 1, :] = dbc[:, D:]
    copies[-1].start()
    for cp in copies:
        cp.wait()


def write_part(mixed, dq, dk, dv, dx, dbc, dla):
    rows = dbc.shape[0]
    outs = tuple(jax.ShapeDtypeStruct(a.shape, a.dtype) for a in (mixed, dq, dk, dv, dx))
    outs += (jax.ShapeDtypeStruct((rows, 2, D), F32), jax.ShapeDtypeStruct(dla.shape, F32))
    return pl.pallas_call(
        write_kernel,
        out_shape=outs,
        in_specs=[VMEM] * 7,
        out_specs=(HBM,) * 7,
        scratch_shapes=[pltpu.VMEM((rows, 2, D), F32), pltpu.SemaphoreType.DMA((16,))],
        compiler_params=pltpu.CompilerParams(vmem_limit_bytes=2 * 2**20),
        name="write",
    )(mixed, dq, dk, dv, dx, dbc, dla)


def shards(n, m, *args):
    *outs, dla = write_part(*block_part(n, m, *args))
    return (*outs, dla.T)


def solution(mesh):
    n, m = mesh.shape["seq"], mesh.shape["head"]
    grid = P("seq", "head")
    part = P("seq", None, None)
    in_specs = (grid, part, P(None, "head"), P(), grid, P("head"), grid, grid, grid, grid)
    out_specs = (grid, grid, grid, grid, grid, part, grid)
    return jax.shard_map(functools.partial(shards, n, m), mesh=mesh, in_specs=in_specs,
                         out_specs=out_specs, check_vma=False)
```
